128 devices in a mesh: tm: 4 (over y), sta: 32 (over x, z, core).
Axes of the slice: x: 4, y: 4, z: 4, core: 2. Of those that a mesh axis runs over, the one named last changes fastest.
Arguments:
- spectra: bfloat16 [4, 32, 2, 3, 2, 2048], P('tm', 'sta'), may hold values from -6 to 6
- pair_blocks: int32 [32, 40, 2], P('sta'), may hold values from 0 to 31, as said below
- block_count: int32 [32], P('sta'), may hold values from 1 to 40, as said below
Outputs:
- correlations: bfloat16 [32, 40, 1, 1, 3, 3, 4096], P('sta', 'tm')
The draws below stay inside these ranges and needn't reach their ends.
Inputs may be any that keep to these rules, and one draw needn't show every extreme that they name: `pair_blocks`: among the first block_count[o] slots of all owners o, every unordered pair of two different station groups stands exactly once, in either order; later slots hold arbitrary group numbers. `block_count`: the counts sum to 496, and one owner uses all 40 slots.
All inputs are finite; a program needn't handle non-finite values.
Results may differ from the reference program's by a relative error of at most 0.014.
Values may be sent and summed in bfloat16 or wider, within the bound.
A program may use at most 64 MiB of HBM per device.

```python
import jax
import jax.numpy as jnp
import numpy as np
from jax import lax

F = 2048
LAGS = 4096
SMOOTH = 64
STA_DEV = 1
SEGS = 2
HOURS = 4
GROUPS = 32
STATIONS = 32
SLOTS = 40


def owner_plan(key):
    pair_total = GROUPS * (GROUPS - 1) // 2
    key_rank, key_weight, key_order, key_filler, key_flip = jax.random.split(jax.random.fold_in(key, 11), 5)
    owner_rank = jax.random.permutation(key_rank, GROUPS)
    ranks = jnp.arange(GROUPS, dtype=jnp.int32)
    weights = jax.random.randint(key_weight, (GROUPS,), 2, 4, dtype=jnp.int32)
    weights = jnp.where(ranks == 0, 0, weights)
    remaining = pair_total - SLOTS
    shares = remaining * weights // jnp.sum(weights)
    leftover = remaining - jnp.sum(shares)
    shares = shares + ((ranks >= 1) & (ranks <= leftover)).astype(jnp.int32)
    by_rank = jnp.where(ranks == 0, SLOTS, shares).astype(jnp.int32)
    counts = jnp.zeros((GROUPS,), jnp.int32).at[owner_rank].set(by_rank)
    offsets = jnp.cumsum(counts) - counts
    upper_pairs = np.triu_indices(GROUPS, 1)
    first_all = jnp.asarray(upper_pairs[0], dtype=jnp.int32)
    second_all = jnp.asarray(upper_pairs[1], dtype=jnp.int32)
    order = jax.random.permutation(key_order, pair_total)
    flipped = jax.random.randint(key_flip, (pair_total,), 0, 2, dtype=jnp.int32) == 1
    first_pick = jnp.where(flipped, second_all[order], first_all[order])
    second_pick = jnp.where(flipped, first_all[order], second_all[order])
    slot_positions = jnp.arange(SLOTS, dtype=jnp.int32)[None, :]
    slot_index = offsets[:, None] + slot_positions
    live = slot_positions < counts[:, None]
    safe_index = jnp.minimum(slot_index, pair_total - 1)
    pairs = jnp.stack([first_pick[safe_index], second_pick[safe_index]], axis=-1)
    filler = jax.random.randint(key_filler, (GROUPS, SLOTS, 2), 0, GROUPS, dtype=jnp.int32)
    blocks = jnp.where(live[..., None], pairs, filler).astype(jnp.int32)
    return (blocks, counts)


def draw_pair_blocks(key, part):
    return owner_plan(key)[0]


def draw_block_count(key, part):
    return owner_plan(key)[1]


def steps_of(stream_key, dims, shards, smallest, high):
    def one(dim, blocks):
        heights = jax.random.uniform(jax.random.fold_in(jax.random.fold_in(stream_key, 6), dim), (blocks,), jnp.float32, smallest / len(shards), high / len(shards))
        return jnp.repeat(jnp.exp(heights), dims[dim] // blocks).reshape((-1,) + (1,) * (len(dims) - dim - 1))

    gain = one(*shards[0])
    for cut in shards[1:]:
        gain = gain * one(*cut)
    return gain


def centred(own_key, extent, deviation, most, cuts=(), held_as=jnp.bfloat16):
    array = jax.random.normal(own_key, extent, jnp.float32) * deviation
    if len(cuts) > 0:
        array = steps_of(own_key, extent, cuts, -0.22, 0.18) * array
    return jnp.clip(array, min=-most, max=most).astype(held_as)


def setup_inputs(seed: int = 0) -> dict:
    streams_of = jax.random.split(jax.random.key(seed), 4)
    return {
        "spectra": centred(streams_of[0], (HOURS, STATIONS, SEGS, 3, 2, F), 1.0, 6.0, ((0, 4), (1, 32))),
        "pair_blocks": draw_pair_blocks(jax.random.fold_in(streams_of[3], 71), 0),
        "block_count": draw_block_count(jax.random.fold_in(streams_of[3], 71), 0),
    }


epsilon = 1e-05

def whiten(spectra):
    values = spectra.astype(jnp.float32)
    amplitude = jnp.sqrt(values[..., 0, :] ** 2 + values[..., 1, :] ** 2)
    width = amplitude.shape[-1]
    padding = [(0, 0)] * (amplitude.ndim - 1) + [(SMOOTH + 1, SMOOTH)]
    running = jnp.cumsum(jnp.pad(amplitude, padding), axis=-1)
    window_sum = running[..., 2 * SMOOTH + 1:] - running[..., :width]
    positions = jnp.arange(width, dtype=jnp.int32)
    lower = jnp.maximum(positions - SMOOTH, 0)
    upper = jnp.minimum(positions + SMOOTH, width - 1)
    bin_count = (upper - lower + 1).astype(jnp.float32)
    smoothed = window_sum / bin_count
    white = values / (smoothed + epsilon)[..., None, :]
    return white.astype(jnp.bfloat16)

def cross_hours(every, firsts, seconds):
    grouped = every.reshape(every.shape[0], GROUPS, STA_DEV, SEGS, 3, 2, F)
    left = grouped[:, firsts].astype(jnp.float32)
    right = grouped[:, seconds].astype(jnp.float32)
    form = 'hnasxf,hnbsyf->hnabxyf'
    high = lax.Precision.HIGHEST
    real_part = jnp.einsum(form, left[..., 0, :], right[..., 0, :], precision=high) + jnp.einsum(form, left[..., 1, :], right[..., 1, :], precision=high)
    imag_part = jnp.einsum(form, left[..., 0, :], right[..., 1, :], precision=high) - jnp.einsum(form, left[..., 1, :], right[..., 0, :], precision=high)
    return jnp.stack([real_part, imag_part], axis=-2)

def lag_values(daily):
    values = daily.astype(jnp.float32)
    spectrum = lax.complex(values[..., 0, :], values[..., 1, :])
    inverse = jnp.fft.ifft(spectrum, n=LAGS, axis=-1)
    scaled = jnp.real(inverse) * (LAGS * F ** (-0.5))
    return jnp.roll(scaled, F, axis=-1).astype(jnp.bfloat16)

def reference(spectra, pair_blocks, block_count):
    white = whiten(spectra)

    def one_owner(owner_args):
        blocks, live_count = owner_args
        partial_value = cross_hours(white, blocks[:, 0], blocks[:, 1]).astype(jnp.bfloat16)
        daily = lax.optimization_barrier(jnp.sum(partial_value.astype(jnp.float32), axis=0))
        live = (jnp.arange(SLOTS, dtype=jnp.int32) < live_count).astype(jnp.float32)
        daily = (daily * live[:, None, None, None, None, None, None]).astype(jnp.bfloat16)
        return lag_values(daily)
    return lax.map(one_owner, (pair_blocks, block_count))
```

```python
import functools
import math

import jax
import jax.numpy as jnp
import numpy as np
from jax import lax
from jax.experimental import pallas as pl
from jax.experimental.pallas import tpu as pltpu
from jax.sharding import PartitionSpec as P

MESH = pl.DeviceIdType.MESH
VMEM = pltpu.VMEM
DMA = pltpu.SemaphoreType.DMA

SMOOTH = 64
epsilon = 1e-05

NY, NX, NZ, NC = 4, 4, 4, 2
CHUNKS = NY * NC
F2 = 32
LOCAL = F2 // CHUNKS
WIDTH = 2048
LAGS = 4096
STATIONS = 32
HOURS = 4
SEGS = 2
SHARE = 10
TILES = SHARE * 9 * LOCAL // 8


def constants():
    lane = np.arange(128)
    part, m, u = lane // 64, (lane // 16) % 4, lane % 16
    f1 = 4 * u + m
    fine = np.arange(128)
    angle = 2.0 * math.pi * ((f1[:, None] * fine[None, :]) % 128) / 128.0
    cos, sin = np.cos(angle), np.sin(angle)
    is_re = (part == 0)[:, None]
    first = np.concatenate([np.where(is_re, cos, -sin), np.where(is_re, sin, cos)], axis=1)
    f2 = np.arange(F2)
    turn = 2.0 * math.pi * (f2[:, None] * fine[None, :]) / LAGS
    sign = np.where(f2 % 2 == 0, 1.0, -1.0)[:, None] * WIDTH ** (-0.5)
    twiddle = np.stack([np.cos(turn) * sign, np.sin(turn) * sign], axis=0)
    twiddle = twiddle.reshape(2, CHUNKS, 1, LOCAL, 128)
    twiddle = np.broadcast_to(twiddle, (2, CHUNKS, 8 // LOCAL, LOCAL, 128))
    twiddle = twiddle.reshape(2, CHUNKS, 8, 128).transpose(1, 0, 2, 3)
    coarse = np.arange(32)
    spin = 2.0 * math.pi * ((coarse[:, None] * f2[None, :]) % 32) / 32.0
    parts = []
    for table in (np.cos(spin), -np.sin(spin)):
        block = np.zeros((2, 32, 4, CHUNKS, 2, 3, LOCAL))
        for which in range(2):
            for comp in range(3):
                block[which, :, comp, :, which, comp, :] = table.reshape(32, CHUNKS, LOCAL)
        parts.append(block.reshape(256, CHUNKS * 6 * LOCAL))
    second = np.stack(parts, axis=0)
    return (
        first.astype(jnp.bfloat16),
        twiddle.astype(np.float32),
        second.astype(jnp.bfloat16),
    )


def band():
    row = lax.broadcasted_iota(jnp.int32, (128, 128), 0)
    col = lax.broadcasted_iota(jnp.int32, (128, 128), 1)
    gap = row - col
    one, zero = jnp.float32(1.0), jnp.float32(0.0)
    same = jnp.where(jnp.abs(gap) <= SMOOTH, one, zero)
    before = jnp.where(gap >= SMOOTH, one, zero)
    after = jnp.where(gap <= -SMOOTH, one, zero)
    return jnp.concatenate([before, same, after], axis=0).astype(jnp.bfloat16)


def whiten_blocks(x_ref):
    fill = jnp.zeros((2, WIDTH), jnp.float32)
    re = jnp.concatenate([x_ref[:, 0, :].astype(jnp.float32), fill], axis=0)
    im = jnp.concatenate([x_ref[:, 1, :].astype(jnp.float32), fill], axis=0)
    blocks = WIDTH // 128

    def rows(value):
        return jnp.concatenate([value[:, 128 * k : 128 * k + 128] for k in range(blocks)], axis=0)

    re, im = rows(re), rows(im)
    amplitude = jnp.sqrt(re * re + im * im)
    high = amplitude.astype(jnp.bfloat16)
    low = (amplitude - high.astype(jnp.float32)).astype(jnp.bfloat16)
    weights = band()
    total = None
    for value in (high, low):
        value = value.astype(jnp.float32)
        edge = jnp.zeros((8, 128), jnp.float32)
        before = jnp.concatenate([edge, value[:-8]], axis=0)
        after = jnp.concatenate([value[8:], edge], axis=0)
        wide = jnp.concatenate([before, value, after], axis=1).astype(jnp.bfloat16)
        term = jnp.dot(wide, weights, preferred_element_type=jnp.float32)
        total = term if total is None else total + term
    row = lax.broadcasted_iota(jnp.int32, (128, 128), 0)
    col = lax.broadcasted_iota(jnp.int32, (128, 128), 1)
    position = (row // 8) * 128 + col
    lower = jnp.maximum(position - SMOOTH, 0)
    upper = jnp.minimum(position + SMOOTH, WIDTH - 1)
    bins = (upper - lower + 1).astype(jnp.float32)
    smoothed = total / bins
    scale = smoothed + epsilon
    return re / scale, im / scale


def exchange_kernel(x_ref, pairs_ref, daily_ref, flat, packed, every, lists, out_buf,
                    list_sem, col_send, col_recv, row_send, row_recv, fwd_send, fwd_recv,
                    day_send, day_recv, own_sem):
    y = lax.axis_index("tm")
    sta = lax.axis_index("sta")
    core = sta % NC
    column = sta // NC
    xx, zz = column // NZ, column % NZ
    chunk = NC * y + core

    def station(x_at, z_at, core_at):
        return (x_at * NZ + z_at) * NC + core_at

    x_peers = [(xx + d) % NX for d in range(1, NX)]
    z_peers = [(zz + d) % NZ for d in range(1, NZ)]
    column_peers = [
        ((y + dy) % NY, (core + dc) % NC)
        for dy, dc in ((2, 0), (2, 1), (1, 0), (1, 1), (3, 0), (3, 1), (0, 1))
    ]

    barrier = pltpu.get_barrier_semaphore()
    for y_at, core_at in column_peers:
        pl.semaphore_signal(barrier, inc=1, device_id=(y_at, station(xx, zz, core_at)), device_id_type=MESH)
    for x_at in x_peers:
        pl.semaphore_signal(barrier, inc=1, device_id=(y, station(x_at, zz, core)), device_id_type=MESH)
    for z_at in z_peers:
        pl.semaphore_signal(barrier, inc=1, device_id=(y, station(xx, z_at, core)), device_id_type=MESH)

    own_list = pltpu.make_async_copy(pairs_ref, lists.at[core], list_sem.at[0])
    own_list.start()

    white_re, white_im = whiten_blocks(x_ref)
    flat[0] = white_re
    flat[1] = white_im
    turned = []
    for row in range(SEGS * 3):
        pieces = []
        for part in range(2):
            tile = flat[part, pl.ds(row, 16, stride=8), :]
            for m in range(4):
                pieces.append(tile if m == 0 else pltpu.roll(tile, 128 - 32 * m, 1))
        stacked = jnp.concatenate(pieces, axis=0)
        turned.append(jnp.transpose(stacked, (1, 0))[:F2])
    for k in range(CHUNKS):
        for comp in range(3):
            tile = jnp.concatenate(
                [turned[seg * 3 + comp][LOCAL * k : LOCAL * k + LOCAL] for seg in range(SEGS)], axis=0
            )
            packed[k, comp] = tile.astype(jnp.bfloat16)

    pl.semaphore_wait(barrier, len(column_peers) + len(x_peers) + len(z_peers))

    list_copy = pltpu.make_async_remote_copy(
        src_ref=pairs_ref,
        dst_ref=lists.at[core],
        send_sem=list_sem.at[1],
        recv_sem=list_sem.at[2],
        device_id=(y, station(xx, zz, 1 - core)),
        device_id_type=MESH,
    )
    list_copy.start()

    column_copies = []
    for at, (y_at, core_at) in enumerate(column_peers):
        copy = pltpu.make_async_remote_copy(
            src_ref=packed.at[NC * y_at + core_at],
            dst_ref=every.at[sta, y],
            send_sem=col_send.at[at],
            recv_sem=col_recv.at[chunk],
            device_id=(y_at, station(xx, zz, core_at)),
            device_id_type=MESH,
        )
        copy.start()
        column_copies.append(copy)
    own = pltpu.make_async_copy(packed.at[chunk], every.at[sta, y], own_sem)
    own.start()
    own.wait()
    for at, (y_at, core_at) in enumerate(column_peers):
        pltpu.make_async_remote_copy(
            src_ref=packed.at[chunk],
            dst_ref=every.at[station(xx, zz, core_at), y_at],
            send_sem=col_send.at[at],
            recv_sem=col_recv.at[NC * y_at + core_at],
            device_id=(y_at, station(xx, zz, core_at)),
            device_id_type=MESH,
        ).wait_recv()

    mine = every.at[pl.ds(station(xx, zz, 0), NC)]
    row_copies = []
    for at in range(3):
        for axis in range(2):
            peer = station(x_peers[at], zz, core) if axis == 0 else station(xx, z_peers[at], core)
            slot = xx if axis == 0 else zz
            copy = pltpu.make_async_remote_copy(
                src_ref=mine,
                dst_ref=mine,
                send_sem=row_send.at[axis, at],
                recv_sem=row_recv.at[axis, slot],
                device_id=(y, peer),
                device_id_type=MESH,
            )
            copy.start()
            row_copies.append(copy)
    forward_copies = []
    for at in range(3):
        for axis in range(2):
            x_at, z_at = (x_peers[at], zz) if axis == 0 else (xx, z_peers[at])
            block = every.at[pl.ds(station(x_at, z_at, 0), NC)]
            pltpu.make_async_remote_copy(
                src_ref=mine,
                dst_ref=block,
                send_sem=row_send.at[axis, at],
                recv_sem=row_recv.at[axis, x_at if axis == 0 else z_at],
                device_id=(y, station(x_at, z_at, core)),
                device_id_type=MESH,
            ).wait_recv()
            piece = every.at[station(x_at, z_at, axis)]
            for to in range(3):
                peer = station(xx, z_peers[to], core) if axis == 0 else station(x_peers[to], zz, core)
                copy = pltpu.make_async_remote_copy(
                    src_ref=piece,
                    dst_ref=piece,
                    send_sem=fwd_send.at[axis, at, to],
                    recv_sem=fwd_recv.at[axis, x_at, z_at] if axis == 0 else fwd_recv.at[axis, x_at, z_at],
                    device_id=(y, peer),
                    device_id_type=MESH,
                )
                copy.start()
                forward_copies.append(copy)
    for x_at in x_peers:
        for z_at in z_peers:
            for axis in range(2):
                piece = every.at[station(x_at, z_at, axis)]
                relay = station(xx, z_at, core) if axis == 0 else station(x_at, zz, core)
                slot_x, slot_z = (x_at, z_at)
                pltpu.make_async_remote_copy(
                    src_ref=piece,
                    dst_ref=piece,
                    send_sem=fwd_send.at[axis, 0, 0],
                    recv_sem=fwd_recv.at[axis, slot_x, slot_z],
                    device_id=(y, relay),
                    device_id_type=MESH,
                ).wait_recv()
    own_list.wait()
    list_copy.wait_send()
    pltpu.make_async_remote_copy(
        src_ref=pairs_ref,
        dst_ref=lists.at[1 - core],
        send_sem=list_sem.at[1],
        recv_sem=list_sem.at[2],
        device_id=(y, station(xx, zz, 1 - core)),
        device_id_type=MESH,
    ).wait_recv()

    lane = lax.broadcasted_iota(jnp.int32, (8, 128), 1)
    sub = lax.broadcasted_iota(jnp.int32, (8, 128), 0)
    is_re = lane < 64
    is_low = sub < LOCAL
    sign = jnp.where(is_re, jnp.float32(-1.0), jnp.float32(1.0))

    def slot_products(first, second):
        plain, crossed = [None] * 9, [None] * 9
        for hour in range(HOURS):
            left = [every[first, hour, comp].astype(jnp.float32) for comp in range(3)]
            right = [every[second, hour, comp].astype(jnp.float32) for comp in range(3)]
            swapped = [pltpu.roll(value, 64, 1) * sign for value in left]
            for a in range(3):
                for b in range(3):
                    at = 3 * a + b
                    one, two = left[a] * right[b], swapped[a] * right[b]
                    plain[at] = one if hour == 0 else plain[at] + one
                    crossed[at] = two if hour == 0 else crossed[at] + two
        joined = []
        for at in range(9):
            keep = jnp.where(is_re, plain[at], crossed[at])
            move = jnp.where(is_re, crossed[at], plain[at])
            joined.append(keep + pltpu.roll(move, 64, 1))
        return joined

    def fill(target, core_at, first_slot):
        def step(at, carry):
            values = []
            for half in range(2):
                slot = first_slot + 2 * at + half
                values += slot_products(lists[core_at, 0, slot], lists[core_at, 1, slot])
            for tile in range(9):
                one, two = values[2 * tile], values[2 * tile + 1]
                keep = jnp.where(is_low, one, two)
                move = jnp.where(is_low, two, one)
                target[9 * at + tile] = (keep + pltpu.roll(move, LOCAL, 0)).astype(jnp.bfloat16)
            return carry

        lax.fori_loop(0, SHARE // 2, step, 0)

    def send(at):
        y_at, core_at = column_peers[at]
        copy = pltpu.make_async_remote_copy(
            src_ref=out_buf.at[at],
            dst_ref=daily_ref.at[chunk],
            send_sem=day_send.at[at],
            recv_sem=day_recv.at[chunk],
            device_id=(y_at, station(xx, zz, core_at)),
            device_id_type=MESH,
        )
        copy.start()
        return copy

    day_copies = []
    for at, (y_at, core_at) in enumerate(column_peers):
        fill(out_buf.at[at], core_at, SHARE * y_at)
        day_copies.append(send(at))
    fill(daily_ref.at[chunk], core, SHARE * y)
    for at, (y_at, core_at) in enumerate(column_peers):
        pltpu.make_async_remote_copy(
            src_ref=out_buf.at[at],
            dst_ref=daily_ref.at[NC * y_at + core_at],
            send_sem=day_send.at[at],
            recv_sem=day_recv.at[NC * y_at + core_at],
            device_id=(y_at, station(xx, zz, core_at)),
            device_id_type=MESH,
        ).wait_recv()
    for copy in column_copies + row_copies + forward_copies + day_copies:
        copy.wait_send()


def lags_kernel(count_ref, daily_ref, first_ref, twiddle_ref, second_ref, out_ref, middle):
    first_slot = lax.axis_index("tm") * SHARE
    count = count_ref[0]

    def stage_one(k, carry):
        rows = daily_ref[k].astype(jnp.float32).reshape(TILES * 8, 128).astype(jnp.bfloat16)
        product = jnp.dot(rows, first_ref[...], preferred_element_type=jnp.float32)
        re = product[:, :128].reshape(TILES, 8, 128)
        im = product[:, 128:].reshape(TILES, 8, 128)
        turn_re, turn_im = twiddle_ref[k, 0], twiddle_ref[k, 1]
        middle[k, 0] = (re * turn_re - im * turn_im).reshape(TILES * 8, 128)
        middle[k, 1] = (re * turn_im + im * turn_re).reshape(TILES * 8, 128)
        return carry

    lax.fori_loop(0, CHUNKS, stage_one, 0)
    rows_of_group = 6 * LOCAL

    def stage_two(group, carry):
        at = pl.multiple_of(group * rows_of_group, 8)
        total = None
        for part in range(2):
            column = jnp.concatenate(
                [middle[k, part, pl.ds(at, rows_of_group), :] for k in range(CHUNKS)], axis=0
            ).astype(jnp.bfloat16)
            term = jnp.dot(second_ref[part], column, preferred_element_type=jnp.float32)
            total = term if total is None else total + term
        for which in range(2):
            index = 2 * group + which
            live = (first_slot + index // 3) < count
            for coarse in range(32):
                start = 128 * which + 4 * coarse
                value = total[start : start + 3]
                value = jnp.where(live, value, jnp.zeros_like(value))
                out_ref[index, :, 128 * coarse : 128 * coarse + 128] = value.astype(jnp.bfloat16)
        return carry

    lax.fori_loop(0, SHARE * 3 // 2, stage_two, 0)


def body(spectra, pair_blocks, block_count):
    values = spectra.reshape(SEGS * 3, 2, WIDTH)
    pairs = pair_blocks[0].T
    first, twiddle, second = (jnp.asarray(value) for value in constants())
    daily = pl.pallas_call(
        exchange_kernel,
        out_shape=jax.ShapeDtypeStruct((CHUNKS, TILES, 8, 128), jnp.bfloat16),
        in_specs=[
            pl.BlockSpec(memory_space=pltpu.VMEM),
            pl.BlockSpec(memory_space=pl.ANY),
        ],
        out_specs=pl.BlockSpec(memory_space=pltpu.VMEM),
        scratch_shapes=[
            VMEM((2, 128, 128), jnp.float32),
            VMEM((CHUNKS, 3, 8, 128), jnp.bfloat16),
            VMEM((STATIONS, HOURS, 3, 8, 128), jnp.bfloat16),
            pltpu.SMEM((NC,) + pairs.shape, jnp.int32),
            VMEM((CHUNKS - 1, TILES, 8, 128), jnp.bfloat16),
            DMA((3,)),
            DMA((CHUNKS - 1,)),
            DMA((CHUNKS,)),
            DMA((2, 3)),
            DMA((2, 4)),
            DMA((2, 3, 3)),
            DMA((2, 4, 4)),
            DMA((CHUNKS - 1,)),
            DMA((CHUNKS,)),
            DMA(()),
        ],
        compiler_params=pltpu.CompilerParams(collective_id=0, has_side_effects=True),
        name="exchange",
    )(values, pairs)
    lags = pl.pallas_call(
        lags_kernel,
        out_shape=jax.ShapeDtypeStruct((SHARE * 3, 3, LAGS), jnp.bfloat16),
        in_specs=[pl.BlockSpec(memory_space=pltpu.SMEM)] + [pl.BlockSpec(memory_space=pltpu.VMEM)] * 4,
        out_specs=pl.BlockSpec(memory_space=pltpu.VMEM),
        scratch_shapes=[VMEM((CHUNKS, 2, TILES * 8, 128), jnp.float32)],
        name="lags",
    )(block_count, daily, first, twiddle, second)
    return lags.reshape(1, SHARE, 1, 1, 3, 3, LAGS)


def solution(mesh):
    placed = (P("tm", "sta", None, None, None, None), P("sta", None, None), P("sta"))
    return jax.shard_map(
        body,
        mesh=mesh,
        in_specs=placed,
        out_specs=P("sta", "tm", None, None, None, None, None),
        check_vma=False,
    )
```

```python
import functools
import math

import jax
import jax.numpy as jnp
import numpy as np
from jax import lax
from jax.experimental import pallas as pl
from jax.experimental.pallas import tpu as pltpu
from jax.sharding import PartitionSpec as P

MESH = pl.DeviceIdType.MESH
VMEM = pltpu.VMEM
DMA = pltpu.SemaphoreType.DMA

SMOOTH = 64
epsilon = 1e-05

NY, NX, NZ, NC = 4, 4, 4, 2
CHUNKS = NY * NC
F2 = 32
LOCAL = F2 // CHUNKS
WIDTH = 2048
LAGS = 4096
STATIONS = 32
HOURS = 4
SEGS = 2
SHARE = 10
TILES = SHARE * 9 * LOCAL // 8


def constants():
    lane = np.arange(128)
    part, m, u = lane // 64, (lane // 16) % 4, lane % 16
    f1 = 4 * u + m
    fine = np.arange(128)
    angle = 2.0 * math.pi * ((f1[:, None] * fine[None, :]) % 128) / 128.0
    cos, sin = np.cos(angle), np.sin(angle)
    is_re = (part == 0)[:, None]
    first = np.concatenate([np.where(is_re, cos, -sin), np.where(is_re, sin, cos)], axis=1)
    f2 = np.arange(F2)
    turn = 2.0 * math.pi * (f2[:, None] * fine[None, :]) / LAGS
    sign = np.where(f2 % 2 == 0, 1.0, -1.0)[:, None] * WIDTH ** (-0.5)
    twiddle = np.stack([np.cos(turn) * sign, np.sin(turn) * sign], axis=0)
    twiddle = twiddle.reshape(2, CHUNKS, 1, LOCAL, 128)
    twiddle = np.broadcast_to(twiddle, (2, CHUNKS, 8 // LOCAL, LOCAL, 128))
    twiddle = twiddle.reshape(2, CHUNKS, 8, 128).transpose(1, 0, 2, 3)
    coarse = np.arange(32)
    spin = 2.0 * math.pi * ((coarse[:, None] * f2[None, :]) % 32) / 32.0
    parts = []
    for table in (np.cos(spin), -np.sin(spin)):
        block = np.zeros((2, 32, 4, CHUNKS, 2, 3, LOCAL))
        for which in range(2):
            for comp in range(3):
                block[which, :, comp, :, which, comp, :] = table.reshape(32, CHUNKS, LOCAL)
        parts.append(block.reshape(256, CHUNKS * 6 * LOCAL))
    second = np.concatenate(parts, axis=1)
    return (
        first.astype(jnp.bfloat16),
        twiddle.astype(np.float32),
        second.astype(jnp.bfloat16),
    )


def band():
    row = lax.broadcasted_iota(jnp.int32, (128, 128), 0)
    col = lax.broadcasted_iota(jnp.int32, (128, 128), 1)
    gap = row - col
    one, zero = jnp.float32(1.0), jnp.float32(0.0)
    same = jnp.where(jnp.abs(gap) <= SMOOTH, one, zero)
    before = jnp.where(gap >= SMOOTH, one, zero)
    after = jnp.where(gap <= -SMOOTH, one, zero)
    return jnp.concatenate([before, same, after], axis=0).astype(jnp.bfloat16)


def whiten_blocks(x_ref):
    fill = jnp.zeros((2, WIDTH), jnp.float32)
    re = jnp.concatenate([x_ref[:, 0, :].astype(jnp.float32), fill], axis=0)
    im = jnp.concatenate([x_ref[:, 1, :].astype(jnp.float32), fill], axis=0)
    blocks = WIDTH // 128

    def rows(value):
        return jnp.concatenate([value[:, 128 * k : 128 * k + 128] for k in range(blocks)], axis=0)

    re, im = rows(re), rows(im)
    amplitude = jnp.sqrt(re * re + im * im)
    high = amplitude.astype(jnp.bfloat16)
    low = (amplitude - high.astype(jnp.float32)).astype(jnp.bfloat16)
    weights = band()
    total = None
    for value in (high, low):
        value = value.astype(jnp.float32)
        edge = jnp.zeros((8, 128), jnp.float32)
        before = jnp.concatenate([edge, value[:-8]], axis=0)
        after = jnp.concatenate([value[8:], edge], axis=0)
        wide = jnp.concatenate([before, value, after], axis=1).astype(jnp.bfloat16)
        term = jnp.dot(wide, weights, preferred_element_type=jnp.float32)
        total = term if total is None else total + term
    row = lax.broadcasted_iota(jnp.int32, (128, 128), 0)
    col = lax.broadcasted_iota(jnp.int32, (128, 128), 1)
    position = (row // 8) * 128 + col
    lower = jnp.maximum(position - SMOOTH, 0)
    upper = jnp.minimum(position + SMOOTH, WIDTH - 1)
    bins = (upper - lower + 1).astype(jnp.float32)
    smoothed = total / bins
    scale = smoothed + epsilon
    return re / scale, im / scale


def station(x_at, z_at, core_at):
    return (x_at * NZ + z_at) * NC + core_at


def arrived(block, sem):
    pltpu.make_async_copy(block, block, sem).wait()


def kernel(count_ref, x_hbm, pairs_ref, first_hbm, twiddle_hbm, second_hbm, out_ref,
           x_ref, first_ref, twiddle_ref, second_ref,
           flat, packed, every, left, swapped, lists, out_buf, daily, middle, staged,
           const_sem, list_sem, one_send, one_recv, fwd_send, fwd_recv, day_send, day_recv, out_sem):
    y = lax.axis_index("tm")
    sta = lax.axis_index("sta")
    core = sta % NC
    column = sta // NC
    xx, zz = column // NZ, column % NZ
    chunk = NC * y + core
    place = xx * (1 - core) + zz * core

    x_peers = [(xx + d) % NX for d in (1, 3, 2)]
    z_peers = [(zz + d) % NZ for d in (1, 3, 2)]
    column_peers = [
        ((y + dy) % NY, (core + dc) % NC)
        for dy, dc in ((2, 0), (2, 1), (1, 0), (1, 1), (3, 0), (3, 1), (0, 1))
    ]

    barrier = pltpu.get_barrier_semaphore()
    greeted = 0
    for dy in range(NY):
        for core_at in (core, 1 - core):
            y_at = (y + dy) % NY
            peers = [(x_at, zz) for x_at in x_peers] + [(xx, z_at) for z_at in z_peers]
            if dy > 0 or core_at is not core:
                peers.append((xx, zz))
            for x_at, z_at in peers:
                pl.semaphore_signal(
                    barrier, inc=1, device_id=(y_at, station(x_at, z_at, core_at)), device_id_type=MESH
                )
                greeted += 1

    load = pltpu.make_async_copy(x_hbm, x_ref, const_sem.at[0])
    load.start()
    own_list = pltpu.make_async_copy(pairs_ref, lists.at[core], list_sem.at[0])
    own_list.start()
    tables = [
        pltpu.make_async_copy(first_hbm, first_ref, const_sem.at[1]),
        pltpu.make_async_copy(twiddle_hbm, twiddle_ref, const_sem.at[2]),
        pltpu.make_async_copy(second_hbm, second_ref, const_sem.at[3]),
    ]
    for table in tables:
        table.start()
    load.wait()

    white_re, white_im = whiten_blocks(x_ref)
    flat[0] = white_re
    flat[1] = white_im
    turned = []
    for row in range(SEGS * 3):
        pieces = []
        for part in range(2):
            tile = flat[part, pl.ds(row, 16, stride=8), :]
            for m in range(4):
                pieces.append(tile if m == 0 else pltpu.roll(tile, 128 - 32 * m, 1))
        stacked = jnp.concatenate(pieces, axis=0)
        turned.append(jnp.transpose(stacked, (1, 0))[:F2])
    for k in range(CHUNKS):
        for comp in range(3):
            tile = jnp.concatenate(
                [turned[seg * 3 + comp][LOCAL * k : LOCAL * k + LOCAL] for seg in range(SEGS)], axis=0
            )
            packed[k, comp] = tile.astype(jnp.bfloat16)

    pl.semaphore_wait(barrier, greeted)

    mine = every.at[xx, zz, core, y]
    one_copies = []
    for dy, di in ((2, 2), (2, 1), (2, 3), (1, 2), (3, 2), (1, 1), (3, 3), (1, 3), (3, 1),
                   (2, 0), (0, 2), (1, 0), (3, 0), (0, 1), (0, 3), (0, 0)):
        for dc in range(NC):
            if (dy, di, dc) == (0, 0, 0):
                continue
            y_at, core_at = (y + dy) % NY, (core + dc) % NC
            x_at, z_at = (xx + di * (1 - core)) % NX, (zz + di * core) % NZ
            copy = pltpu.make_async_remote_copy(
                src_ref=packed.at[NC * y_at + core_at],
                dst_ref=mine,
                send_sem=one_send.at[len(one_copies)],
                recv_sem=one_recv.at[core, place, y],
                device_id=(y_at, station(x_at, z_at, core_at)),
                device_id_type=MESH,
            )
            copy.start()
            one_copies.append(copy)
    pltpu.make_async_copy(packed.at[chunk], mine, one_recv.at[core, place, y]).start()
    list_copy = pltpu.make_async_remote_copy(
        src_ref=pairs_ref,
        dst_ref=lists.at[core],
        send_sem=list_sem.at[1],
        recv_sem=list_sem.at[2],
        device_id=(y, station(xx, zz, 1 - core)),
        device_id_type=MESH,
    )
    list_copy.start()

    lane = lax.broadcasted_iota(jnp.int32, (8, 128), 1)
    sub = lax.broadcasted_iota(jnp.int32, (8, 128), 0)
    is_re = lane < 64
    is_low = sub < LOCAL
    sign = jnp.where(is_re, jnp.float32(-1.0), jnp.float32(1.0))

    def widen(x_at, z_at, core_at):
        at = station(x_at, z_at, core_at)
        for hour in range(HOURS):
            for comp in range(3):
                value = every[x_at, z_at, core_at, hour, comp].astype(jnp.float32)
                left[at, hour, comp] = value
                swapped[at, hour, comp] = pltpu.roll(value, 64, 1) * sign

    fwd_copies = []
    here = []
    for d in (0, 1, 3, 2):
        for side in range(2):
            x_at, z_at = ((xx + d) % NX, zz) if side == 0 else (xx, (zz + d) % NZ)
            for dy in (0, 1, 3, 2):
                y_at = (y + dy) % NY
                arrived(every.at[x_at, z_at, side, y_at], one_recv.at[side, x_at if side == 0 else z_at, y_at])
            piece = every.at[x_at, z_at, side]
            for to in (2, 0, 1):
                copy = pltpu.make_async_remote_copy(
                    src_ref=piece,
                    dst_ref=piece,
                    send_sem=fwd_send.at[len(fwd_copies)],
                    recv_sem=fwd_recv.at[side, x_at, z_at],
                    device_id=(y, station(xx, z_peers[to], core) if side == 0 else station(x_peers[to], zz, core)),
                    device_id_type=MESH,
                )
                copy.start()
                fwd_copies.append(copy)
            here.append((x_at, z_at, side))
    for spot in here:
        widen(*spot)
    for to in range(3):
        for d in (0, 1, 3, 2):
            for side in range(2):
                x_at, z_at = ((xx + d) % NX, z_peers[to]) if side == 0 else (x_peers[to], (zz + d) % NZ)
                arrived(every.at[x_at, z_at, side], fwd_recv.at[side, x_at, z_at])
                widen(x_at, z_at, side)
    own_list.wait()
    arrived(lists.at[1 - core], list_sem.at[2])

    def slot_products(first, second):
        plain, crossed = [None] * 9, [None] * 9
        for hour in range(HOURS):
            one = [left[first, hour, comp] for comp in range(3)]
            turn = [swapped[first, hour, comp] for comp in range(3)]
            two = [left[second, hour, comp] for comp in range(3)]
            for a in range(3):
                for b in range(3):
                    at = 3 * a + b
                    p, q = one[a] * two[b], turn[a] * two[b]
                    plain[at] = p if hour == 0 else plain[at] + p
                    crossed[at] = q if hour == 0 else crossed[at] + q
        joined = []
        for at in range(9):
            keep = jnp.where(is_re, plain[at], crossed[at])
            move = jnp.where(is_re, crossed[at], plain[at])
            joined.append(keep + pltpu.roll(move, 64, 1))
        return joined

    def fill(target, core_at, first_slot):
        def step(at, carry):
            values = []
            for half in range(2):
                slot = first_slot + 2 * at + half
                values += slot_products(lists[core_at, 0, slot], lists[core_at, 1, slot])
            for tile in range(9):
                one, two = values[2 * tile], values[2 * tile + 1]
                keep = jnp.where(is_low, one, two)
                move = jnp.where(is_low, two, one)
                target[9 * at + tile] = (keep + pltpu.roll(move, LOCAL, 0)).astype(jnp.bfloat16)
            return carry

        lax.fori_loop(0, SHARE // 2, step, 0)

    day_copies = []
    for at, (y_at, core_at) in enumerate(column_peers):
        fill(out_buf.at[at], core_at, SHARE * y_at)
        copy = pltpu.make_async_remote_copy(
            src_ref=out_buf.at[at],
            dst_ref=daily.at[chunk],
            send_sem=day_send.at[at],
            recv_sem=day_recv.at[chunk],
            device_id=(y_at, station(xx, zz, core_at)),
            device_id_type=MESH,
        )
        copy.start()
        day_copies.append(copy)
    fill(daily.at[chunk], core, SHARE * y)

    for table in tables:
        table.wait()

    def stage_one(k):
        rows = daily[k].astype(jnp.float32).reshape(TILES * 8, 128).astype(jnp.bfloat16)
        product = jnp.dot(rows, first_ref[...], preferred_element_type=jnp.float32)
        re = product[:, :128].reshape(TILES, 8, 128)
        im = product[:, 128:].reshape(TILES, 8, 128)
        turn_re, turn_im = twiddle_ref[k, 0], twiddle_ref[k, 1]
        middle[k, 0] = (re * turn_re - im * turn_im).reshape(TILES * 8, 128)
        middle[k, 1] = (re * turn_im + im * turn_re).reshape(TILES * 8, 128)

    stage_one(chunk)
    for y_at, core_at in column_peers[::-1][:1] + column_peers[:-1]:
        k = NC * y_at + core_at
        arrived(daily.at[k], day_recv.at[k])
        stage_one(k)

    count = count_ref[0]
    first_slot = SHARE * y
    rows_of_group = 6 * LOCAL

    def group_copy(group):
        return pltpu.make_async_copy(
            staged.at[pl.ds(2 * group, 2)], out_ref.at[pl.ds(2 * group, 2)], out_sem.at[group]
        )

    def stage_two(group, carry):
        at = pl.multiple_of(group * rows_of_group, 8)
        columns = jnp.concatenate(
            [middle[k, part, pl.ds(at, rows_of_group), :] for part in range(2) for k in range(CHUNKS)], axis=0
        ).astype(jnp.bfloat16)
        total = jnp.dot(second_ref[...], columns, preferred_element_type=jnp.float32)
        for which in range(2):
            index = 2 * group + which
            live = (first_slot + index // 3) < count
            for coarse in range(32):
                start = 128 * which + 4 * coarse
                value = total[start : start + 3]
                value = jnp.where(live, value, jnp.zeros_like(value))
                staged[index, :, 128 * coarse : 128 * coarse + 128] = value.astype(jnp.bfloat16)
        group_copy(group).start()
        return carry

    groups = SHARE * 3 // 2
    lax.fori_loop(0, groups, stage_two, 0)

    def drain(group, carry):
        group_copy(group).wait()
        return carry

    lax.fori_loop(0, groups, drain, 0)
    list_copy.wait_send()
    for copy in one_copies + fwd_copies + day_copies:
        copy.wait_send()


def body(spectra, pair_blocks, block_count):
    values = spectra.reshape(SEGS * 3, 2, WIDTH)
    pairs = pair_blocks[0].T
    first, twiddle, second = (jnp.asarray(value) for value in constants())
    f32, bf16 = jnp.float32, jnp.bfloat16
    anywhere = pl.BlockSpec(memory_space=pl.ANY)
    lags = pl.pallas_call(
        kernel,
        out_shape=jax.ShapeDtypeStruct((SHARE * 3, 3, LAGS), bf16),
        in_specs=[pl.BlockSpec(memory_space=pltpu.SMEM)] + [anywhere] * 5,
        out_specs=anywhere,
        scratch_shapes=[
            VMEM(values.shape, bf16),
            VMEM(first.shape, bf16),
            VMEM(twiddle.shape, f32),
            VMEM(second.shape, bf16),
            VMEM((2, 128, 128), f32),
            VMEM((CHUNKS, 3, 8, 128), bf16),
            VMEM((NX, NZ, NC, HOURS, 3, 8, 128), bf16),
            VMEM((STATIONS, HOURS, 3, 8, 128), f32),
            VMEM((STATIONS, HOURS, 3, 8, 128), f32),
            pltpu.SMEM((NC,) + pairs.shape, jnp.int32),
            VMEM((CHUNKS - 1, TILES, 8, 128), bf16),
            VMEM((CHUNKS, TILES, 8, 128), bf16),
            VMEM((CHUNKS, 2, TILES * 8, 128), f32),
            VMEM((SHARE * 3, 3, LAGS), bf16),
            DMA((4,)),
            DMA((3,)),
            DMA((31,)),
            DMA((2, 4, 4)),
            DMA((24,)),
            DMA((2, 4, 4)),
            DMA((CHUNKS - 1,)),
            DMA((CHUNKS,)),
            DMA((SHARE * 3 // 2,)),
        ],
        compiler_params=pltpu.CompilerParams(collective_id=0, has_side_effects=True),
        name="correlate",
    )(block_count, values, pairs, first, twiddle, second)
    return lags.reshape(1, SHARE, 1, 1, 3, 3, LAGS)


def solution(mesh):
    placed = (P("tm", "sta", None, None, None, None), P("sta", None, None), P("sta"))
    return jax.shard_map(
        body,
        mesh=mesh,
        in_specs=placed,
        out_specs=P("sta", "tm", None, None, None, None, None),
        check_vma=False,
    )
```

```python
import functools
import math

import jax
import jax.numpy as jnp
import numpy as np
from jax import lax
from jax.experimental import pallas as pl
from jax.experimental.pallas import tpu as pltpu
from jax.sharding import PartitionSpec as P

MESH = pl.DeviceIdType.MESH
VMEM = pltpu.VMEM
DMA = pltpu.SemaphoreType.DMA

SMOOTH = 64
epsilon = 1e-05

NY, NX, NZ, NC = 4, 4, 4, 2
CHUNKS = NY * NC
F2 = 32
LOCAL = F2 // CHUNKS
WIDTH = 2048
LAGS = 4096
STATIONS = 32
HOURS = 4
SEGS = 2
SHARE = 10
TILES = SHARE * 9 * LOCAL // 8


def constants():
    lane = np.arange(128)
    part, m, u = lane // 64, (lane // 16) % 4, lane % 16
    f1 = 4 * u + m
    fine = np.arange(128)
    angle = 2.0 * math.pi * ((f1[:, None] * fine[None, :]) % 128) / 128.0
    cos, sin = np.cos(angle), np.sin(angle)
    is_re = (part == 0)[:, None]
    first = np.concatenate([np.where(is_re, cos, -sin), np.where(is_re, sin, cos)], axis=1)
    f2 = np.arange(F2)
    turn = 2.0 * math.pi * (f2[:, None] * fine[None, :]) / LAGS
    sign = np.where(f2 % 2 == 0, 1.0, -1.0)[:, None] * WIDTH ** (-0.5)
    twiddle = np.stack([np.cos(turn) * sign, np.sin(turn) * sign], axis=0)
    twiddle = twiddle.reshape(2, CHUNKS, 1, LOCAL, 128)
    twiddle = np.broadcast_to(twiddle, (2, CHUNKS, 8 // LOCAL, LOCAL, 128))
    twiddle = twiddle.reshape(2, CHUNKS, 8, 128).transpose(1, 0, 2, 3)
    coarse = np.arange(32)
    spin = 2.0 * math.pi * ((coarse[:, None] * f2[None, :]) % 32) / 32.0
    parts = []
    for table in (np.cos(spin), -np.sin(spin)):
        block = np.zeros((2, 32, 4, CHUNKS, 2, 3, LOCAL))
        for which in range(2):
            for comp in range(3):
                block[which, :, comp, :, which, comp, :] = table.reshape(32, CHUNKS, LOCAL)
        parts.append(block.reshape(256, CHUNKS * 6 * LOCAL))
    second = np.concatenate(parts, axis=1)
    return (
        first.astype(jnp.bfloat16),
        twiddle.astype(np.float32),
        second.astype(jnp.bfloat16),
    )


def band():
    row = lax.broadcasted_iota(jnp.int32, (128, 128), 0)
    col = lax.broadcasted_iota(jnp.int32, (128, 128), 1)
    gap = row - col
    one, zero = jnp.float32(1.0), jnp.float32(0.0)
    same = jnp.where(jnp.abs(gap) <= SMOOTH, one, zero)
    before = jnp.where(gap >= SMOOTH, one, zero)
    after = jnp.where(gap <= -SMOOTH, one, zero)
    return jnp.concatenate([before, same, after], axis=0).astype(jnp.bfloat16)


def whiten_blocks(x_ref):
    fill = jnp.zeros((2, WIDTH), jnp.float32)
    re = jnp.concatenate([x_ref[:, 0, :].astype(jnp.float32), fill], axis=0)
    im = jnp.concatenate([x_ref[:, 1, :].astype(jnp.float32), fill], axis=0)
    blocks = WIDTH // 128

    def rows(value):
        return jnp.concatenate([value[:, 128 * k : 128 * k + 128] for k in range(blocks)], axis=0)

    re, im = rows(re), rows(im)
    amplitude = jnp.sqrt(re * re + im * im)
    high = amplitude.astype(jnp.bfloat16)
    low = (amplitude - high.astype(jnp.float32)).astype(jnp.bfloat16)
    weights = band()
    total = None
    for value in (high, low):
        value = value.astype(jnp.float32)
        edge = jnp.zeros((8, 128), jnp.float32)
        before = jnp.concatenate([edge, value[:-8]], axis=0)
        after = jnp.concatenate([value[8:], edge], axis=0)
        wide = jnp.concatenate([before, value, after], axis=1).astype(jnp.bfloat16)
        term = jnp.dot(wide, weights, preferred_element_type=jnp.float32)
        total = term if total is None else total + term
    row = lax.broadcasted_iota(jnp.int32, (128, 128), 0)
    col = lax.broadcasted_iota(jnp.int32, (128, 128), 1)
    position = (row // 8) * 128 + col
    lower = jnp.maximum(position - SMOOTH, 0)
    upper = jnp.minimum(position + SMOOTH, WIDTH - 1)
    bins = (upper - lower + 1).astype(jnp.float32)
    smoothed = total / bins
    scale = smoothed + epsilon
    return re / scale, im / scale


def station(x_at, z_at, core_at):
    return (x_at * NZ + z_at) * NC + core_at


def arrived(block, sem):
    pltpu.make_async_copy(block, block, sem).wait()


def kernel(x_hbm, pairs_ref, first_hbm, twiddle_hbm, out_ref,
           x_ref, first_ref, twiddle_ref, sent,
           flat, packed, every, left, swapped, lists, out_buf, daily, middle,
           const_sem, list_sem, one_send, one_recv, fwd_send, fwd_recv, day_send, day_recv, out_sem):
    y = lax.axis_index("tm")
    sta = lax.axis_index("sta")
    core = sta % NC
    column = sta // NC
    xx, zz = column // NZ, column % NZ
    chunk = NC * y + core
    place = xx * (1 - core) + zz * core

    x_peers = [(xx + d) % NX for d in (1, 3, 2)]
    z_peers = [(zz + d) % NZ for d in (1, 3, 2)]
    column_peers = [
        ((y + dy) % NY, (core + dc) % NC)
        for dy, dc in ((2, 0), (2, 1), (1, 0), (1, 1), (3, 0), (3, 1), (0, 1))
    ]

    load = pltpu.make_async_copy(x_hbm, x_ref, const_sem.at[0])
    load.start()
    barrier = pltpu.get_barrier_semaphore()
    greeted = 0
    for dy in range(NY):
        for core_at in (core, 1 - core):
            y_at = (y + dy) % NY
            peers = [(x_at, zz) for x_at in x_peers] + [(xx, z_at) for z_at in z_peers]
            if dy > 0 or core_at is not core:
                peers.append((xx, zz))
            for x_at, z_at in peers:
                pl.semaphore_signal(
                    barrier, inc=1, device_id=(y_at, station(x_at, z_at, core_at)), device_id_type=MESH
                )
                greeted += 1

    own_list = pltpu.make_async_copy(pairs_ref, lists.at[core], list_sem.at[0])
    own_list.start()
    tables = [
        pltpu.make_async_copy(first_hbm, first_ref, const_sem.at[1]),
        pltpu.make_async_copy(twiddle_hbm, twiddle_ref, const_sem.at[2]),
    ]
    for table in tables:
        table.start()
    load.wait()

    white_re, white_im = whiten_blocks(x_ref)
    flat[0] = white_re
    flat[1] = white_im
    turned = []
    for row in range(SEGS * 3):
        pieces = []
        for part in range(2):
            tile = flat[part, pl.ds(row, 16, stride=8), :]
            for m in range(4):
                pieces.append(tile if m == 0 else pltpu.roll(tile, 128 - 32 * m, 1))
        stacked = jnp.concatenate(pieces, axis=0)
        turned.append(jnp.transpose(stacked, (1, 0))[:F2])
    for k in range(CHUNKS):
        for comp in range(3):
            tile = jnp.concatenate(
                [turned[seg * 3 + comp][LOCAL * k : LOCAL * k + LOCAL] for seg in range(SEGS)], axis=0
            )
            packed[k, comp] = tile.astype(jnp.bfloat16)

    pl.semaphore_wait(barrier, greeted)

    mine = every.at[xx, zz, core, y]
    for dy, di in ((2, 2), (2, 1), (2, 3), (1, 2), (3, 2), (1, 1), (3, 3), (1, 3), (3, 1),
                   (2, 0), (0, 2), (1, 0), (3, 0), (0, 1), (0, 3), (0, 0)):
        for dc in range(NC):
            if (dy, di, dc) == (0, 0, 0):
                continue
            y_at, core_at = (y + dy) % NY, (core + dc) % NC
            x_at, z_at = (xx + di * (1 - core)) % NX, (zz + di * core) % NZ
            pltpu.make_async_remote_copy(
                src_ref=packed.at[NC * y_at + core_at],
                dst_ref=mine,
                send_sem=one_send,
                recv_sem=one_recv.at[core, place],
                device_id=(y_at, station(x_at, z_at, core_at)),
                device_id_type=MESH,
            ).start()
    pltpu.make_async_copy(packed.at[chunk], mine, one_recv.at[core, place]).start()
    list_copy = pltpu.make_async_remote_copy(
        src_ref=pairs_ref,
        dst_ref=lists.at[core],
        send_sem=list_sem.at[1],
        recv_sem=list_sem.at[2],
        device_id=(y, station(xx, zz, 1 - core)),
        device_id_type=MESH,
    )
    list_copy.start()

    lane = lax.broadcasted_iota(jnp.int32, (8, 128), 1)
    sub = lax.broadcasted_iota(jnp.int32, (8, 128), 0)
    is_re = lane < 64
    is_low = sub < LOCAL
    sign = jnp.where(is_re, jnp.float32(-1.0), jnp.float32(1.0))

    def widen(x_at, z_at, core_at):
        at = station(x_at, z_at, core_at)
        for hour in range(HOURS):
            for comp in range(3):
                value = every[x_at, z_at, core_at, hour, comp].astype(jnp.float32)
                left[at, hour, comp] = value
                swapped[at, hour, comp] = pltpu.roll(value, 64, 1) * sign

    here = []
    for d in (0, 1, 3, 2):
        for side in range(2):
            x_at, z_at = ((xx + d) % NX, zz) if side == 0 else (xx, (zz + d) % NZ)
            piece = every.at[x_at, z_at, side]
            arrived(piece, one_recv.at[side, x_at if side == 0 else z_at])
            for to in (2, 0, 1):
                pltpu.make_async_remote_copy(
                    src_ref=piece,
                    dst_ref=piece,
                    send_sem=fwd_send,
                    recv_sem=fwd_recv.at[side, zz if side == 0 else xx],
                    device_id=(y, station(xx, z_peers[to], core) if side == 0 else station(x_peers[to], zz, core)),
                    device_id_type=MESH,
                ).start()
            here.append((x_at, z_at, side))
    for spot in here:
        widen(*spot)
    for to in range(3):
        for side in range(2):
            if side == 0:
                arrived(every.at[:, z_peers[to], 0], fwd_recv.at[0, z_peers[to]])
            else:
                arrived(every.at[x_peers[to], :, 1], fwd_recv.at[1, x_peers[to]])
            for d in range(4):
                widen(*((d, z_peers[to], 0) if side == 0 else (x_peers[to], d, 1)))
    own_list.wait()
    arrived(lists.at[1 - core], list_sem.at[2])

    def slot_products(first, second):
        plain, crossed = [None] * 9, [None] * 9
        for hour in range(HOURS):
            one = [left[first, hour, comp] for comp in range(3)]
            turn = [swapped[first, hour, comp] for comp in range(3)]
            two = [left[second, hour, comp] for comp in range(3)]
            for a in range(3):
                for b in range(3):
                    at = 3 * a + b
                    p, q = one[a] * two[b], turn[a] * two[b]
                    plain[at] = p if hour == 0 else plain[at] + p
                    crossed[at] = q if hour == 0 else crossed[at] + q
        joined = []
        for at in range(9):
            keep = jnp.where(is_re, plain[at], crossed[at])
            move = jnp.where(is_re, crossed[at], plain[at])
            joined.append(keep + pltpu.roll(move, 64, 1))
        return joined

    def fill(target, core_at, first_slot):
        def step(at, carry):
            values = []
            for half in range(2):
                slot = first_slot + 2 * at + half
                values += slot_products(lists[core_at, 0, slot], lists[core_at, 1, slot])
            for tile in range(9):
                one, two = values[2 * tile], values[2 * tile + 1]
                keep = jnp.where(is_low, one, two)
                move = jnp.where(is_low, two, one)
                target[9 * at + tile] = (keep + pltpu.roll(move, LOCAL, 0)).astype(jnp.bfloat16)
            return carry

        lax.fori_loop(0, SHARE // 2, step, 0)

    for at, (y_at, core_at) in enumerate(column_peers):
        fill(out_buf.at[at], core_at, SHARE * y_at)
        pltpu.make_async_remote_copy(
            src_ref=out_buf.at[at],
            dst_ref=daily.at[chunk],
            send_sem=day_send,
            recv_sem=day_recv.at[chunk],
            device_id=(y_at, station(xx, zz, core_at)),
            device_id_type=MESH,
        ).start()
    fill(daily.at[chunk], core, SHARE * y)

    for table in tables:
        table.wait()

    def stage_one(k):
        rows = daily[k].astype(jnp.float32).reshape(TILES * 8, 128).astype(jnp.bfloat16)
        product = jnp.dot(rows, first_ref[...], preferred_element_type=jnp.float32)
        re = product[:, :128].reshape(TILES, 8, 128)
        im = product[:, 128:].reshape(TILES, 8, 128)
        turn_re, turn_im = twiddle_ref[k, 0], twiddle_ref[k, 1]
        middle[k, 0] = (re * turn_re - im * turn_im).reshape(TILES * 8, 128).astype(jnp.bfloat16)
        middle[k, 1] = (re * turn_im + im * turn_re).reshape(TILES * 8, 128).astype(jnp.bfloat16)
        pltpu.make_async_copy(middle.at[k], out_ref.at[k], out_sem).start()

    stage_one(chunk)
    for y_at, core_at in column_peers[::-1][:1] + column_peers[:-1]:
        k = NC * y_at + core_at
        arrived(daily.at[k], day_recv.at[k])
        stage_one(k)

    arrived(middle, out_sem)
    list_copy.wait_send()
    arrived(sent, one_send)
    arrived(every.at[pl.ds(0, 3)], fwd_send)
    arrived(out_buf, day_send)


GROUPS_AT_ONCE = 5
GROUPS = SHARE * 3 // 2


def lags_kernel(count_ref, middle_ref, second_ref, out_ref):
    first_slot = lax.axis_index("tm") * SHARE
    count = count_ref[0]
    rows = 6 * LOCAL
    for group in range(GROUPS_AT_ONCE):
        columns = jnp.concatenate(
            [middle_ref[k, part, rows * group : rows * group + rows].astype(jnp.float32)
             for part in range(2) for k in range(CHUNKS)], axis=0
        ).astype(jnp.bfloat16)
        total = jnp.dot(second_ref[...], columns, preferred_element_type=jnp.float32)
        for which in range(2):
            index = 2 * group + which
            slot = first_slot + (2 * GROUPS_AT_ONCE * pl.program_id(0) + index) // 3
            live = slot < count
            for coarse in range(32):
                start = 128 * which + 4 * coarse
                value = total[start : start + 3]
                value = jnp.where(live, value, jnp.zeros_like(value))
                out_ref[index, :, 128 * coarse : 128 * coarse + 128] = value.astype(jnp.bfloat16)


def body(spectra, pair_blocks, block_count):
    values = spectra.reshape(SEGS * 3, 2, WIDTH)
    pairs = pair_blocks[0].T
    first, twiddle, second = (jnp.asarray(value) for value in constants())
    f32, bf16 = jnp.float32, jnp.bfloat16
    anywhere = pl.BlockSpec(memory_space=pl.ANY)
    middle = pl.pallas_call(
        kernel,
        out_shape=jax.ShapeDtypeStruct((CHUNKS, 2, TILES * 8, 128), bf16),
        in_specs=[anywhere] * 4,
        out_specs=anywhere,
        scratch_shapes=[
            VMEM(values.shape, bf16),
            VMEM(first.shape, bf16),
            VMEM(twiddle.shape, f32),
            VMEM((31, 3, 8, 128), bf16),
            VMEM((2, 128, 128), f32),
            VMEM((CHUNKS, 3, 8, 128), bf16),
            VMEM((NX, NZ, NC, HOURS, 3, 8, 128), bf16),
            VMEM((STATIONS, HOURS, 3, 8, 128), f32),
            VMEM((STATIONS, HOURS, 3, 8, 128), f32),
            pltpu.SMEM((NC,) + pairs.shape, jnp.int32),
            VMEM((CHUNKS - 1, TILES, 8, 128), bf16),
            VMEM((CHUNKS, TILES, 8, 128), bf16),
            VMEM((CHUNKS, 2, TILES * 8, 128), bf16),
            DMA((3,)),
            DMA((3,)),
            DMA(()),
            DMA((2, 4)),
            DMA(()),
            DMA((2, 4)),
            DMA(()),
            DMA((CHUNKS,)),
            DMA(()),
        ],
        compiler_params=pltpu.CompilerParams(collective_id=0, has_side_effects=True),
        name="correlate",
    )(values, pairs, first, twiddle)
    at_once = GROUPS_AT_ONCE
    lags = pl.pallas_call(
        lags_kernel,
        grid=(GROUPS // at_once,),
        out_shape=jax.ShapeDtypeStruct((SHARE * 3, 3, LAGS), bf16),
        in_specs=[
            pl.BlockSpec(memory_space=pltpu.SMEM),
            pl.BlockSpec((CHUNKS, 2, 6 * LOCAL * at_once, 128), lambda i: (0, 0, i, 0)),
            pl.BlockSpec(second.shape, lambda i: (0, 0), pipeline_mode=pl.Buffered(1)),
        ],
        out_specs=pl.BlockSpec((2 * at_once, 3, LAGS), lambda i: (i, 0, 0)),
        name="lags",
    )(block_count, middle, second)
    return lags.reshape(1, SHARE, 1, 1, 3, 3, LAGS)


def solution(mesh):
    placed = (P("tm", "sta", None, None, None, None), P("sta", None, None), P("sta"))
    return jax.shard_map(
        body,
        mesh=mesh,
        in_specs=placed,
        out_specs=P("sta", "tm", None, None, None, None, None),
        check_vma=False,
    )
```

```python
import functools
import math

import jax
import jax.numpy as jnp
import numpy as np
from jax import lax
from jax.experimental import pallas as pl
from jax.experimental.pallas import tpu as pltpu
from jax.sharding import PartitionSpec as P

MESH = pl.DeviceIdType.MESH
VMEM = pltpu.VMEM
DMA = pltpu.SemaphoreType.DMA

SMOOTH = 64
epsilon = 1e-05

NY, NX, NZ, NC = 4, 4, 4, 2
SETS = 2
CHUNKS = 8
SOURCES = SETS * CHUNKS
F2 = 32
LOCAL = F2 // SOURCES
WIDTH = 2048
LAGS = 4096
STATIONS = 32
HOURS = 4
SEGS = 2
ROWS = SEGS * LOCAL
SHARE = 10
TILES = -(-SHARE * 9 * LOCAL // 8)
GROUPS = SHARE * 3 // 2
CUTS = (0, 5, 9, 14, 18, 23)


def constants():
    lane = np.arange(128)
    part, m, u = lane // 64, (lane // 16) % 4, lane % 16
    f1 = 4 * u + m
    fine = np.arange(128)
    angle = 2.0 * math.pi * ((f1[:, None] * fine[None, :]) % 128) / 128.0
    cos, sin = np.cos(angle), np.sin(angle)
    is_re = (part == 0)[:, None]
    first = np.concatenate([np.where(is_re, cos, -sin), np.where(is_re, sin, cos)], axis=1)
    f2 = np.arange(F2)
    turn = 2.0 * math.pi * (f2[:, None] * fine[None, :]) / LAGS
    sign = np.where(f2 % 2 == 0, 1.0, -1.0)[:, None] * WIDTH ** (-0.5)
    twiddle = np.stack([np.cos(turn) * sign, np.sin(turn) * sign], axis=0)
    twiddle = twiddle.reshape(2, SOURCES, 1, LOCAL, 128)
    twiddle = np.broadcast_to(twiddle, (2, SOURCES, 8 // LOCAL, LOCAL, 128))
    twiddle = twiddle.reshape(2, SOURCES, 8, 128).transpose(1, 0, 2, 3)
    coarse = np.arange(32)
    spin = 2.0 * math.pi * ((coarse[:, None] * f2[None, :]) % 32) / 32.0
    second = np.zeros((2, 2, 32, 4, 2, SOURCES, 8, LOCAL))
    for odd in range(2):
        for which in range(2):
            for comp in range(3):
                at = 2 * odd + 3 * which + comp
                for part_at, table in enumerate((np.cos(spin), -np.sin(spin))):
                    second[odd, which, :, comp, part_at, :, at, :] = table.reshape(32, SOURCES, LOCAL)
    second = second.reshape(2, 256, 2 * SOURCES * 8 * LOCAL)
    return (
        first.astype(jnp.bfloat16),
        twiddle.astype(np.float32),
        second.astype(jnp.bfloat16),
    )


def band():
    row = lax.broadcasted_iota(jnp.int32, (128, 128), 0)
    col = lax.broadcasted_iota(jnp.int32, (128, 128), 1)
    gap = row - col
    one, zero = jnp.float32(1.0), jnp.float32(0.0)
    same = jnp.where(jnp.abs(gap) <= SMOOTH, one, zero)
    before = jnp.where(gap >= SMOOTH, one, zero)
    after = jnp.where(gap <= -SMOOTH, one, zero)
    return jnp.concatenate([before, same, after], axis=0).astype(jnp.bfloat16)


def whiten_blocks(x_ref):
    fill = jnp.zeros((2, WIDTH), jnp.float32)
    re = jnp.concatenate([x_ref[:, 0, :].astype(jnp.float32), fill], axis=0)
    im = jnp.concatenate([x_ref[:, 1, :].astype(jnp.float32), fill], axis=0)
    blocks = WIDTH // 128

    def rows(value):
        return jnp.concatenate([value[:, 128 * k : 128 * k + 128] for k in range(blocks)], axis=0)

    re, im = rows(re), rows(im)
    amplitude = jnp.sqrt(re * re + im * im)
    high = amplitude.astype(jnp.bfloat16)
    low = (amplitude - high.astype(jnp.float32)).astype(jnp.bfloat16)
    weights = band()
    total = None
    for value in (high, low):
        value = value.astype(jnp.float32)
        edge = jnp.zeros((8, 128), jnp.float32)
        before = jnp.concatenate([edge, value[:-8]], axis=0)
        after = jnp.concatenate([value[8:], edge], axis=0)
        wide = jnp.concatenate([before, value, after], axis=1).astype(jnp.bfloat16)
        term = jnp.dot(wide, weights, preferred_element_type=jnp.float32)
        total = term if total is None else total + term
    row = lax.broadcasted_iota(jnp.int32, (128, 128), 0)
    col = lax.broadcasted_iota(jnp.int32, (128, 128), 1)
    position = (row // 8) * 128 + col
    lower = jnp.maximum(position - SMOOTH, 0)
    upper = jnp.minimum(position + SMOOTH, WIDTH - 1)
    bins = (upper - lower + 1).astype(jnp.float32)
    smoothed = total / bins
    scale = smoothed + epsilon
    return re / scale, im / scale


def station(x_at, z_at, core_at):
    return (x_at * NZ + z_at) * NC + core_at


def arrived(block, sem):
    pltpu.make_async_copy(block, block, sem).wait()


def kernel(x_hbm, pairs_ref, first_hbm, twiddle_hbm, out_ref,
           x_ref, first_ref, twiddle_ref, sent,
           flat, packed, every, left, swapped, lists, out_buf, daily, middle,
           const_sem, list_send, list_recv, one_send, one_recv, fwd_send, fwd_recv, day_send, day_recv, out_sem):
    y = lax.axis_index("tm")
    sta = lax.axis_index("sta")
    core = sta % NC
    column = sta // NC
    xx, zz = column // NZ, column % NZ
    chunks = (NC * y + core, NC * zz + core)

    def send(src, dst, send_sem, recv_sem, x_at, y_at, z_at, core_at):
        pltpu.make_async_remote_copy(
            src_ref=src,
            dst_ref=dst,
            send_sem=send_sem,
            recv_sem=recv_sem,
            device_id=(y_at, station(x_at, z_at, core_at)),
            device_id_type=MESH,
        ).start()

    load = pltpu.make_async_copy(x_hbm, x_ref, const_sem.at[0])
    load.start()
    barrier = pltpu.get_barrier_semaphore()
    greeted = 0
    for dx in (2, 1, 3, 0):
        for dy in (2, 1, 3, 0):
            for dz in (2, 1, 3, 0):
                if dx > 0 and dy > 0 and dz > 0:
                    continue
                for dc in range(NC):
                    if (dx, dy, dz, dc) == (0, 0, 0, 0):
                        continue
                    peer = station((xx + dx) % NX, (zz + dz) % NZ, (core + dc) % NC)
                    pl.semaphore_signal(
                        barrier, inc=1, device_id=((y + dy) % NY, peer), device_id_type=MESH
                    )
                    greeted += 1

    pltpu.make_async_copy(pairs_ref, lists.at[zz, core], list_recv.at[zz, core]).start()
    tables = [
        pltpu.make_async_copy(first_hbm, first_ref, const_sem.at[1]),
        pltpu.make_async_copy(twiddle_hbm, twiddle_ref, const_sem.at[2]),
    ]
    for table in tables:
        table.start()
    load.wait()

    white_re, white_im = whiten_blocks(x_ref)
    flat[0] = white_re
    flat[1] = white_im
    turned = []
    for row in range(SEGS * 3):
        pieces = []
        for part in range(2):
            tile = flat[part, pl.ds(row, 16, stride=8), :]
            for m in range(4):
                pieces.append(tile if m == 0 else pltpu.roll(tile, 128 - 32 * m, 1))
        stacked = jnp.concatenate(pieces, axis=0)
        turned.append(jnp.transpose(stacked, (1, 0))[:F2])
    for source in range(SOURCES):
        for comp in range(3):
            tile = jnp.concatenate(
                [turned[seg * 3 + comp][LOCAL * source : LOCAL * source + LOCAL] for seg in range(SEGS)],
                axis=0,
            )
            packed[source, comp] = tile.astype(jnp.bfloat16)

    pl.semaphore_wait(barrier, greeted)

    places = (xx * (1 - core) + zz * core, xx * (1 - core) + y * core)
    for dj, di in ((2, 2), (2, 1), (2, 3), (1, 2), (3, 2), (1, 1), (3, 3), (1, 3), (3, 1),
                   (2, 0), (0, 2), (1, 0), (3, 0), (0, 1), (0, 3), (0, 0)):
        for dc in range(NC):
            for bins in range(SETS):
                if (dj, di, dc) == (0, 0, 0):
                    continue
                core_at = (core + dc) % NC
                x_at = (xx + di * (1 - core)) % NX
                if bins == 0:
                    y_at, z_at = (y + dj) % NY, (zz + di * core) % NZ
                    chunk = NC * y_at + core_at
                else:
                    y_at, z_at = (y + di * core) % NY, (zz + dj) % NZ
                    chunk = NC * z_at + core_at
                send(packed.at[CHUNKS * bins + chunk], every.at[bins, xx, zz, core, y],
                     one_send, one_recv.at[bins, core, places[bins]], x_at, y_at, z_at, core_at)
    for bins in range(SETS):
        pltpu.make_async_copy(
            packed.at[CHUNKS * bins + chunks[bins]],
            every.at[bins, xx, zz, core, y],
            one_recv.at[bins, core, places[bins]],
        ).start()
    list_peers = [(dz, dc) for dz in (2, 1, 3, 0) for dc in range(NC) if (dz, dc) != (0, 0)]
    for at, (dz, dc) in enumerate(list_peers):
        send(pairs_ref, lists.at[zz, core], list_send.at[at], list_recv.at[zz, core],
             xx, y, (zz + dz) % NZ, (core + dc) % NC)

    lane = lax.broadcasted_iota(jnp.int32, (8, 128), 1)
    sub = lax.broadcasted_iota(jnp.int32, (8, 128), 0)
    is_re = lane < 64
    is_low = sub < 4
    is_even = (sub // 2) % 2 == 0
    sign = jnp.where(is_re, jnp.float32(-1.0), jnp.float32(1.0))

    def widen(bins, x_at, z_at, core_at):
        at = station(x_at, z_at, core_at)
        for pair in range(HOURS // 2):
            for comp in range(3):
                value = jnp.concatenate(
                    [every[bins, x_at, z_at, core_at, 2 * pair + hour, comp].astype(jnp.float32)
                     for hour in range(2)], axis=0
                )
                left[bins, at, pair, comp] = value
                swapped[bins, at, pair, comp] = pltpu.roll(value, 64, 1) * sign

    for d in (0, 1, 3, 2):
        for bins in range(SETS):
            for side in range(2):
                if side == 0:
                    spot = (xx + d) % NX
                    piece = every.at[0, spot, zz, 0] if bins == 0 else every.at[1, spot, :, 0, y]
                elif bins == 0:
                    spot = (zz + d) % NZ
                    piece = every.at[0, xx, spot, 1]
                else:
                    spot = (y + d) % NY
                    piece = every.at[1, xx, :, 1, spot]
                arrived(piece, one_recv.at[bins, side, spot])
                for to in (2, 1, 3):
                    if side == 1:
                        x_at, y_at, z_at, mine = (xx + to) % NX, y, zz, xx
                    elif bins == 0:
                        x_at, y_at, z_at, mine = xx, y, (zz + to) % NZ, zz
                    else:
                        x_at, y_at, z_at, mine = xx, (y + to) % NY, zz, y
                    send(piece, piece, fwd_send, fwd_recv.at[bins, side, mine], x_at, y_at, z_at, core)
    for d in range(4):
        widen(0, d, zz, 0)
        widen(0, xx, d, 1)
        widen(1, xx, d, 1)
    for to in (1, 3, 2):
        x_at, z_at, y_at = (xx + to) % NX, (zz + to) % NZ, (y + to) % NY
        arrived(every.at[0, :, z_at, 0], fwd_recv.at[0, 0, z_at])
        for d in range(4):
            widen(0, d, z_at, 0)
        for bins in range(SETS):
            arrived(every.at[bins, x_at, :, 1], fwd_recv.at[bins, 1, x_at])
            for d in range(4):
                widen(bins, x_at, d, 1)
        arrived(every.at[1, :, :, 0, y_at], fwd_recv.at[1, 0, y_at])
    for x_at in range(NX):
        for z_at in range(NZ):
            widen(1, x_at, z_at, 0)
    for z_at in range(NZ):
        for core_at in range(NC):
            arrived(lists.at[z_at, core_at], list_recv.at[z_at, core_at])

    def slot_products(bins, first, second):
        plain, crossed = [None] * 9, [None] * 9
        for pair in range(HOURS // 2):
            one = [left[bins, first, pair, comp] for comp in range(3)]
            turn = [swapped[bins, first, pair, comp] for comp in range(3)]
            two = [left[bins, second, pair, comp] for comp in range(3)]
            for a in range(3):
                for b in range(3):
                    at = 3 * a + b
                    p, q = one[a] * two[b], turn[a] * two[b]
                    plain[at] = p if pair == 0 else plain[at] + p
                    crossed[at] = q if pair == 0 else crossed[at] + q
        joined = []
        for at in range(9):
            keep = jnp.where(is_re, plain[at], crossed[at])
            move = jnp.where(is_re, crossed[at], plain[at])
            joined.append(keep + pltpu.roll(move, 64, 1))
        return joined

    def fold(one, two, mask, distance):
        keep = jnp.where(mask, one, two)
        move = jnp.where(mask, two, one)
        return keep + pltpu.roll(move, distance, 0)

    def fill(target, bins, z_at, core_at, first_slot):
        def make(slot, slots, tile):
            values = []
            for at in range(slots):
                values += slot_products(bins, lists[z_at, core_at, 0, slot + at], lists[z_at, core_at, 1, slot + at])
            values += values[-2:] * ((-len(values) % 4) // 2)
            for at in range(len(values) // 4):
                a, b, c, d = values[4 * at : 4 * at + 4]
                target[tile + at] = fold(
                    fold(a, b, is_even, 2), fold(c, d, is_even, 2), is_low, 4
                ).astype(jnp.bfloat16)

        def step(at, carry):
            make(first_slot + 4 * at, 4, 9 * at)
            return carry

        lax.fori_loop(0, SHARE // 4, step, 0)
        make(first_slot + SHARE // 4 * 4, SHARE % 4, SHARE // 4 * 9)

    offsets = ((2, 0), (2, 1), (1, 0), (1, 1), (3, 0), (3, 1), (0, 1))
    for at, (d, dc) in enumerate(offsets):
        for bins in range(SETS):
            core_at = (core + dc) % NC
            y_at, z_at = ((y + d) % NY, zz) if bins == 0 else (y, (zz + d) % NZ)
            fill(out_buf.at[bins, at], bins, z_at, core_at, SHARE * y_at)
            send(out_buf.at[bins, at], daily.at[bins, chunks[bins]], day_send,
                 day_recv.at[bins, chunks[bins]], xx, y_at, z_at, core_at)
    for bins in range(SETS):
        fill(daily.at[bins, chunks[bins]], bins, zz, core, SHARE * y)

    for table in tables:
        table.wait()

    def stage_one(bins, chunk):
        rows = daily[bins, chunk].astype(jnp.float32).reshape(TILES * 8, 128).astype(jnp.bfloat16)
        product = jnp.dot(rows, first_ref[...], preferred_element_type=jnp.float32)
        re = product[:, :128].reshape(TILES, 8, 128)
        im = product[:, 128:].reshape(TILES, 8, 128)
        source = CHUNKS * bins + chunk
        turn_re, turn_im = twiddle_ref[source, 0], twiddle_ref[source, 1]
        middle[source, 0] = (re * turn_re - im * turn_im).astype(jnp.bfloat16)
        middle[source, 1] = (re * turn_im + im * turn_re).astype(jnp.bfloat16)
        pltpu.make_async_copy(middle.at[source], out_ref.at[source], out_sem).start()

    for d, dc in ((0, 0), (0, 1), (2, 0), (2, 1), (1, 0), (1, 1), (3, 0), (3, 1)):
        for bins in range(SETS):
            at = (y if bins == 0 else zz) + 4 - d
            chunk = NC * (at % 4) + (core + dc) % NC
            if (d, dc) != (0, 0):
                arrived(daily.at[bins, chunk], day_recv.at[bins, chunk])
            stage_one(bins, chunk)

    arrived(middle, out_sem)
    for at in range(7):
        arrived(lists.at[0, 0], list_send.at[at])
    arrived(sent, one_send)
    arrived(every.at[:, pl.ds(0, 3)], fwd_send)
    arrived(out_buf, day_send)


def lags_kernel(count_ref, middle_hbm, second_hbm, out_ref, middle, second, staged, in_sem, second_sem, out_sem):
    first_slot = lax.axis_index("tm") * SHARE
    count = count_ref[0]
    table = pltpu.make_async_copy(second_hbm, second, second_sem)
    table.start()
    loads = []
    for at in range(len(CUTS) - 1):
        span = pl.ds(CUTS[at], CUTS[at + 1] - CUTS[at])
        load = pltpu.make_async_copy(middle_hbm.at[:, :, span], middle.at[:, :, span], in_sem.at[at])
        load.start()
        loads.append(load)
    table.wait()
    stores = []
    for at, load in enumerate(loads):
        load.wait()
        for group in range(3 * at, 3 * at + 3):
            tile = 3 * group // 2
            columns = jnp.concatenate(
                [middle[source, part, tile : tile + 2].astype(jnp.float32).reshape(16, 128)
                 for part in range(2) for source in range(SOURCES)], axis=0
            ).astype(jnp.bfloat16)
            total = jnp.dot(second[group % 2], columns, preferred_element_type=jnp.float32)
            for which in range(2):
                index = 2 * group + which
                live = first_slot + index // 3 < count
                for coarse in range(32):
                    start = 128 * which + 4 * coarse
                    value = total[start : start + 3]
                    value = jnp.where(live, value, jnp.zeros_like(value))
                    staged[index, :, 128 * coarse : 128 * coarse + 128] = value.astype(jnp.bfloat16)
        block = pl.ds(6 * at, 6)
        store = pltpu.make_async_copy(staged.at[block], out_ref.at[block], out_sem.at[at])
        store.start()
        stores.append(store)
    for store in stores:
        store.wait()


def body(spectra, pair_blocks, block_count):
    values = spectra.reshape(SEGS * 3, 2, WIDTH)
    pairs = pair_blocks[0].T
    first, twiddle, second = (jnp.asarray(value) for value in constants())
    f32, bf16 = jnp.float32, jnp.bfloat16
    anywhere = pl.BlockSpec(memory_space=pl.ANY)
    middle_shape = (SOURCES, 2, TILES, 8, 128)
    middle = pl.pallas_call(
        kernel,
        out_shape=jax.ShapeDtypeStruct(middle_shape, bf16),
        in_specs=[anywhere] * 4,
        out_specs=anywhere,
        scratch_shapes=[
            VMEM(values.shape, bf16),
            VMEM(first.shape, bf16),
            VMEM(twiddle.shape, f32),
            VMEM((31 * SETS, 3, ROWS, 128), bf16),
            VMEM((2, 128, 128), f32),
            VMEM((SOURCES, 3, ROWS, 128), bf16),
            VMEM((SETS, NX, NZ, NC, HOURS, 3, ROWS, 128), bf16),
            VMEM((SETS, STATIONS, HOURS // 2, 3, 8, 128), f32),
            VMEM((SETS, STATIONS, HOURS // 2, 3, 8, 128), f32),
            pltpu.SMEM((NZ, NC) + pairs.shape, jnp.int32),
            VMEM((SETS, 7, TILES, 8, 128), bf16),
            VMEM((SETS, CHUNKS, TILES, 8, 128), bf16),
            VMEM(middle_shape, bf16),
            DMA((3,)),
            DMA((7,)),
            DMA((NZ, NC)),
            DMA(()),
            DMA((SETS, 2, 4)),
            DMA(()),
            DMA((SETS, 2, 4)),
            DMA(()),
            DMA((SETS, CHUNKS)),
            DMA(()),
        ],
        compiler_params=pltpu.CompilerParams(collective_id=0, has_side_effects=True),
        name="correlate",
    )(values, pairs, first, twiddle)
    lags = pl.pallas_call(
        lags_kernel,
        out_shape=jax.ShapeDtypeStruct((SHARE * 3, 3, LAGS), bf16),
        in_specs=[pl.BlockSpec(memory_space=pltpu.SMEM), anywhere, anywhere],
        out_specs=anywhere,
        scratch_shapes=[
            VMEM(middle_shape, bf16),
            VMEM(second.shape, bf16),
            VMEM((SHARE * 3, 3, LAGS), bf16),
            DMA((len(CUTS) - 1,)),
            DMA(()),
            DMA((len(CUTS) - 1,)),
        ],
        name="lags",
    )(block_count, middle, second)
    return lags.reshape(1, SHARE, 1, 1, 3, 3, LAGS)


def solution(mesh):
    placed = (P("tm", "sta", None, None, None, None), P("sta", None, None), P("sta"))
    return jax.shard_map(
        body,
        mesh=mesh,
        in_specs=placed,
        out_specs=P("sta", "tm", None, None, None, None, None),
        check_vma=False,
    )
```

```python
import functools
import math

import jax
import jax.numpy as jnp
import numpy as np
from jax import lax
from jax.experimental import pallas as pl
from jax.experimental.pallas import tpu as pltpu
from jax.sharding import PartitionSpec as P

MESH = pl.DeviceIdType.MESH
VMEM = pltpu.VMEM
DMA = pltpu.SemaphoreType.DMA

SMOOTH = 64
epsilon = 1e-05

NY, NX, NZ, NC = 4, 4, 4, 2
SETS = 2
CHUNKS = 8
SOURCES = SETS * CHUNKS
F2 = 32
LOCAL = F2 // SOURCES
WIDTH = 2048
LAGS = 4096
STATIONS = 32
HOURS = 4
SEGS = 2
ROWS = SEGS * LOCAL
SHARE = 10
TILES = -(-SHARE * 9 * LOCAL // 8)
GROUPS = SHARE * 3 // 2
CUTS = (0, 3, 6, 9, 12, 14, 15)


def constants():
    lane = np.arange(128)
    part, m, u = lane // 64, (lane // 16) % 4, lane % 16
    f1 = 4 * u + m
    fine = np.arange(128)
    angle = 2.0 * math.pi * ((f1[:, None] * fine[None, :]) % 128) / 128.0
    cos, sin = np.cos(angle), np.sin(angle)
    is_re = (part == 0)[:, None]
    first = np.concatenate([np.where(is_re, cos, -sin), np.where(is_re, sin, cos)], axis=1)
    f2 = np.arange(F2)
    turn = 2.0 * math.pi * (f2[:, None] * fine[None, :]) / LAGS
    sign = np.where(f2 % 2 == 0, 1.0, -1.0)[:, None] * WIDTH ** (-0.5)
    twiddle = np.stack([np.cos(turn) * sign, np.sin(turn) * sign], axis=0)
    twiddle = twiddle.reshape(2, SOURCES, 1, LOCAL, 128)
    twiddle = np.broadcast_to(twiddle, (2, SOURCES, 8 // LOCAL, LOCAL, 128))
    twiddle = twiddle.reshape(2, SOURCES, 8, 128).transpose(1, 0, 2, 3)
    coarse = np.arange(32)
    spin = 2.0 * math.pi * ((coarse[:, None] * f2[None, :]) % 32) / 32.0
    second = np.zeros((2, 2, 32, 4, 2, SOURCES, 8, LOCAL))
    for odd in range(2):
        for which in range(2):
            for comp in range(3):
                at = 2 * odd + 3 * which + comp
                for part_at, table in enumerate((np.cos(spin), -np.sin(spin))):
                    second[odd, which, :, comp, part_at, :, at, :] = table.reshape(32, SOURCES, LOCAL)
    second = second.reshape(2, 256, 2 * SOURCES * 8 * LOCAL)
    return (
        first.astype(jnp.bfloat16),
        twiddle.astype(np.float32),
        second.astype(jnp.bfloat16),
    )


def band():
    row = lax.broadcasted_iota(jnp.int32, (128, 128), 0)
    col = lax.broadcasted_iota(jnp.int32, (128, 128), 1)
    gap = row - col
    one, zero = jnp.float32(1.0), jnp.float32(0.0)
    same = jnp.where(jnp.abs(gap) <= SMOOTH, one, zero)
    before = jnp.where(gap >= SMOOTH, one, zero)
    after = jnp.where(gap <= -SMOOTH, one, zero)
    return jnp.concatenate([before, same, after], axis=0).astype(jnp.bfloat16)


def whiten_blocks(x_ref):
    fill = jnp.zeros((2, WIDTH), jnp.float32)
    re = jnp.concatenate([x_ref[:, 0, :].astype(jnp.float32), fill], axis=0)
    im = jnp.concatenate([x_ref[:, 1, :].astype(jnp.float32), fill], axis=0)
    blocks = WIDTH // 128

    def rows(value):
        return jnp.concatenate([value[:, 128 * k : 128 * k + 128] for k in range(blocks)], axis=0)

    re, im = rows(re), rows(im)
    amplitude = jnp.sqrt(re * re + im * im)
    high = amplitude.astype(jnp.bfloat16)
    low = (amplitude - high.astype(jnp.float32)).astype(jnp.bfloat16)
    weights = band()
    total = None
    for value in (high, low):
        value = value.astype(jnp.float32)
        edge = jnp.zeros((8, 128), jnp.float32)
        before = jnp.concatenate([edge, value[:-8]], axis=0)
        after = jnp.concatenate([value[8:], edge], axis=0)
        wide = jnp.concatenate([before, value, after], axis=1).astype(jnp.bfloat16)
        term = jnp.dot(wide, weights, preferred_element_type=jnp.float32)
        total = term if total is None else total + term
    row = lax.broadcasted_iota(jnp.int32, (128, 128), 0)
    col = lax.broadcasted_iota(jnp.int32, (128, 128), 1)
    position = (row // 8) * 128 + col
    lower = jnp.maximum(position - SMOOTH, 0)
    upper = jnp.minimum(position + SMOOTH, WIDTH - 1)
    bins = (upper - lower + 1).astype(jnp.float32)
    smoothed = total / bins
    scale = smoothed + epsilon
    return re / scale, im / scale


def station(x_at, z_at, core_at):
    return (x_at * NZ + z_at) * NC + core_at


def arrived(block, sem):
    pltpu.make_async_copy(block, block, sem).wait()


def kernel(x_hbm, pairs_ref, first_hbm, twiddle_hbm, middle,
           x_ref, first_ref, twiddle_ref, sent,
           flat, packed, every, left, swapped, lists, out_buf, daily,
           const_sem, list_send, list_recv, one_send, one_recv, fwd_send, fwd_recv, day_send, day_recv):
    y = lax.axis_index("tm")
    sta = lax.axis_index("sta")
    core = sta % NC
    column = sta // NC
    xx, zz = column // NZ, column % NZ
    chunks = (NC * y + core, NC * zz + core)

    def send(src, dst, send_sem, recv_sem, x_at, y_at, z_at, core_at):
        pltpu.make_async_remote_copy(
            src_ref=src,
            dst_ref=dst,
            send_sem=send_sem,
            recv_sem=recv_sem,
            device_id=(y_at, station(x_at, z_at, core_at)),
            device_id_type=MESH,
        ).start()

    load = pltpu.make_async_copy(x_hbm, x_ref, const_sem.at[0])
    load.start()
    barrier = pltpu.get_barrier_semaphore()
    greeted = 0
    for dx in (2, 1, 3, 0):
        for dy in (2, 1, 3, 0):
            for dz in (2, 1, 3, 0):
                if dx > 0 and dy > 0 and dz > 0:
                    continue
                for dc in range(NC):
                    if (dx, dy, dz, dc) == (0, 0, 0, 0):
                        continue
                    peer = station((xx + dx) % NX, (zz + dz) % NZ, (core + dc) % NC)
                    pl.semaphore_signal(
                        barrier, inc=1, device_id=((y + dy) % NY, peer), device_id_type=MESH
                    )
                    greeted += 1

    pltpu.make_async_copy(pairs_ref, lists.at[zz, core], list_recv.at[zz, core]).start()
    tables = [
        pltpu.make_async_copy(first_hbm, first_ref, const_sem.at[1]),
        pltpu.make_async_copy(twiddle_hbm, twiddle_ref, const_sem.at[2]),
    ]
    for table in tables:
        table.start()
    load.wait()

    white_re, white_im = whiten_blocks(x_ref)
    flat[0] = white_re
    flat[1] = white_im
    turned = []
    for row in range(SEGS * 3):
        pieces = []
        for part in range(2):
            tile = flat[part, pl.ds(row, 16, stride=8), :]
            for m in range(4):
                pieces.append(tile if m == 0 else pltpu.roll(tile, 128 - 32 * m, 1))
        stacked = jnp.concatenate(pieces, axis=0)
        turned.append(jnp.transpose(stacked, (1, 0))[:F2])
    for source in range(SOURCES):
        for comp in range(3):
            tile = jnp.concatenate(
                [turned[seg * 3 + comp][LOCAL * source : LOCAL * source + LOCAL] for seg in range(SEGS)],
                axis=0,
            )
            packed[source, comp] = tile.astype(jnp.bfloat16)

    pl.semaphore_wait(barrier, greeted)

    scatter, across = (y, zz), (zz, y)
    spots = tuple(NY * core + s_at for s_at in scatter)
    parts = tuple(core * ((s_at + 3) // 4) for s_at in scatter)
    places = tuple(xx * (1 - p) + w_at * p for p, w_at in zip(parts, across))

    def at_axes(bins, s_at, w_at):
        return (s_at, w_at) if bins == 0 else (w_at, s_at)

    for dj, di in ((2, 2), (2, 1), (2, 3), (1, 2), (3, 2), (1, 1), (3, 3), (1, 3), (3, 1),
                   (2, 0), (0, 2), (1, 0), (3, 0), (0, 1), (0, 3), (0, 0)):
        for dc in range(NC):
            for bins in range(SETS):
                if (dj, di, dc) == (0, 0, 0):
                    continue
                core_at = (core + dc) % NC
                s_at = (scatter[bins] + dj) % 4
                x_at = (xx + di * (1 - parts[bins])) % NX
                w_at = (across[bins] + di * parts[bins]) % 4
                y_at, z_at = at_axes(bins, s_at, w_at)
                send(packed.at[CHUNKS * bins + NC * s_at + core_at], every.at[bins, xx, across[bins], spots[bins]],
                     one_send, one_recv.at[bins, parts[bins], places[bins]], x_at, y_at, z_at, core_at)
    for bins in range(SETS):
        pltpu.make_async_copy(
            packed.at[CHUNKS * bins + chunks[bins]],
            every.at[bins, xx, across[bins], spots[bins]],
            one_recv.at[bins, parts[bins], places[bins]],
        ).start()
    list_peers = [(dz, dc) for dz in (2, 1, 3, 0) for dc in range(NC) if (dz, dc) != (0, 0)]
    for at, (dz, dc) in enumerate(list_peers):
        send(pairs_ref, lists.at[zz, core], list_send.at[at], list_recv.at[zz, core],
             xx, y, (zz + dz) % NZ, (core + dc) % NC)

    lane = lax.broadcasted_iota(jnp.int32, (8, 128), 1)
    sub = lax.broadcasted_iota(jnp.int32, (8, 128), 0)
    is_re = lane < 64
    is_low = sub < 4
    is_even = (sub // 2) % 2 == 0
    sign = jnp.where(is_re, jnp.float32(-1.0), jnp.float32(1.0))

    def widen(bins, x_at, z_at, core_at):
        at = station(x_at, z_at, core_at)
        for pair in range(HOURS // 2):
            for comp in range(3):
                hours = (2 * pair, 2 * pair + 1)
                if bins == 0:
                    halves = [every[0, x_at, z_at, NY * core_at + hour, comp] for hour in hours]
                else:
                    halves = [every[1, x_at, hour, NZ * core_at + z_at, comp] for hour in hours]
                value = jnp.concatenate([half.astype(jnp.float32) for half in halves], axis=0)
                left[bins, at, pair, comp] = value
                swapped[bins, at, pair, comp] = pltpu.roll(value, 64, 1) * sign

    split = (pl.ds(0, 5), pl.ds(5, 3))
    for d in (0, 1, 3, 2):
        for bins in range(SETS):
            for part in range(2):
                if part == 0:
                    spot = (xx + d) % NX
                    piece = every.at[bins, spot, across[bins], split[0]]
                else:
                    spot = (across[bins] + d) % 4
                    piece = every.at[bins, xx, spot, split[1]]
                arrived(piece, one_recv.at[bins, part, spot])
                for to in (2, 1, 3):
                    if part == 1:
                        x_at, y_at, z_at, mine = (xx + to) % NX, y, zz, xx
                    else:
                        y_at, z_at = at_axes(bins, scatter[bins], (across[bins] + to) % 4)
                        x_at, mine = xx, across[bins]
                    send(piece, piece, fwd_send, fwd_recv.at[bins, part, mine], x_at, y_at, z_at, core)
    for d in range(4):
        widen(0, d, zz, 0)
        if d > 0:
            widen(1, xx, d, 1)
    for to in (1, 3, 2):
        z_at = (zz + to) % NZ
        arrived(every.at[0, :, z_at, split[0]], fwd_recv.at[0, 0, z_at])
        for d in range(4):
            widen(0, d, z_at, 0)
    for d in range(4):
        widen(0, xx, d, 1)
    for to in (1, 3, 2):
        x_at = (xx + to) % NX
        for bins in range(SETS):
            arrived(every.at[bins, x_at, :, split[1]], fwd_recv.at[bins, 1, x_at])
            for d in range(bins, 4):
                widen(bins, x_at, d, 1)
    for to in (1, 3, 2):
        y_at = (y + to) % NY
        arrived(every.at[1, :, y_at, split[0]], fwd_recv.at[1, 0, y_at])
    for x_at in range(NX):
        for z_at in range(NZ):
            widen(1, x_at, z_at, 0)
        widen(1, x_at, 0, 1)
    for z_at in range(NZ):
        for core_at in range(NC):
            arrived(lists.at[z_at, core_at], list_recv.at[z_at, core_at])

    def slot_products(bins, first, second):
        plain, crossed = [None] * 9, [None] * 9
        for pair in range(HOURS // 2):
            one = [left[bins, first, pair, comp] for comp in range(3)]
            turn = [swapped[bins, first, pair, comp] for comp in range(3)]
            two = [left[bins, second, pair, comp] for comp in range(3)]
            for a in range(3):
                for b in range(3):
                    at = 3 * a + b
                    p, q = one[a] * two[b], turn[a] * two[b]
                    plain[at] = p if pair == 0 else plain[at] + p
                    crossed[at] = q if pair == 0 else crossed[at] + q
        joined = []
        for at in range(9):
            keep = jnp.where(is_re, plain[at], crossed[at])
            move = jnp.where(is_re, crossed[at], plain[at])
            joined.append(keep + pltpu.roll(move, 64, 1))
        return joined

    def fold(one, two, mask, distance):
        keep = jnp.where(mask, one, two)
        move = jnp.where(mask, two, one)
        return keep + pltpu.roll(move, distance, 0)

    def fill(target, bins, z_at, core_at, first_slot):
        def make(slot, slots, tile):
            values = []
            for at in range(slots):
                values += slot_products(bins, lists[z_at, core_at, 0, slot + at], lists[z_at, core_at, 1, slot + at])
            values += values[-2:] * ((-len(values) % 4) // 2)
            for at in range(len(values) // 4):
                a, b, c, d = values[4 * at : 4 * at + 4]
                target[tile + at] = fold(
                    fold(a, b, is_even, 2), fold(c, d, is_even, 2), is_low, 4
                ).astype(jnp.bfloat16)

        def step(at, carry):
            make(first_slot + 4 * at, 4, 9 * at)
            return carry

        lax.fori_loop(0, SHARE // 4, step, 0)
        make(first_slot + SHARE // 4 * 4, SHARE % 4, SHARE // 4 * 9)

    offsets = ((2, 0), (2, 1), (1, 0), (1, 1), (3, 0), (3, 1), (0, 1))
    for at, (d, dc) in enumerate(offsets):
        for bins in range(SETS):
            core_at = (core + dc) % NC
            y_at, z_at = ((y + d) % NY, zz) if bins == 0 else (y, (zz + d) % NZ)
            fill(out_buf.at[bins, at], bins, z_at, core_at, SHARE * y_at)
            send(out_buf.at[bins, at], daily.at[bins, chunks[bins]], day_send,
                 day_recv.at[bins, chunks[bins]], xx, y_at, z_at, core_at)
    for bins in range(SETS):
        fill(daily.at[bins, chunks[bins]], bins, zz, core, SHARE * y)

    for table in tables:
        table.wait()

    def stage_one(bins, chunk):
        rows = daily[bins, chunk].astype(jnp.float32).reshape(TILES * 8, 128).astype(jnp.bfloat16)
        product = jnp.dot(rows, first_ref[...], preferred_element_type=jnp.float32)
        re = product[:, :128].reshape(TILES, 8, 128)
        im = product[:, 128:].reshape(TILES, 8, 128)
        source = CHUNKS * bins + chunk
        turn_re, turn_im = twiddle_ref[source, 0], twiddle_ref[source, 1]
        middle[source, 0] = (re * turn_re - im * turn_im).astype(jnp.bfloat16)
        middle[source, 1] = (re * turn_im + im * turn_re).astype(jnp.bfloat16)

    for d, dc in ((0, 0), (0, 1), (2, 0), (2, 1), (1, 0), (1, 1), (3, 0), (3, 1)):
        for bins in range(SETS):
            at = (y if bins == 0 else zz) + 4 - d
            chunk = NC * (at % 4) + (core + dc) % NC
            if (d, dc) != (0, 0):
                arrived(daily.at[bins, chunk], day_recv.at[bins, chunk])
            stage_one(bins, chunk)

    for at in range(7):
        arrived(lists.at[0, 0], list_send.at[at])
    arrived(sent, one_send)
    arrived(every.at[:, pl.ds(0, 3)], fwd_send)
    arrived(out_buf, day_send)


def lags_kernel(count_ref, middle, second, out_ref, staged, out_sem):
    first_slot = lax.axis_index("tm") * SHARE
    count = count_ref[0]
    stores = []
    for at, (begin, end) in enumerate(zip(CUTS, CUTS[1:])):
        for group in range(begin, end):
            tile = 3 * group // 2
            columns = jnp.concatenate(
                [middle[source, part, tile : tile + 2].astype(jnp.float32).reshape(16, 128)
                 for part in range(2) for source in range(SOURCES)], axis=0
            ).astype(jnp.bfloat16)
            total = jnp.dot(second[group % 2], columns, preferred_element_type=jnp.float32)
            for which in range(2):
                index = 2 * group + which
                live = first_slot + index // 3 < count
                for coarse in range(32):
                    start = 128 * which + 4 * coarse
                    value = total[start : start + 3]
                    value = jnp.where(live, value, jnp.zeros_like(value))
                    staged[index, :, 128 * coarse : 128 * coarse + 128] = value.astype(jnp.bfloat16)
        block = pl.ds(2 * begin, 2 * (end - begin))
        store = pltpu.make_async_copy(staged.at[block], out_ref.at[block], out_sem.at[at])
        store.start()
        stores.append(store)
    for store in stores:
        store.wait()


def body(spectra, pair_blocks, block_count):
    values = spectra.reshape(SEGS * 3, 2, WIDTH)
    pairs = pair_blocks[0].T
    first, twiddle, second = (jnp.asarray(value) for value in constants())
    f32, bf16 = jnp.float32, jnp.bfloat16
    anywhere = pl.BlockSpec(memory_space=pl.ANY)
    middle_shape = (SOURCES, 2, TILES, 8, 128)
    in_vmem = pl.BlockSpec(memory_space=pltpu.VMEM)
    middle = pl.pallas_call(
        kernel,
        out_shape=jax.ShapeDtypeStruct(middle_shape, bf16),
        in_specs=[pl.BlockSpec(memory_space=pltpu.HBM)] * 4,
        out_specs=in_vmem,
        scratch_shapes=[
            VMEM(values.shape, bf16),
            VMEM(first.shape, bf16),
            VMEM(twiddle.shape, f32),
            VMEM((31 * SETS, 3, ROWS, 128), bf16),
            VMEM((2, 128, 128), f32),
            VMEM((SOURCES, 3, ROWS, 128), bf16),
            VMEM((SETS, NX, 4, NC * 4, 3, ROWS, 128), bf16),
            VMEM((SETS, STATIONS, HOURS // 2, 3, 8, 128), f32),
            VMEM((SETS, STATIONS, HOURS // 2, 3, 8, 128), f32),
            pltpu.SMEM((NZ, NC) + pairs.shape, jnp.int32),
            VMEM((SETS, 7, TILES, 8, 128), bf16),
            VMEM((SETS, CHUNKS, TILES, 8, 128), bf16),
            DMA((3,)),
            DMA((7,)),
            DMA((NZ, NC)),
            DMA(()),
            DMA((SETS, 2, 4)),
            DMA(()),
            DMA((SETS, 2, 4)),
            DMA(()),
            DMA((SETS, CHUNKS)),
        ],
        compiler_params=pltpu.CompilerParams(
            collective_id=0, has_side_effects=True, vmem_limit_bytes=24 << 20
        ),
        name="correlate",
    )(*(pltpu.with_memory_space_constraint(value, pltpu.HBM) for value in (values, pairs, first, twiddle)))
    lags = pl.pallas_call(
        lags_kernel,
        out_shape=jax.ShapeDtypeStruct((SHARE * 3, 3, LAGS), bf16),
        in_specs=[pl.BlockSpec(memory_space=pltpu.SMEM), in_vmem, in_vmem],
        out_specs=anywhere,
        scratch_shapes=[
            VMEM((SHARE * 3, 3, LAGS), bf16),
            DMA((len(CUTS) - 1,)),
        ],
        compiler_params=pltpu.CompilerParams(vmem_limit_bytes=16 << 20),
        name="lags",
    )(block_count, middle, second)
    return lags.reshape(1, SHARE, 1, 1, 3, 3, LAGS)


def solution(mesh):
    placed = (P("tm", "sta", None, None, None, None), P("sta", None, None), P("sta"))
    return jax.shard_map(
        body,
        mesh=mesh,
        in_specs=placed,
        out_specs=P("sta", "tm", None, None, None, None, None),
        check_vma=False,
    )
```

```python
import functools
import math

import jax
import jax.numpy as jnp
import numpy as np
from jax import lax
from jax.experimental import pallas as pl
from jax.experimental.pallas import tpu as pltpu
from jax.sharding import PartitionSpec as P

MESH = pl.DeviceIdType.MESH
VMEM = pltpu.VMEM
DMA = pltpu.SemaphoreType.DMA

SMOOTH = 64
epsilon = 1e-05

NY, NX, NZ, NC = 4, 4, 4, 2
SETS = 2
CHUNKS = 8
SOURCES = SETS * CHUNKS
F2 = 32
LOCAL = F2 // SOURCES
WIDTH = 2048
LAGS = 4096
STATIONS = 32
HOURS = 4
SEGS = 2
ROWS = SEGS * LOCAL
SHARE = 10
TILES = -(-SHARE * 9 * LOCAL // 8)
GROUPS = SHARE * 3 // 2
CUTS = (0, 3, 6, 9, 12, 14, 15)


GREETED = sorted(
    [d for d in np.ndindex(NX, NY, NZ) if 0 in d], key=lambda d: -sum(min(at, 4 - at) for at in d)
)


def constants():
    lane = np.arange(128)
    part, m, u = lane // 64, (lane // 16) % 4, lane % 16
    f1 = 4 * u + m
    fine = np.arange(128)
    angle = 2.0 * math.pi * ((f1[:, None] * fine[None, :]) % 128) / 128.0
    cos, sin = np.cos(angle), np.sin(angle)
    is_re = (part == 0)[:, None]
    first = np.concatenate([np.where(is_re, cos, -sin), np.where(is_re, sin, cos)], axis=1)
    f2 = np.arange(F2)
    turn = 2.0 * math.pi * (f2[:, None] * fine[None, :]) / LAGS
    sign = np.where(f2 % 2 == 0, 1.0, -1.0)[:, None] * WIDTH ** (-0.5)
    twiddle = np.stack([np.cos(turn) * sign, np.sin(turn) * sign], axis=0)
    twiddle = twiddle.reshape(2, SOURCES, 1, LOCAL, 128)
    twiddle = np.broadcast_to(twiddle, (2, SOURCES, 8 // LOCAL, LOCAL, 128))
    twiddle = twiddle.reshape(2, SOURCES, 8, 128).transpose(1, 0, 2, 3)
    coarse = np.arange(32)
    spin = 2.0 * math.pi * ((coarse[:, None] * f2[None, :]) % 32) / 32.0
    second = np.zeros((2, 2, 32, 4, 2, SOURCES, 8, LOCAL))
    for odd in range(2):
        for which in range(2):
            for comp in range(3):
                at = 2 * odd + 3 * which + comp
                for part_at, table in enumerate((np.cos(spin), -np.sin(spin))):
                    second[odd, which, :, comp, part_at, :, at, :] = table.reshape(32, SOURCES, LOCAL)
    second = second.reshape(2, 256, 2 * SOURCES * 8 * LOCAL)
    return (
        first.astype(jnp.bfloat16),
        twiddle.astype(np.float32),
        second.astype(jnp.bfloat16),
    )


def band():
    row = lax.broadcasted_iota(jnp.int32, (128, 128), 0)
    col = lax.broadcasted_iota(jnp.int32, (128, 128), 1)
    gap = row - col
    one, zero = jnp.float32(1.0), jnp.float32(0.0)
    same = jnp.where(jnp.abs(gap) <= SMOOTH, one, zero)
    before = jnp.where(gap >= SMOOTH, one, zero)
    after = jnp.where(gap <= -SMOOTH, one, zero)
    return jnp.concatenate([before, same, after], axis=0).astype(jnp.bfloat16)


def whiten_blocks(x_ref):
    fill = jnp.zeros((2, WIDTH), jnp.float32)
    re = jnp.concatenate([x_ref[:, 0, :].astype(jnp.float32), fill], axis=0)
    im = jnp.concatenate([x_ref[:, 1, :].astype(jnp.float32), fill], axis=0)
    blocks = WIDTH // 128

    def rows(value):
        return jnp.concatenate([value[:, 128 * k : 128 * k + 128] for k in range(blocks)], axis=0)

    re, im = rows(re), rows(im)
    amplitude = jnp.sqrt(re * re + im * im)
    high = amplitude.astype(jnp.bfloat16)
    low = (amplitude - high.astype(jnp.float32)).astype(jnp.bfloat16)
    weights = band()
    total = None
    for value in (high, low):
        value = value.astype(jnp.float32)
        edge = jnp.zeros((8, 128), jnp.float32)
        before = jnp.concatenate([edge, value[:-8]], axis=0)
        after = jnp.concatenate([value[8:], edge], axis=0)
        wide = jnp.concatenate([before, value, after], axis=1).astype(jnp.bfloat16)
        term = jnp.dot(wide, weights, preferred_element_type=jnp.float32)
        total = term if total is None else total + term
    row = lax.broadcasted_iota(jnp.int32, (128, 128), 0)
    col = lax.broadcasted_iota(jnp.int32, (128, 128), 1)
    position = (row // 8) * 128 + col
    lower = jnp.maximum(position - SMOOTH, 0)
    upper = jnp.minimum(position + SMOOTH, WIDTH - 1)
    bins = (upper - lower + 1).astype(jnp.float32)
    smoothed = total / bins
    scale = smoothed + epsilon
    return re / scale, im / scale


def station(x_at, z_at, core_at):
    return (x_at * NZ + z_at) * NC + core_at


def arrived(block, sem):
    pltpu.make_async_copy(block, block, sem).wait()


def kernel(x_hbm, pairs_ref, first_hbm, twiddle_hbm, middle,
           x_ref, first_ref, twiddle_ref, sent,
           flat, packed, every, left, swapped, lists, out_buf, daily,
           const_sem, list_send, list_recv, one_send, one_recv, fwd_send, fwd_recv, day_send, day_recv):
    y = lax.axis_index("tm")
    sta = lax.axis_index("sta")
    core = sta % NC
    column = sta // NC
    xx, zz = column // NZ, column % NZ
    chunks = (NC * y + core, NC * zz + core)

    def send(src, dst, send_sem, recv_sem, x_at, y_at, z_at, core_at):
        pltpu.make_async_remote_copy(
            src_ref=src,
            dst_ref=dst,
            send_sem=send_sem,
            recv_sem=recv_sem,
            device_id=(y_at, station(x_at, z_at, core_at)),
            device_id_type=MESH,
        ).start()

    load = pltpu.make_async_copy(x_hbm, x_ref, const_sem.at[0])
    load.start()
    barrier = pltpu.get_barrier_semaphore()
    greeted = 0
    for dx, dy, dz in GREETED:
        for dc in range(NC):
            if (dx, dy, dz, dc) == (0, 0, 0, 0):
                continue
            peer = station((xx + dx) % NX, (zz + dz) % NZ, (core + dc) % NC)
            pl.semaphore_signal(barrier, inc=1, device_id=((y + dy) % NY, peer), device_id_type=MESH)
            greeted += 1

    pltpu.make_async_copy(pairs_ref, lists.at[zz, core], list_recv.at[zz, core]).start()
    tables = [
        pltpu.make_async_copy(first_hbm, first_ref, const_sem.at[1]),
        pltpu.make_async_copy(twiddle_hbm, twiddle_ref, const_sem.at[2]),
    ]
    for table in tables:
        table.start()
    load.wait()

    white_re, white_im = whiten_blocks(x_ref)
    flat[0] = white_re
    flat[1] = white_im
    turned = []
    for row in range(SEGS * 3):
        pieces = []
        for part in range(2):
            tile = flat[part, pl.ds(row, 16, stride=8), :]
            for m in range(4):
                pieces.append(tile if m == 0 else pltpu.roll(tile, 128 - 32 * m, 1))
        stacked = jnp.concatenate(pieces, axis=0)
        turned.append(jnp.transpose(stacked, (1, 0))[:F2])
    for source in range(SOURCES):
        for comp in range(3):
            tile = jnp.concatenate(
                [turned[seg * 3 + comp][LOCAL * source : LOCAL * source + LOCAL] for seg in range(SEGS)],
                axis=0,
            )
            packed[source, comp] = tile.astype(jnp.bfloat16)

    pl.semaphore_wait(barrier, greeted)

    scatter, across = (y, zz), (zz, y)
    spots = tuple(NY * core + s_at for s_at in scatter)
    parts = tuple(core * ((s_at + 3) // 4) for s_at in scatter)
    places = tuple(xx * (1 - p) + w_at * p for p, w_at in zip(parts, across))

    def at_axes(bins, s_at, w_at):
        return (s_at, w_at) if bins == 0 else (w_at, s_at)

    for dj, di in ((2, 2), (2, 1), (2, 3), (1, 2), (3, 2), (1, 1), (3, 3), (1, 3), (3, 1),
                   (2, 0), (0, 2), (1, 0), (3, 0), (0, 1), (0, 3), (0, 0)):
        for dc in range(NC):
            for bins in range(SETS):
                if (dj, di, dc) == (0, 0, 0):
                    continue
                core_at = (core + dc) % NC
                s_at = (scatter[bins] + dj) % 4
                x_at = (xx + di * (1 - parts[bins])) % NX
                w_at = (across[bins] + di * parts[bins]) % 4
                y_at, z_at = at_axes(bins, s_at, w_at)
                send(packed.at[CHUNKS * bins + NC * s_at + core_at], every.at[bins, xx, across[bins], spots[bins]],
                     one_send, one_recv.at[bins, parts[bins], places[bins]], x_at, y_at, z_at, core_at)
    for bins in range(SETS):
        pltpu.make_async_copy(
            packed.at[CHUNKS * bins + chunks[bins]],
            every.at[bins, xx, across[bins], spots[bins]],
            one_recv.at[bins, parts[bins], places[bins]],
        ).start()
    list_peers = [(dz, dc) for dz in (2, 1, 3, 0) for dc in range(NC) if (dz, dc) != (0, 0)]
    for at, (dz, dc) in enumerate(list_peers):
        send(pairs_ref, lists.at[zz, core], list_send.at[at], list_recv.at[zz, core],
             xx, y, (zz + dz) % NZ, (core + dc) % NC)

    lane = lax.broadcasted_iota(jnp.int32, (8, 128), 1)
    sub = lax.broadcasted_iota(jnp.int32, (8, 128), 0)
    is_re = lane < 64
    is_low = sub < 4
    is_even = (sub // 2) % 2 == 0
    sign = jnp.where(is_re, jnp.float32(-1.0), jnp.float32(1.0))

    def widen(bins, x_at, z_at, core_at):
        at = station(x_at, z_at, core_at)
        for pair in range(HOURS // 2):
            for comp in range(3):
                hours = (2 * pair, 2 * pair + 1)
                if bins == 0:
                    halves = [every[0, x_at, z_at, NY * core_at + hour, comp] for hour in hours]
                else:
                    halves = [every[1, x_at, hour, NZ * core_at + z_at, comp] for hour in hours]
                value = jnp.concatenate([half.astype(jnp.float32) for half in halves], axis=0)
                left[bins, at, pair, comp] = value
                swapped[bins, at, pair, comp] = pltpu.roll(value, 64, 1) * sign

    split = (pl.ds(0, 5), pl.ds(5, 3))
    for d in (0, 1, 3, 2):
        for bins in range(SETS):
            for part in range(2):
                if part == 0:
                    spot = (xx + d) % NX
                    piece = every.at[bins, spot, across[bins], split[0]]
                else:
                    spot = (across[bins] + d) % 4
                    piece = every.at[bins, xx, spot, split[1]]
                arrived(piece, one_recv.at[bins, part, spot])
                for to in (2, 1, 3):
                    if part == 1:
                        x_at, y_at, z_at, mine = (xx + to) % NX, y, zz, xx
                    else:
                        y_at, z_at = at_axes(bins, scatter[bins], (across[bins] + to) % 4)
                        x_at, mine = xx, across[bins]
                    send(piece, piece, fwd_send, fwd_recv.at[bins, part, mine], x_at, y_at, z_at, core)
    for d in range(4):
        widen(0, d, zz, 0)
        if d > 0:
            widen(1, xx, d, 1)
    for to in (1, 3, 2):
        z_at = (zz + to) % NZ
        arrived(every.at[0, :, z_at, split[0]], fwd_recv.at[0, 0, z_at])
        for d in range(4):
            widen(0, d, z_at, 0)
    for d in range(4):
        widen(0, xx, d, 1)
    for to in (1, 3, 2):
        x_at = (xx + to) % NX
        for bins in range(SETS):
            arrived(every.at[bins, x_at, :, split[1]], fwd_recv.at[bins, 1, x_at])
            for d in range(bins, 4):
                widen(bins, x_at, d, 1)
    for to in (1, 3, 2):
        y_at = (y + to) % NY
        arrived(every.at[1, :, y_at, split[0]], fwd_recv.at[1, 0, y_at])
    for x_at in range(NX):
        for z_at in range(NZ):
            widen(1, x_at, z_at, 0)
        widen(1, x_at, 0, 1)
    for z_at in range(NZ):
        for core_at in range(NC):
            arrived(lists.at[z_at, core_at], list_recv.at[z_at, core_at])

    def slot_products(bins, first, second):
        plain, crossed = [None] * 9, [None] * 9
        for pair in range(HOURS // 2):
            one = [left[bins, first, pair, comp] for comp in range(3)]
            turn = [swapped[bins, first, pair, comp] for comp in range(3)]
            two = [left[bins, second, pair, comp] for comp in range(3)]
            for a in range(3):
                for b in range(3):
                    at = 3 * a + b
                    p, q = one[a] * two[b], turn[a] * two[b]
                    plain[at] = p if pair == 0 else plain[at] + p
                    crossed[at] = q if pair == 0 else crossed[at] + q
        joined = []
        for at in range(9):
            keep = jnp.where(is_re, plain[at], crossed[at])
            move = jnp.where(is_re, crossed[at], plain[at])
            joined.append(keep + pltpu.roll(move, 64, 1))
        return joined

    def fold(one, two, mask, distance):
        keep = jnp.where(mask, one, two)
        move = jnp.where(mask, two, one)
        return keep + pltpu.roll(move, distance, 0)

    def fill(target, bins, z_at, core_at, first_slot):
        def make(slot, slots, tile):
            values = []
            for at in range(slots):
                values += slot_products(bins, lists[z_at, core_at, 0, slot + at], lists[z_at, core_at, 1, slot + at])
            values += values[-2:] * ((-len(values) % 4) // 2)
            for at in range(len(values) // 4):
                a, b, c, d = values[4 * at : 4 * at + 4]
                target[tile + at] = fold(
                    fold(a, b, is_even, 2), fold(c, d, is_even, 2), is_low, 4
                ).astype(jnp.bfloat16)

        def step(at, carry):
            make(first_slot + 4 * at, 4, 9 * at)
            return carry

        lax.fori_loop(0, SHARE // 4, step, 0)
        make(first_slot + SHARE // 4 * 4, SHARE % 4, SHARE // 4 * 9)

    offsets = ((2, 0), (1, 0), (3, 0), (2, 1), (1, 1), (3, 1), (0, 1))
    for at, (d, dc) in enumerate(offsets):
        for bins in range(SETS):
            core_at = (core + dc) % NC
            y_at, z_at = ((y + d) % NY, zz) if bins == 0 else (y, (zz + d) % NZ)
            fill(out_buf.at[bins, at], bins, z_at, core_at, SHARE * y_at)
            send(out_buf.at[bins, at], daily.at[bins, chunks[bins]], day_send,
                 day_recv.at[bins, chunks[bins]], xx, y_at, z_at, core_at)
    for bins in range(SETS):
        fill(daily.at[bins, chunks[bins]], bins, zz, core, SHARE * y)

    for table in tables:
        table.wait()

    def stage_one(bins, chunk):
        rows = daily[bins, chunk].reshape(TILES * 8, 128)
        product = jnp.dot(rows, first_ref[...], preferred_element_type=jnp.float32)
        re = product[:, :128].reshape(TILES, 8, 128)
        im = product[:, 128:].reshape(TILES, 8, 128)
        source = CHUNKS * bins + chunk
        turn_re, turn_im = twiddle_ref[source, 0], twiddle_ref[source, 1]
        middle[source, 0] = (re * turn_re - im * turn_im).astype(jnp.bfloat16)
        middle[source, 1] = (re * turn_im + im * turn_re).astype(jnp.bfloat16)

    for batch in (((0, 0), (2, 0)), ((1, 0), (3, 0)), ((0, 1), (2, 1)), ((1, 1), (3, 1))):
        ready = []
        for d, dc in batch:
            for bins in range(SETS):
                at = (y if bins == 0 else zz) + 4 - d
                chunk = NC * (at % 4) + (core + dc) % NC
                if (d, dc) != (0, 0):
                    arrived(daily.at[bins, chunk], day_recv.at[bins, chunk])
                ready.append((bins, chunk))
        for bins, chunk in ready:
            stage_one(bins, chunk)

    for at in range(7):
        arrived(lists.at[0, 0], list_send.at[at])
    arrived(sent, one_send)
    arrived(every.at[:, pl.ds(0, 3)], fwd_send)
    arrived(out_buf, day_send)


def lags_kernel(count_ref, middle, second, out_ref, staged, out_sem):
    first_slot = lax.axis_index("tm") * SHARE
    count = count_ref[0]
    stores = []
    for at, (begin, end) in enumerate(zip(CUTS, CUTS[1:])):
        for group in range(begin, end):
            tile = 3 * group // 2
            columns = jnp.concatenate(
                [middle[source, part, tile : tile + 2].astype(jnp.float32).reshape(16, 128)
                 for part in range(2) for source in range(SOURCES)], axis=0
            ).astype(jnp.bfloat16)
            total = jnp.dot(second[group % 2], columns, preferred_element_type=jnp.float32)
            for which in range(2):
                index = 2 * group + which
                live = first_slot + index // 3 < count
                for coarse in range(32):
                    start = 128 * which + 4 * coarse
                    value = total[start : start + 3]
                    value = jnp.where(live, value, jnp.zeros_like(value))
                    staged[index, :, 128 * coarse : 128 * coarse + 128] = value.astype(jnp.bfloat16)
        block = pl.ds(2 * begin, 2 * (end - begin))
        store = pltpu.make_async_copy(staged.at[block], out_ref.at[block], out_sem.at[at])
        store.start()
        stores.append(store)
    for store in stores:
        store.wait()


def body(spectra, pair_blocks, block_count):
    values = spectra.reshape(SEGS * 3, 2, WIDTH)
    pairs = pair_blocks[0].T
    first, twiddle, second = (jnp.asarray(value) for value in constants())
    f32, bf16 = jnp.float32, jnp.bfloat16
    anywhere = pl.BlockSpec(memory_space=pl.ANY)
    middle_shape = (SOURCES, 2, TILES, 8, 128)
    in_vmem = pl.BlockSpec(memory_space=pltpu.VMEM)
    middle = pl.pallas_call(
        kernel,
        out_shape=jax.ShapeDtypeStruct(middle_shape, bf16),
        in_specs=[pl.BlockSpec(memory_space=pltpu.HBM)] * 4,
        out_specs=in_vmem,
        scratch_shapes=[
            VMEM(values.shape, bf16),
            VMEM(first.shape, bf16),
            VMEM(twiddle.shape, f32),
            VMEM((31 * SETS, 3, ROWS, 128), bf16),
            VMEM((2, 128, 128), f32),
            VMEM((SOURCES, 3, ROWS, 128), bf16),
            VMEM((SETS, NX, 4, NC * 4, 3, ROWS, 128), bf16),
            VMEM((SETS, STATIONS, HOURS // 2, 3, 8, 128), f32),
            VMEM((SETS, STATIONS, HOURS // 2, 3, 8, 128), f32),
            pltpu.SMEM((NZ, NC) + pairs.shape, jnp.int32),
            VMEM((SETS, 7, TILES, 8, 128), bf16),
            VMEM((SETS, CHUNKS, TILES, 8, 128), bf16),
            DMA((3,)),
            DMA((7,)),
            DMA((NZ, NC)),
            DMA(()),
            DMA((SETS, 2, 4)),
            DMA(()),
            DMA((SETS, 2, 4)),
            DMA(()),
            DMA((SETS, CHUNKS)),
        ],
        compiler_params=pltpu.CompilerParams(
            collective_id=0, has_side_effects=True, vmem_limit_bytes=24 << 20
        ),
        name="correlate",
    )(*(pltpu.with_memory_space_constraint(value, pltpu.HBM) for value in (values, pairs, first, twiddle)))
    lags = pl.pallas_call(
        lags_kernel,
        out_shape=jax.ShapeDtypeStruct((SHARE * 3, 3, LAGS), bf16),
        in_specs=[pl.BlockSpec(memory_space=pltpu.SMEM), in_vmem, in_vmem],
        out_specs=anywhere,
        scratch_shapes=[
            VMEM((SHARE * 3, 3, LAGS), bf16),
            DMA((len(CUTS) - 1,)),
        ],
        compiler_params=pltpu.CompilerParams(vmem_limit_bytes=16 << 20),
        name="lags",
    )(block_count, middle, second)
    return lags.reshape(1, SHARE, 1, 1, 3, 3, LAGS)


def solution(mesh):
    placed = (P("tm", "sta", None, None, None, None), P("sta", None, None), P("sta"))
    return jax.shard_map(
        body,
        mesh=mesh,
        in_specs=placed,
        out_specs=P("sta", "tm", None, None, None, None, None),
        check_vma=False,
    )
```

```python
import functools
import math

import jax
import jax.numpy as jnp
import numpy as np
from jax import lax
from jax.experimental import pallas as pl
from jax.experimental.pallas import tpu as pltpu
from jax.sharding import PartitionSpec as P

MESH = pl.DeviceIdType.MESH
VMEM = pltpu.VMEM
DMA = pltpu.SemaphoreType.DMA

SMOOTH = 64
epsilon = 1e-05

NY, NX, NZ, NC = 4, 4, 4, 2
SETS = 2
CHUNKS = 8
SOURCES = SETS * CHUNKS
F2 = 32
LOCAL = F2 // SOURCES
WIDTH = 2048
LAGS = 4096
STATIONS = 32
HOURS = 4
SEGS = 2
ROWS = SEGS * LOCAL
SHARE = 10
TILES = -(-SHARE * 9 * LOCAL // 8)
GROUPS = SHARE * 3 // 2
CUTS = (0, 4, 8, 12, 15)


GREETED = sorted(
    [d for d in np.ndindex(NX, NY, NZ) if 0 in d], key=lambda d: -sum(min(at, 4 - at) for at in d)
)


def constants():
    lane = np.arange(128)
    part, m, u = lane // 64, (lane // 16) % 4, lane % 16
    f1 = 4 * u + m
    fine = np.arange(128)
    angle = 2.0 * math.pi * ((f1[:, None] * fine[None, :]) % 128) / 128.0
    cos, sin = np.cos(angle), np.sin(angle)
    is_re = (part == 0)[:, None]
    first = np.concatenate([np.where(is_re, cos, -sin), np.where(is_re, sin, cos)], axis=1)
    f2 = np.arange(F2)
    turn = 2.0 * math.pi * (f2[:, None] * fine[None, :]) / LAGS
    sign = np.where(f2 % 2 == 0, 1.0, -1.0)[:, None] * WIDTH ** (-0.5)
    twiddle = np.stack([np.cos(turn) * sign, np.sin(turn) * sign], axis=0)
    twiddle = twiddle.reshape(2, SOURCES, 1, LOCAL, 128)
    twiddle = np.broadcast_to(twiddle, (2, SOURCES, 8 // LOCAL, LOCAL, 128))
    twiddle = twiddle.reshape(2, SOURCES, 8, 128).transpose(1, 0, 2, 3)
    coarse = np.arange(32)
    spin = 2.0 * math.pi * ((coarse[:, None] * f2[None, :]) % 32) / 32.0
    second = np.zeros((2, 2, 32, 4, 2, SOURCES, 8, LOCAL))
    for odd in range(2):
        for which in range(2):
            for comp in range(3):
                at = 2 * odd + 3 * which + comp
                for part_at, table in enumerate((np.cos(spin), -np.sin(spin))):
                    second[odd, which, :, comp, part_at, :, at, :] = table.reshape(32, SOURCES, LOCAL)
    second = second.reshape(2, 256, 2 * SOURCES * 8 * LOCAL)
    return (
        first.astype(jnp.bfloat16),
        twiddle.astype(np.float32),
        second.astype(jnp.bfloat16),
    )


def band():
    row = lax.broadcasted_iota(jnp.int32, (128, 128), 0)
    col = lax.broadcasted_iota(jnp.int32, (128, 128), 1)
    gap = row - col
    one, zero = jnp.float32(1.0), jnp.float32(0.0)
    same = jnp.where(jnp.abs(gap) <= SMOOTH, one, zero)
    before = jnp.where(gap >= SMOOTH, one, zero)
    after = jnp.where(gap <= -SMOOTH, one, zero)
    return jnp.concatenate([before, same, after], axis=0).astype(jnp.bfloat16)


def whiten_blocks(x_ref):
    fill = jnp.zeros((2, WIDTH), jnp.float32)
    re = jnp.concatenate([x_ref[:, 0, :].astype(jnp.float32), fill], axis=0)
    im = jnp.concatenate([x_ref[:, 1, :].astype(jnp.float32), fill], axis=0)
    blocks = WIDTH // 128

    def rows(value):
        return jnp.concatenate([value[:, 128 * k : 128 * k + 128] for k in range(blocks)], axis=0)

    re, im = rows(re), rows(im)
    amplitude = jnp.sqrt(re * re + im * im)
    high = amplitude.astype(jnp.bfloat16)
    low = (amplitude - high.astype(jnp.float32)).astype(jnp.bfloat16)
    weights = band()
    total = None
    for value in (high, low):
        value = value.astype(jnp.float32)
        edge = jnp.zeros((8, 128), jnp.float32)
        before = jnp.concatenate([edge, value[:-8]], axis=0)
        after = jnp.concatenate([value[8:], edge], axis=0)
        wide = jnp.concatenate([before, value, after], axis=1).astype(jnp.bfloat16)
        term = jnp.dot(wide, weights, preferred_element_type=jnp.float32)
        total = term if total is None else total + term
    row = lax.broadcasted_iota(jnp.int32, (128, 128), 0)
    col = lax.broadcasted_iota(jnp.int32, (128, 128), 1)
    position = (row // 8) * 128 + col
    lower = jnp.maximum(position - SMOOTH, 0)
    upper = jnp.minimum(position + SMOOTH, WIDTH - 1)
    bins = (upper - lower + 1).astype(jnp.float32)
    smoothed = total / bins
    scale = smoothed + epsilon
    return re / scale, im / scale


def station(x_at, z_at, core_at):
    return (x_at * NZ + z_at) * NC + core_at


def arrived(block, sem):
    pltpu.make_async_copy(block, block, sem).wait()


def kernel(x_hbm, pairs_ref, first_hbm, twiddle_hbm, middle,
           x_ref, first_ref, twiddle_ref, sent,
           flat, packed, every, left, swapped, lists, out_buf, daily,
           const_sem, list_send, list_recv, one_send, one_recv, fwd_send, fwd_recv, day_send, day_recv):
    y = lax.axis_index("tm")
    sta = lax.axis_index("sta")
    core = sta % NC
    column = sta // NC
    xx, zz = column // NZ, column % NZ
    chunks = (NC * y + core, NC * zz + core)

    def send(src, dst, send_sem, recv_sem, x_at, y_at, z_at, core_at):
        pltpu.make_async_remote_copy(
            src_ref=src,
            dst_ref=dst,
            send_sem=send_sem,
            recv_sem=recv_sem,
            device_id=(y_at, station(x_at, z_at, core_at)),
            device_id_type=MESH,
        ).start()

    load = pltpu.make_async_copy(x_hbm, x_ref, const_sem.at[0])
    load.start()
    barrier = pltpu.get_barrier_semaphore()
    greeted = 0
    for dx, dy, dz in GREETED:
        for dc in range(NC):
            if (dx, dy, dz, dc) == (0, 0, 0, 0):
                continue
            peer = station((xx + dx) % NX, (zz + dz) % NZ, (core + dc) % NC)
            pl.semaphore_signal(barrier, inc=1, device_id=((y + dy) % NY, peer), device_id_type=MESH)
            greeted += 1

    pltpu.make_async_copy(pairs_ref, lists.at[zz, core], list_recv.at[zz, core]).start()
    tables = [
        pltpu.make_async_copy(first_hbm, first_ref, const_sem.at[1]),
        pltpu.make_async_copy(twiddle_hbm, twiddle_ref, const_sem.at[2]),
    ]
    for table in tables:
        table.start()
    load.wait()

    white_re, white_im = whiten_blocks(x_ref)
    flat[0] = white_re
    flat[1] = white_im
    turned = []
    for row in range(SEGS * 3):
        pieces = []
        for part in range(2):
            tile = flat[part, pl.ds(row, 16, stride=8), :]
            for m in range(4):
                pieces.append(tile if m == 0 else pltpu.roll(tile, 128 - 32 * m, 1))
        stacked = jnp.concatenate(pieces, axis=0)
        turned.append(jnp.transpose(stacked, (1, 0))[:F2])
    for source in range(SOURCES):
        for comp in range(3):
            tile = jnp.concatenate(
                [turned[seg * 3 + comp][LOCAL * source : LOCAL * source + LOCAL] for seg in range(SEGS)],
                axis=0,
            )
            packed[source, comp] = tile.astype(jnp.bfloat16)

    pl.semaphore_wait(barrier, greeted)

    scatter, across = (y, zz), (zz, y)
    spots = tuple(NY * core + s_at for s_at in scatter)
    parts = tuple(core * ((s_at + 3) // 4) for s_at in scatter)
    places = tuple(xx * (1 - p) + w_at * p for p, w_at in zip(parts, across))

    def at_axes(bins, s_at, w_at):
        return (s_at, w_at) if bins == 0 else (w_at, s_at)

    for dj, di in ((2, 2), (2, 1), (2, 3), (1, 2), (3, 2), (1, 1), (3, 3), (1, 3), (3, 1),
                   (2, 0), (0, 2), (1, 0), (3, 0), (0, 1), (0, 3), (0, 0)):
        for dc in range(NC):
            for bins in range(SETS):
                if (dj, di, dc) == (0, 0, 0):
                    continue
                core_at = (core + dc) % NC
                s_at = (scatter[bins] + dj) % 4
                x_at = (xx + di * (1 - parts[bins])) % NX
                w_at = (across[bins] + di * parts[bins]) % 4
                y_at, z_at = at_axes(bins, s_at, w_at)
                send(packed.at[CHUNKS * bins + NC * s_at + core_at], every.at[bins, xx, across[bins], spots[bins]],
                     one_send, one_recv.at[bins, parts[bins], places[bins]], x_at, y_at, z_at, core_at)
    for bins in range(SETS):
        pltpu.make_async_copy(
            packed.at[CHUNKS * bins + chunks[bins]],
            every.at[bins, xx, across[bins], spots[bins]],
            one_recv.at[bins, parts[bins], places[bins]],
        ).start()
    list_peers = [(dz, dc) for dz in (2, 1, 3, 0) for dc in range(NC) if (dz, dc) != (0, 0)]
    for at, (dz, dc) in enumerate(list_peers):
        send(pairs_ref, lists.at[zz, core], list_send.at[at], list_recv.at[zz, core],
             xx, y, (zz + dz) % NZ, (core + dc) % NC)

    lane = lax.broadcasted_iota(jnp.int32, (8, 128), 1)
    sub = lax.broadcasted_iota(jnp.int32, (8, 128), 0)
    is_re = lane < 64
    is_low = sub < 4
    is_even = (sub // 2) % 2 == 0
    sign = jnp.where(is_re, jnp.float32(-1.0), jnp.float32(1.0))

    def widen(bins, x_at, z_at, core_at):
        at = station(x_at, z_at, core_at)
        for pair in range(HOURS // 2):
            for comp in range(3):
                hours = (2 * pair, 2 * pair + 1)
                if bins == 0:
                    halves = [every[0, x_at, z_at, NY * core_at + hour, comp] for hour in hours]
                else:
                    halves = [every[1, x_at, hour, NZ * core_at + z_at, comp] for hour in hours]
                value = jnp.concatenate([half.astype(jnp.float32) for half in halves], axis=0)
                left[bins, at, pair, comp] = value
                swapped[bins, at, pair, comp] = pltpu.roll(value, 64, 1) * sign

    split = (pl.ds(0, 5), pl.ds(5, 3))
    for d in (0, 1, 3, 2):
        for bins in range(SETS):
            for part in range(2):
                if part == 0:
                    spot = (xx + d) % NX
                    piece = every.at[bins, spot, across[bins], split[0]]
                else:
                    spot = (across[bins] + d) % 4
                    piece = every.at[bins, xx, spot, split[1]]
                arrived(piece, one_recv.at[bins, part, spot])
                for to in (2, 1, 3):
                    if part == 1:
                        x_at, y_at, z_at, mine = (xx + to) % NX, y, zz, xx
                    else:
                        y_at, z_at = at_axes(bins, scatter[bins], (across[bins] + to) % 4)
                        x_at, mine = xx, across[bins]
                    send(piece, piece, fwd_send, fwd_recv.at[bins, part, mine], x_at, y_at, z_at, core)
    for d in range(4):
        widen(0, d, zz, 0)
        if d > 0:
            widen(1, xx, d, 1)
    for to in (1, 3, 2):
        z_at = (zz + to) % NZ
        arrived(every.at[0, :, z_at, split[0]], fwd_recv.at[0, 0, z_at])
        for d in range(4):
            widen(0, d, z_at, 0)
    for d in range(4):
        widen(0, xx, d, 1)
    for to in (1, 3, 2):
        x_at = (xx + to) % NX
        for bins in range(SETS):
            arrived(every.at[bins, x_at, :, split[1]], fwd_recv.at[bins, 1, x_at])
            for d in range(bins, 4):
                widen(bins, x_at, d, 1)
    for to in (1, 3, 2):
        y_at = (y + to) % NY
        arrived(every.at[1, :, y_at, split[0]], fwd_recv.at[1, 0, y_at])
    for x_at in range(NX):
        for z_at in range(NZ):
            widen(1, x_at, z_at, 0)
        widen(1, x_at, 0, 1)
    for z_at in range(NZ):
        for core_at in range(NC):
            arrived(lists.at[z_at, core_at], list_recv.at[z_at, core_at])

    def slot_products(bins, first, second):
        plain, crossed = [None] * 9, [None] * 9
        for pair in range(HOURS // 2):
            one = [left[bins, first, pair, comp] for comp in range(3)]
            turn = [swapped[bins, first, pair, comp] for comp in range(3)]
            two = [left[bins, second, pair, comp] for comp in range(3)]
            for a in range(3):
                for b in range(3):
                    at = 3 * a + b
                    p, q = one[a] * two[b], turn[a] * two[b]
                    plain[at] = p if pair == 0 else plain[at] + p
                    crossed[at] = q if pair == 0 else crossed[at] + q
        joined = []
        for at in range(9):
            keep = jnp.where(is_re, plain[at], crossed[at])
            move = jnp.where(is_re, crossed[at], plain[at])
            joined.append(keep + pltpu.roll(move, 64, 1))
        return joined

    def fold(one, two, mask, distance):
        keep = jnp.where(mask, one, two)
        move = jnp.where(mask, two, one)
        return keep + pltpu.roll(move, distance, 0)

    def fill(target, bins, z_at, core_at, first_slot):
        def make(slot, slots, tile):
            values = []
            for at in range(slots):
                values += slot_products(bins, lists[z_at, core_at, 0, slot + at], lists[z_at, core_at, 1, slot + at])
            values += values[-2:] * ((-len(values) % 4) // 2)
            for at in range(len(values) // 4):
                a, b, c, d = values[4 * at : 4 * at + 4]
                target[tile + at] = fold(
                    fold(a, b, is_even, 2), fold(c, d, is_even, 2), is_low, 4
                ).astype(jnp.bfloat16)

        for at in range(SHARE // 4):
            make(first_slot + 4 * at, 4, 9 * at)
        make(first_slot + SHARE // 4 * 4, SHARE % 4, SHARE // 4 * 9)

    offsets = ((2, 0), (1, 0), (3, 0), (2, 1), (1, 1), (3, 1), (0, 1))
    for at, (d, dc) in enumerate(offsets):
        for bins in range(SETS):
            core_at = (core + dc) % NC
            y_at, z_at = ((y + d) % NY, zz) if bins == 0 else (y, (zz + d) % NZ)
            fill(out_buf.at[bins, at], bins, z_at, core_at, SHARE * y_at)
            send(out_buf.at[bins, at], daily.at[bins, chunks[bins]], day_send,
                 day_recv.at[bins, chunks[bins]], xx, y_at, z_at, core_at)
    for bins in range(SETS):
        fill(daily.at[bins, chunks[bins]], bins, zz, core, SHARE * y)

    for table in tables:
        table.wait()

    def stage_one(bins, chunk):
        rows = daily[bins, chunk].reshape(TILES * 8, 128)
        product = jnp.dot(rows, first_ref[...], preferred_element_type=jnp.float32)
        re = product[:, :128].reshape(TILES, 8, 128)
        im = product[:, 128:].reshape(TILES, 8, 128)
        source = CHUNKS * bins + chunk
        turn_re, turn_im = twiddle_ref[source, 0], twiddle_ref[source, 1]
        middle[source, 0] = (re * turn_re - im * turn_im).astype(jnp.bfloat16)
        middle[source, 1] = (re * turn_im + im * turn_re).astype(jnp.bfloat16)

    for batch in (((0, 0), (2, 0)), ((1, 0), (3, 0)), ((0, 1), (2, 1)), ((1, 1), (3, 1))):
        ready = []
        for d, dc in batch:
            for bins in range(SETS):
                at = (y if bins == 0 else zz) + 4 - d
                chunk = NC * (at % 4) + (core + dc) % NC
                if (d, dc) != (0, 0):
                    arrived(daily.at[bins, chunk], day_recv.at[bins, chunk])
                ready.append((bins, chunk))
        for bins, chunk in ready:
            stage_one(bins, chunk)

    for at in range(7):
        arrived(lists.at[0, 0], list_send.at[at])
    arrived(sent, one_send)
    arrived(every.at[:, pl.ds(0, 3)], fwd_send)
    arrived(out_buf, day_send)


def lags_kernel(count_ref, middle, second, out_ref, staged, out_sem):
    first_slot = lax.axis_index("tm") * SHARE
    count = count_ref[0]
    stores = []
    for at, (begin, end) in enumerate(zip(CUTS, CUTS[1:])):
        for odd in (1, 0):
            groups = range(begin + odd, end, 2)
            columns = []
            for group in groups:
                tile = 3 * group // 2
                columns.append(jnp.concatenate(
                    [middle[source, part, tile : tile + 2].astype(jnp.float32).reshape(16, 128)
                     for part in range(2) for source in range(SOURCES)], axis=0
                ).astype(jnp.bfloat16))
            totals = jnp.dot(
                second[odd], jnp.concatenate(columns, axis=1), preferred_element_type=jnp.float32
            )
            for side, group in enumerate(groups):
                for which in range(2):
                    index = 2 * group + which
                    live = first_slot + index // 3 < count
                    for coarse in range(32):
                        start = 128 * which + 4 * coarse
                        value = totals[start : start + 3, 128 * side : 128 * side + 128]
                        value = jnp.where(live, value, jnp.zeros_like(value))
                        staged[index, :, 128 * coarse : 128 * coarse + 128] = value.astype(jnp.bfloat16)
        block = pl.ds(2 * begin, 2 * (end - begin))
        store = pltpu.make_async_copy(staged.at[block], out_ref.at[block], out_sem.at[at])
        store.start()
        stores.append(store)
    for store in stores:
        store.wait()


def body(spectra, pair_blocks, block_count):
    values = spectra.reshape(SEGS * 3, 2, WIDTH)
    pairs = pair_blocks[0].T
    first, twiddle, second = (jnp.asarray(value) for value in constants())
    f32, bf16 = jnp.float32, jnp.bfloat16
    anywhere = pl.BlockSpec(memory_space=pl.ANY)
    middle_shape = (SOURCES, 2, TILES, 8, 128)
    in_vmem = pl.BlockSpec(memory_space=pltpu.VMEM)
    middle = pl.pallas_call(
        kernel,
        out_shape=jax.ShapeDtypeStruct(middle_shape, bf16),
        in_specs=[pl.BlockSpec(memory_space=pltpu.HBM)] * 4,
        out_specs=in_vmem,
        scratch_shapes=[
            VMEM(values.shape, bf16),
            VMEM(first.shape, bf16),
            VMEM(twiddle.shape, f32),
            VMEM((31 * SETS, 3, ROWS, 128), bf16),
            VMEM((2, 128, 128), f32),
            VMEM((SOURCES, 3, ROWS, 128), bf16),
            VMEM((SETS, NX, 4, NC * 4, 3, ROWS, 128), bf16),
            VMEM((SETS, STATIONS, HOURS // 2, 3, 8, 128), f32),
            VMEM((SETS, STATIONS, HOURS // 2, 3, 8, 128), f32),
            pltpu.SMEM((NZ, NC) + pairs.shape, jnp.int32),
            VMEM((SETS, 7, TILES, 8, 128), bf16),
            VMEM((SETS, CHUNKS, TILES, 8, 128), bf16),
            DMA((3,)),
            DMA((7,)),
            DMA((NZ, NC)),
            DMA(()),
            DMA((SETS, 2, 4)),
            DMA(()),
            DMA((SETS, 2, 4)),
            DMA(()),
            DMA((SETS, CHUNKS)),
        ],
        compiler_params=pltpu.CompilerParams(
            collective_id=0, has_side_effects=True, vmem_limit_bytes=24 << 20
        ),
        name="correlate",
    )(*(pltpu.with_memory_space_constraint(value, pltpu.HBM) for value in (values, pairs, first, twiddle)))
    lags = pl.pallas_call(
        lags_kernel,
        out_shape=jax.ShapeDtypeStruct((SHARE * 3, 3, LAGS), bf16),
        in_specs=[pl.BlockSpec(memory_space=pltpu.SMEM), in_vmem, in_vmem],
        out_specs=anywhere,
        scratch_shapes=[
            VMEM((SHARE * 3, 3, LAGS), bf16),
            DMA((len(CUTS) - 1,)),
        ],
        compiler_params=pltpu.CompilerParams(vmem_limit_bytes=16 << 20),
        name="lags",
    )(block_count, middle, second)
    return lags.reshape(1, SHARE, 1, 1, 3, 3, LAGS)


def solution(mesh):
    placed = (P("tm", "sta", None, None, None, None), P("sta", None, None), P("sta"))
    return jax.shard_map(
        body,
        mesh=mesh,
        in_specs=placed,
        out_specs=P("sta", "tm", None, None, None, None, None),
        check_vma=False,
    )
```

```python
import functools
import math

import jax
import jax.numpy as jnp
import numpy as np
from jax import lax
from jax.experimental import pallas as pl
from jax.experimental.pallas import tpu as pltpu
from jax.sharding import PartitionSpec as P

MESH = pl.DeviceIdType.MESH
VMEM = pltpu.VMEM
DMA = pltpu.SemaphoreType.DMA

SMOOTH = 64
epsilon = 1e-05

NY, NX, NZ, NC = 4, 4, 4, 2
SETS = 2
CHUNKS = 8
SOURCES = SETS * CHUNKS
F2 = 32
LOCAL = F2 // SOURCES
WIDTH = 2048
LAGS = 4096
STATIONS = 32
HOURS = 4
SEGS = 2
ROWS = SEGS * LOCAL
SHARE = 10
TILES = -(-SHARE * 9 * LOCAL // 8)
GROUPS = SHARE * 3 // 2
CUTS = (0, 4, 8, 12, 15)


GREETED = sorted(
    [d for d in np.ndindex(NX, NY, NZ) if 0 in d], key=lambda d: -sum(min(at, 4 - at) for at in d)
)


def constants():
    lane = np.arange(128)
    part, m, u = lane // 64, (lane // 16) % 4, lane % 16
    f1 = 4 * u + m
    fine = np.arange(128)
    angle = 2.0 * math.pi * ((f1[:, None] * fine[None, :]) % 128) / 128.0
    cos, sin = np.cos(angle), np.sin(angle)
    is_re = (part == 0)[:, None]
    first = np.concatenate([np.where(is_re, cos, -sin), np.where(is_re, sin, cos)], axis=1)
    f2 = np.arange(F2)
    turn = 2.0 * math.pi * (f2[:, None] * fine[None, :]) / LAGS
    sign = np.where(f2 % 2 == 0, 1.0, -1.0)[:, None] * WIDTH ** (-0.5)
    twiddle = np.stack([np.cos(turn) * sign, np.sin(turn) * sign], axis=0)
    twiddle = twiddle.reshape(2, SOURCES, 1, LOCAL, 128)
    twiddle = np.broadcast_to(twiddle, (2, SOURCES, 8 // LOCAL, LOCAL, 128))
    twiddle = twiddle.reshape(2, SOURCES, 8, 128).transpose(1, 0, 2, 3)
    coarse = np.arange(32)
    spin = 2.0 * math.pi * ((coarse[:, None] * f2[None, :]) % 32) / 32.0
    second = np.zeros((2, 2, 32, 4, 2, SOURCES, 8, LOCAL))
    for odd in range(2):
        for which in range(2):
            for comp in range(3):
                at = 2 * odd + 3 * which + comp
                for part_at, table in enumerate((np.cos(spin), -np.sin(spin))):
                    second[odd, which, :, comp, part_at, :, at, :] = table.reshape(32, SOURCES, LOCAL)
    second = second.reshape(2, 256, 2 * SOURCES * 8 * LOCAL)
    return (
        first.astype(jnp.bfloat16),
        twiddle.astype(np.float32),
        second.astype(jnp.bfloat16),
    )


def band():
    row = lax.broadcasted_iota(jnp.int32, (128, 128), 0)
    col = lax.broadcasted_iota(jnp.int32, (128, 128), 1)
    gap = row - col
    one, zero = jnp.float32(1.0), jnp.float32(0.0)
    same = jnp.where(jnp.abs(gap) <= SMOOTH, one, zero)
    before = jnp.where(gap >= SMOOTH, one, zero)
    after = jnp.where(gap <= -SMOOTH, one, zero)
    return jnp.concatenate([before, same, after], axis=0).astype(jnp.bfloat16)


def whiten_blocks(x_ref):
    fill = jnp.zeros((2, WIDTH), jnp.float32)
    re = jnp.concatenate([x_ref[:, 0, :].astype(jnp.float32), fill], axis=0)
    im = jnp.concatenate([x_ref[:, 1, :].astype(jnp.float32), fill], axis=0)
    blocks = WIDTH // 128

    def rows(value):
        return jnp.concatenate([value[:, 128 * k : 128 * k + 128] for k in range(blocks)], axis=0)

    re, im = rows(re), rows(im)
    amplitude = jnp.sqrt(re * re + im * im)
    high = amplitude.astype(jnp.bfloat16)
    low = (amplitude - high.astype(jnp.float32)).astype(jnp.bfloat16)
    weights = band()
    total = None
    for value in (high, low):
        value = value.astype(jnp.float32)
        edge = jnp.zeros((8, 128), jnp.float32)
        before = jnp.concatenate([edge, value[:-8]], axis=0)
        after = jnp.concatenate([value[8:], edge], axis=0)
        wide = jnp.concatenate([before, value, after], axis=1).astype(jnp.bfloat16)
        term = jnp.dot(wide, weights, preferred_element_type=jnp.float32)
        total = term if total is None else total + term
    row = lax.broadcasted_iota(jnp.int32, (128, 128), 0)
    col = lax.broadcasted_iota(jnp.int32, (128, 128), 1)
    position = (row // 8) * 128 + col
    lower = jnp.maximum(position - SMOOTH, 0)
    upper = jnp.minimum(position + SMOOTH, WIDTH - 1)
    bins = (upper - lower + 1).astype(jnp.float32)
    smoothed = total / bins
    scale = smoothed + epsilon
    return re / scale, im / scale


def station(x_at, z_at, core_at):
    return (x_at * NZ + z_at) * NC + core_at


def arrived(block, sem):
    pltpu.make_async_copy(block, block, sem).wait()


def kernel(x_hbm, pairs_ref, first_hbm, twiddle_hbm, middle,
           x_ref, first_ref, twiddle_ref, sent,
           flat, packed, every, left, swapped, lists, out_buf, daily,
           const_sem, list_send, list_recv, one_send, one_recv, fwd_send, fwd_recv, day_send, day_recv):
    y = lax.axis_index("tm")
    sta = lax.axis_index("sta")
    core = sta % NC
    column = sta // NC
    xx, zz = column // NZ, column % NZ
    chunks = (NC * y + core, NC * zz + core)

    def send(src, dst, send_sem, recv_sem, x_at, y_at, z_at, core_at):
        pltpu.make_async_remote_copy(
            src_ref=src,
            dst_ref=dst,
            send_sem=send_sem,
            recv_sem=recv_sem,
            device_id=(y_at, station(x_at, z_at, core_at)),
            device_id_type=MESH,
        ).start()

    load = pltpu.make_async_copy(x_hbm, x_ref, const_sem.at[0])
    load.start()
    barrier = pltpu.get_barrier_semaphore()
    greeted = 0
    for dx, dy, dz in GREETED:
        for dc in range(NC):
            if (dx, dy, dz, dc) == (0, 0, 0, 0):
                continue
            peer = station((xx + dx) % NX, (zz + dz) % NZ, (core + dc) % NC)
            pl.semaphore_signal(barrier, inc=1, device_id=((y + dy) % NY, peer), device_id_type=MESH)
            greeted += 1

    pltpu.make_async_copy(pairs_ref, lists.at[zz, core], list_recv.at[zz, core]).start()
    tables = [
        pltpu.make_async_copy(first_hbm, first_ref, const_sem.at[1]),
        pltpu.make_async_copy(twiddle_hbm, twiddle_ref, const_sem.at[2]),
    ]
    for table in tables:
        table.start()
    load.wait()

    white_re, white_im = whiten_blocks(x_ref)
    flat[0] = white_re
    flat[1] = white_im
    turned = []
    for row in range(SEGS * 3):
        pieces = []
        for part in range(2):
            tile = flat[part, pl.ds(row, 16, stride=8), :]
            for m in range(4):
                pieces.append(tile if m == 0 else pltpu.roll(tile, 128 - 32 * m, 1))
        stacked = jnp.concatenate(pieces, axis=0)
        turned.append(jnp.transpose(stacked, (1, 0))[:F2])
    for source in range(SOURCES):
        for comp in range(3):
            tile = jnp.concatenate(
                [turned[seg * 3 + comp][LOCAL * source : LOCAL * source + LOCAL] for seg in range(SEGS)],
                axis=0,
            )
            packed[source, comp] = tile.astype(jnp.bfloat16)

    pl.semaphore_wait(barrier, greeted)

    scatter, across = (y, zz), (zz, y)
    spots = tuple(NY * core + s_at for s_at in scatter)
    parts = tuple(core * ((s_at + 3) // 4) for s_at in scatter)
    places = tuple(xx * (1 - p) + w_at * p for p, w_at in zip(parts, across))

    def at_axes(bins, s_at, w_at):
        return (s_at, w_at) if bins == 0 else (w_at, s_at)

    for dj, di in ((2, 2), (2, 1), (2, 3), (1, 2), (3, 2), (1, 1), (3, 3), (1, 3), (3, 1),
                   (2, 0), (0, 2), (1, 0), (3, 0), (0, 1), (0, 3), (0, 0)):
        for dc in range(NC):
            for bins in range(SETS):
                if (dj, di, dc) == (0, 0, 0):
                    continue
                core_at = (core + dc) % NC
                s_at = (scatter[bins] + dj) % 4
                x_at = (xx + di * (1 - parts[bins])) % NX
                w_at = (across[bins] + di * parts[bins]) % 4
                y_at, z_at = at_axes(bins, s_at, w_at)
                send(packed.at[CHUNKS * bins + NC * s_at + core_at], every.at[bins, xx, across[bins], spots[bins]],
                     one_send, one_recv.at[bins, parts[bins], places[bins]], x_at, y_at, z_at, core_at)
    for bins in range(SETS):
        pltpu.make_async_copy(
            packed.at[CHUNKS * bins + chunks[bins]],
            every.at[bins, xx, across[bins], spots[bins]],
            one_recv.at[bins, parts[bins], places[bins]],
        ).start()
    list_peers = [(dz, dc) for dz in (2, 1, 3, 0) for dc in range(NC) if (dz, dc) != (0, 0)]
    for at, (dz, dc) in enumerate(list_peers):
        send(pairs_ref, lists.at[zz, core], list_send.at[at], list_recv.at[zz, core],
             xx, y, (zz + dz) % NZ, (core + dc) % NC)

    lane = lax.broadcasted_iota(jnp.int32, (8, 128), 1)
    sub = lax.broadcasted_iota(jnp.int32, (8, 128), 0)
    is_re = lane < 64
    is_low = sub < 4
    is_even = (sub // 2) % 2 == 0
    sign = jnp.where(is_re, jnp.float32(-1.0), jnp.float32(1.0))

    def widen(bins, x_at, z_at, core_at, pairs=(0, 1)):
        at = station(x_at, z_at, core_at)
        for pair in pairs:
            for comp in range(3):
                hours = (2 * pair, 2 * pair + 1)
                if bins == 0:
                    halves = [every[0, x_at, z_at, NY * core_at + hour, comp] for hour in hours]
                else:
                    hours = [(y + hour) % HOURS for hour in hours]
                    halves = [every[1, x_at, hour, NZ * core_at + z_at, comp] for hour in hours]
                value = jnp.concatenate([half.astype(jnp.float32) for half in halves], axis=0)
                left[bins, at, pair, comp] = value
                swapped[bins, at, pair, comp] = pltpu.roll(value, 64, 1) * sign

    split = (pl.ds(0, 5), pl.ds(5, 3))
    for d in (0, 1, 3, 2):
        for bins in range(SETS):
            for part in range(2):
                if part == 0:
                    spot = (xx + d) % NX
                    piece = every.at[bins, spot, across[bins], split[0]]
                else:
                    spot = (across[bins] + d) % 4
                    piece = every.at[bins, xx, spot, split[1]]
                arrived(piece, one_recv.at[bins, part, spot])
                for to in (2, 1, 3):
                    if part == 1:
                        x_at, y_at, z_at, mine = (xx + to) % NX, y, zz, xx
                    else:
                        y_at, z_at = at_axes(bins, scatter[bins], (across[bins] + to) % 4)
                        x_at, mine = xx, across[bins]
                    send(piece, piece, fwd_send, fwd_recv.at[bins, part, mine], x_at, y_at, z_at, core)
    for d in range(4):
        widen(0, d, zz, 0)
        if d > 0:
            widen(1, xx, d, 1)
    for to in (1, 3, 2):
        z_at = (zz + to) % NZ
        arrived(every.at[0, :, z_at, split[0]], fwd_recv.at[0, 0, z_at])
        for d in range(4):
            widen(0, d, z_at, 0)
    for d in range(4):
        widen(0, xx, d, 1)
    for to in (1, 3, 2):
        x_at = (xx + to) % NX
        for bins in range(SETS):
            arrived(every.at[bins, x_at, :, split[1]], fwd_recv.at[bins, 1, x_at])
            for d in range(bins, 4):
                widen(bins, x_at, d, 1)
    for pair, late in ((0, (1,)), (1, (3, 2))):
        for to in late:
            y_at = (y + to) % NY
            arrived(every.at[1, :, y_at, split[0]], fwd_recv.at[1, 0, y_at])
        for x_at in range(NX):
            for z_at in range(NZ):
                widen(1, x_at, z_at, 0, (pair,))
            widen(1, x_at, 0, 1, (pair,))
    for z_at in range(NZ):
        for core_at in range(NC):
            arrived(lists.at[z_at, core_at], list_recv.at[z_at, core_at])

    def slot_products(bins, first, second):
        plain, crossed = [None] * 9, [None] * 9
        for pair in range(HOURS // 2):
            one = [left[bins, first, pair, comp] for comp in range(3)]
            turn = [swapped[bins, first, pair, comp] for comp in range(3)]
            two = [left[bins, second, pair, comp] for comp in range(3)]
            for a in range(3):
                for b in range(3):
                    at = 3 * a + b
                    p, q = one[a] * two[b], turn[a] * two[b]
                    plain[at] = p if pair == 0 else plain[at] + p
                    crossed[at] = q if pair == 0 else crossed[at] + q
        joined = []
        for at in range(9):
            keep = jnp.where(is_re, plain[at], crossed[at])
            move = jnp.where(is_re, crossed[at], plain[at])
            joined.append(keep + pltpu.roll(move, 64, 1))
        return joined

    def fold(one, two, mask, distance):
        keep = jnp.where(mask, one, two)
        move = jnp.where(mask, two, one)
        return keep + pltpu.roll(move, distance, 0)

    def fill(target, bins, z_at, core_at, first_slot):
        def make(slot, slots, tile):
            values = []
            for at in range(slots):
                values += slot_products(bins, lists[z_at, core_at, 0, slot + at], lists[z_at, core_at, 1, slot + at])
            values += values[-2:] * ((-len(values) % 4) // 2)
            for at in range(len(values) // 4):
                a, b, c, d = values[4 * at : 4 * at + 4]
                target[tile + at] = fold(
                    fold(a, b, is_even, 2), fold(c, d, is_even, 2), is_low, 4
                ).astype(jnp.bfloat16)

        for at in range(SHARE // 4):
            make(first_slot + 4 * at, 4, 9 * at)
        make(first_slot + SHARE // 4 * 4, SHARE % 4, SHARE // 4 * 9)

    offsets = ((2, 0), (1, 0), (3, 0), (2, 1), (1, 1), (3, 1), (0, 1))
    batches = (((0, 0), (2, 0)), ((1, 0), (3, 0)), ((0, 1), (2, 1)), ((1, 1), (3, 1)))
    batch_of = {offset: at for at, batch in enumerate(batches) for offset in batch}
    for at, (d, dc) in enumerate(offsets):
        for bins in range(SETS):
            core_at = (core + dc) % NC
            y_at, z_at = ((y + d) % NY, zz) if bins == 0 else (y, (zz + d) % NZ)
            fill(out_buf.at[bins, at], bins, z_at, core_at, SHARE * y_at)
            send(out_buf.at[bins, at], daily.at[bins, chunks[bins]], day_send,
                 day_recv.at[batch_of[d, dc]], xx, y_at, z_at, core_at)
    for bins in range(SETS):
        fill(daily.at[bins, chunks[bins]], bins, zz, core, SHARE * y)

    for table in tables:
        table.wait()

    def stage_one(bins, chunk):
        rows = daily[bins, chunk].reshape(TILES * 8, 128)
        product = jnp.dot(rows, first_ref[...], preferred_element_type=jnp.float32)
        re = product[:, :128].reshape(TILES, 8, 128)
        im = product[:, 128:].reshape(TILES, 8, 128)
        source = CHUNKS * bins + chunk
        turn_re, turn_im = twiddle_ref[source, 0], twiddle_ref[source, 1]
        middle[source, 0] = (re * turn_re - im * turn_im).astype(jnp.bfloat16)
        middle[source, 1] = (re * turn_im + im * turn_re).astype(jnp.bfloat16)

    for at, batch in enumerate(batches):
        ready = [
            (bins, NC * (((y if bins == 0 else zz) + 4 - d) % 4) + (core + dc) % NC)
            for d, dc in batch for bins in range(SETS)
        ]
        coming = SETS * sum(offset != (0, 0) for offset in batch)
        arrived(daily.at[0, pl.ds(0, coming)], day_recv.at[at])
        for bins, chunk in ready:
            stage_one(bins, chunk)

    for at in range(7):
        arrived(lists.at[0, 0], list_send.at[at])
    arrived(sent, one_send)
    arrived(every.at[:, pl.ds(0, 3)], fwd_send)
    arrived(out_buf, day_send)


def lags_kernel(count_ref, middle, second, out_ref, staged, out_sem):
    first_slot = lax.axis_index("tm") * SHARE
    count = count_ref[0]
    stores = []
    for at, (begin, end) in enumerate(zip(CUTS, CUTS[1:])):
        for odd in (1, 0):
            groups = range(begin + odd, end, 2)
            columns = []
            for group in groups:
                tile = 3 * group // 2
                columns.append(jnp.concatenate(
                    [middle[source, part, tile : tile + 2].astype(jnp.float32).reshape(16, 128)
                     for part in range(2) for source in range(SOURCES)], axis=0
                ).astype(jnp.bfloat16))
            totals = jnp.dot(
                second[odd], jnp.concatenate(columns, axis=1), preferred_element_type=jnp.float32
            )
            for side, group in enumerate(groups):
                for which in range(2):
                    index = 2 * group + which
                    live = first_slot + index // 3 < count
                    for coarse in range(32):
                        start = 128 * which + 4 * coarse
                        value = totals[start : start + 3, 128 * side : 128 * side + 128]
                        value = jnp.where(live, value, jnp.zeros_like(value))
                        staged[index, :, 128 * coarse : 128 * coarse + 128] = value.astype(jnp.bfloat16)
        block = pl.ds(2 * begin, 2 * (end - begin))
        store = pltpu.make_async_copy(staged.at[block], out_ref.at[block], out_sem.at[at])
        store.start()
        stores.append(store)
    for store in stores:
        store.wait()


def body(spectra, pair_blocks, block_count):
    values = spectra.reshape(SEGS * 3, 2, WIDTH)
    pairs = pair_blocks[0].T
    first, twiddle, second = (jnp.asarray(value) for value in constants())
    f32, bf16 = jnp.float32, jnp.bfloat16
    anywhere = pl.BlockSpec(memory_space=pl.ANY)
    middle_shape = (SOURCES, 2, TILES, 8, 128)
    in_vmem = pl.BlockSpec(memory_space=pltpu.VMEM)
    middle = pl.pallas_call(
        kernel,
        out_shape=jax.ShapeDtypeStruct(middle_shape, bf16),
        in_specs=[pl.BlockSpec(memory_space=pltpu.HBM)] * 4,
        out_specs=in_vmem,
        scratch_shapes=[
            VMEM(values.shape, bf16),
            VMEM(first.shape, bf16),
            VMEM(twiddle.shape, f32),
            VMEM((31 * SETS, 3, ROWS, 128), bf16),
            VMEM((2, 128, 128), f32),
            VMEM((SOURCES, 3, ROWS, 128), bf16),
            VMEM((SETS, NX, 4, NC * 4, 3, ROWS, 128), bf16),
            VMEM((SETS, STATIONS, HOURS // 2, 3, 8, 128), f32),
            VMEM((SETS, STATIONS, HOURS // 2, 3, 8, 128), f32),
            pltpu.SMEM((NZ, NC) + pairs.shape, jnp.int32),
            VMEM((SETS, 7, TILES, 8, 128), bf16),
            VMEM((SETS, CHUNKS, TILES, 8, 128), bf16),
            DMA((3,)),
            DMA((7,)),
            DMA((NZ, NC)),
            DMA(()),
            DMA((SETS, 2, 4)),
            DMA(()),
            DMA((SETS, 2, 4)),
            DMA(()),
            DMA((4,)),
        ],
        compiler_params=pltpu.CompilerParams(
            collective_id=0, has_side_effects=True, vmem_limit_bytes=24 << 20
        ),
        name="correlate",
    )(*(pltpu.with_memory_space_constraint(value, pltpu.HBM) for value in (values, pairs, first, twiddle)))
    lags = pl.pallas_call(
        lags_kernel,
        out_shape=jax.ShapeDtypeStruct((SHARE * 3, 3, LAGS), bf16),
        in_specs=[pl.BlockSpec(memory_space=pltpu.SMEM), in_vmem, in_vmem],
        out_specs=anywhere,
        scratch_shapes=[
            VMEM((SHARE * 3, 3, LAGS), bf16),
            DMA((len(CUTS) - 1,)),
        ],
        compiler_params=pltpu.CompilerParams(vmem_limit_bytes=16 << 20),
        name="lags",
    )(block_count, middle, second)
    return lags.reshape(1, SHARE, 1, 1, 3, 3, LAGS)


def solution(mesh):
    placed = (P("tm", "sta", None, None, None, None), P("sta", None, None), P("sta"))
    return jax.shard_map(
        body,
        mesh=mesh,
        in_specs=placed,
        out_specs=P("sta", "tm", None, None, None, None, None),
        check_vma=False,
    )
```

```python
import functools
import math

import jax
import jax.numpy as jnp
import numpy as np
from jax import lax
from jax.experimental import pallas as pl
from jax.experimental.pallas import tpu as pltpu
from jax.sharding import PartitionSpec as P

MESH = pl.DeviceIdType.MESH
VMEM = pltpu.VMEM
DMA = pltpu.SemaphoreType.DMA

SMOOTH = 64
epsilon = 1e-05

NY, NX, NZ, NC = 4, 4, 4, 2
SETS = 2
CHUNKS = 8
SOURCES = SETS * CHUNKS
F2 = 32
LOCAL = F2 // SOURCES
WIDTH = 2048
LAGS = 4096
STATIONS = 32
HOURS = 4
SEGS = 2
ROWS = SEGS * LOCAL
SHARE = 10
TILES = -(-SHARE * 9 * LOCAL // 8)
GROUPS = SHARE * 3 // 2
CUTS = (0, 4, 8, 12, 15)


GREETED = sorted(
    [d for d in np.ndindex(NX, NY, NZ) if 0 in d], key=lambda d: -sum(min(at, 4 - at) for at in d)
)


def constants():
    lane = np.arange(128)
    part, m, u = lane // 64, (lane // 16) % 4, lane % 16
    f1 = 4 * u + m
    fine = np.arange(128)
    angle = 2.0 * math.pi * ((f1[:, None] * fine[None, :]) % 128) / 128.0
    cos, sin = np.cos(angle), np.sin(angle)
    is_re = (part == 0)[:, None]
    first = np.concatenate([np.where(is_re, cos, -sin), np.where(is_re, sin, cos)], axis=1)
    f2 = np.arange(F2)
    turn = 2.0 * math.pi * (f2[:, None] * fine[None, :]) / LAGS
    sign = np.where(f2 % 2 == 0, 1.0, -1.0)[:, None] * WIDTH ** (-0.5)
    twiddle = np.stack([np.cos(turn) * sign, np.sin(turn) * sign], axis=0)
    twiddle = twiddle.reshape(2, SOURCES, 1, LOCAL, 128)
    twiddle = np.broadcast_to(twiddle, (2, SOURCES, 8 // LOCAL, LOCAL, 128))
    twiddle = twiddle.reshape(2, SOURCES, 8, 128).transpose(1, 0, 2, 3)
    coarse = np.arange(32)
    spin = 2.0 * math.pi * ((coarse[:, None] * f2[None, :]) % 32) / 32.0
    second = np.zeros((2, 2, 32, 4, 2, SOURCES, 8, LOCAL))
    for odd in range(2):
        for which in range(2):
            for comp in range(3):
                at = 2 * odd + 3 * which + comp
                for part_at, table in enumerate((np.cos(spin), -np.sin(spin))):
                    second[odd, which, :, comp, part_at, :, at, :] = table.reshape(32, SOURCES, LOCAL)
    second = second.reshape(2, 256, 2 * SOURCES * 8 * LOCAL)
    return (
        first.astype(jnp.bfloat16),
        twiddle.astype(np.float32),
        second.astype(jnp.bfloat16),
    )


def band():
    row = lax.broadcasted_iota(jnp.int32, (128, 128), 0)
    col = lax.broadcasted_iota(jnp.int32, (128, 128), 1)
    gap = row - col
    one, zero = jnp.float32(1.0), jnp.float32(0.0)
    same = jnp.where(jnp.abs(gap) <= SMOOTH, one, zero)
    before = jnp.where(gap >= SMOOTH, one, zero)
    after = jnp.where(gap <= -SMOOTH, one, zero)
    return jnp.concatenate([before, same, after], axis=0).astype(jnp.bfloat16)


def whiten_blocks(x_ref):
    fill = jnp.zeros((2, WIDTH), jnp.float32)
    re = jnp.concatenate([x_ref[:, 0, :].astype(jnp.float32), fill], axis=0)
    im = jnp.concatenate([x_ref[:, 1, :].astype(jnp.float32), fill], axis=0)
    blocks = WIDTH // 128

    def rows(value):
        return jnp.concatenate([value[:, 128 * k : 128 * k + 128] for k in range(blocks)], axis=0)

    re, im = rows(re), rows(im)
    amplitude = jnp.sqrt(re * re + im * im)
    high = amplitude.astype(jnp.bfloat16)
    low = (amplitude - high.astype(jnp.float32)).astype(jnp.bfloat16)
    weights = band()
    total = None
    for value in (high, low):
        value = value.astype(jnp.float32)
        edge = jnp.zeros((8, 128), jnp.float32)
        before = jnp.concatenate([edge, value[:-8]], axis=0)
        after = jnp.concatenate([value[8:], edge], axis=0)
        wide = jnp.concatenate([before, value, after], axis=1).astype(jnp.bfloat16)
        term = jnp.dot(wide, weights, preferred_element_type=jnp.float32)
        total = term if total is None else total + term
    row = lax.broadcasted_iota(jnp.int32, (128, 128), 0)
    col = lax.broadcasted_iota(jnp.int32, (128, 128), 1)
    position = (row // 8) * 128 + col
    lower = jnp.maximum(position - SMOOTH, 0)
    upper = jnp.minimum(position + SMOOTH, WIDTH - 1)
    bins = (upper - lower + 1).astype(jnp.float32)
    smoothed = total / bins
    scale = smoothed + epsilon
    return re / scale, im / scale


def station(x_at, z_at, core_at):
    return (x_at * NZ + z_at) * NC + core_at


def arrived(block, sem):
    pltpu.make_async_copy(block, block, sem).wait()


def kernel(x_hbm, pairs_ref, first_hbm, twiddle_hbm, middle,
           x_ref, first_ref, twiddle_ref, sent,
           flat, packed, every, left, swapped, lists, out_buf, daily,
           const_sem, list_send, list_recv, one_send, one_recv, fwd_send, fwd_recv, day_send, day_recv):
    y = lax.axis_index("tm")
    sta = lax.axis_index("sta")
    core = sta % NC
    column = sta // NC
    xx, zz = column // NZ, column % NZ
    chunks = (NC * y + core, NC * zz + core)

    def send(src, dst, send_sem, recv_sem, x_at, y_at, z_at, core_at):
        pltpu.make_async_remote_copy(
            src_ref=src,
            dst_ref=dst,
            send_sem=send_sem,
            recv_sem=recv_sem,
            device_id=(y_at, station(x_at, z_at, core_at)),
            device_id_type=MESH,
        ).start()

    load = pltpu.make_async_copy(x_hbm, x_ref, const_sem.at[0])
    load.start()
    barrier = pltpu.get_barrier_semaphore()
    greeted = 0
    for dx, dy, dz in GREETED:
        for dc in range(NC):
            if (dx, dy, dz, dc) == (0, 0, 0, 0):
                continue
            peer = station((xx + dx) % NX, (zz + dz) % NZ, (core + dc) % NC)
            pl.semaphore_signal(barrier, inc=1, device_id=((y + dy) % NY, peer), device_id_type=MESH)
            greeted += 1

    pltpu.make_async_copy(pairs_ref, lists.at[zz, core], list_recv.at[zz, core]).start()
    tables = [
        pltpu.make_async_copy(first_hbm, first_ref, const_sem.at[1]),
        pltpu.make_async_copy(twiddle_hbm, twiddle_ref, const_sem.at[2]),
    ]
    for table in tables:
        table.start()
    load.wait()

    white_re, white_im = whiten_blocks(x_ref)
    flat[0] = white_re
    flat[1] = white_im
    turned = []
    for row in range(SEGS * 3):
        pieces = []
        for part in range(2):
            tile = flat[part, pl.ds(row, 16, stride=8), :]
            for m in range(4):
                pieces.append(tile if m == 0 else pltpu.roll(tile, 128 - 32 * m, 1))
        stacked = jnp.concatenate(pieces, axis=0)
        turned.append(jnp.transpose(stacked, (1, 0))[:F2])
    for source in range(SOURCES):
        for comp in range(3):
            tile = jnp.concatenate(
                [turned[seg * 3 + comp][LOCAL * source : LOCAL * source + LOCAL] for seg in range(SEGS)],
                axis=0,
            )
            packed[source, comp] = tile.astype(jnp.bfloat16)

    pl.semaphore_wait(barrier, greeted)

    scatter, across = (y, zz), (zz, y)
    spots = tuple(NY * core + s_at for s_at in scatter)
    parts = tuple(core * ((s_at + 3) // 4) for s_at in scatter)
    places = tuple(xx * (1 - p) + w_at * p for p, w_at in zip(parts, across))

    def at_axes(bins, s_at, w_at):
        return (s_at, w_at) if bins == 0 else (w_at, s_at)

    for dj, di in ((2, 2), (2, 1), (2, 3), (1, 2), (3, 2), (1, 1), (3, 3), (1, 3), (3, 1),
                   (2, 0), (0, 2), (1, 0), (3, 0), (0, 1), (0, 3), (0, 0)):
        for dc in range(NC):
            for bins in range(SETS):
                if (dj, di, dc) == (0, 0, 0):
                    continue
                core_at = (core + dc) % NC
                s_at = (scatter[bins] + dj) % 4
                x_at = (xx + di * (1 - parts[bins])) % NX
                w_at = (across[bins] + di * parts[bins]) % 4
                y_at, z_at = at_axes(bins, s_at, w_at)
                send(packed.at[CHUNKS * bins + NC * s_at + core_at], every.at[bins, xx, across[bins], spots[bins]],
                     one_send, one_recv.at[bins, parts[bins], places[bins]], x_at, y_at, z_at, core_at)
    for bins in range(SETS):
        pltpu.make_async_copy(
            packed.at[CHUNKS * bins + chunks[bins]],
            every.at[bins, xx, across[bins], spots[bins]],
            one_recv.at[bins, parts[bins], places[bins]],
        ).start()
    list_peers = [(dz, dc) for dz in (2, 1, 3, 0) for dc in range(NC) if (dz, dc) != (0, 0)]
    for at, (dz, dc) in enumerate(list_peers):
        send(pairs_ref, lists.at[zz, core], list_send.at[at], list_recv.at[zz, core],
             xx, y, (zz + dz) % NZ, (core + dc) % NC)

    lane = lax.broadcasted_iota(jnp.int32, (8, 128), 1)
    sub = lax.broadcasted_iota(jnp.int32, (8, 128), 0)
    is_re = lane < 64
    is_low = sub < 4
    is_even = (sub // 2) % 2 == 0
    sign = jnp.where(is_re, jnp.float32(-1.0), jnp.float32(1.0))

    def widen(bins, x_at, z_at, core_at, pairs=(0, 1)):
        at = station(x_at, z_at, core_at)
        for pair in pairs:
            for comp in range(3):
                hours = (2 * pair, 2 * pair + 1)
                if bins == 0:
                    halves = [every[0, x_at, z_at, NY * core_at + hour, comp] for hour in hours]
                else:
                    hours = [(y + hour) % HOURS for hour in hours]
                    halves = [every[1, x_at, hour, NZ * core_at + z_at, comp] for hour in hours]
                value = jnp.concatenate([half.astype(jnp.float32) for half in halves], axis=0)
                left[bins, at, pair, comp] = value
                swapped[bins, at, pair, comp] = pltpu.roll(value, 64, 1) * sign

    split = (pl.ds(0, 5), pl.ds(5, 3))
    for d in (0, 1, 3, 2):
        for bins in range(SETS):
            for part in range(2):
                if part == 0:
                    spot = (xx + d) % NX
                    piece = every.at[bins, spot, across[bins], split[0]]
                else:
                    spot = (across[bins] + d) % 4
                    piece = every.at[bins, xx, spot, split[1]]
                arrived(piece, one_recv.at[bins, part, spot])
                for to in (2, 1, 3):
                    if part == 1:
                        x_at, y_at, z_at, mine = (xx + to) % NX, y, zz, xx
                    else:
                        y_at, z_at = at_axes(bins, scatter[bins], (across[bins] + to) % 4)
                        x_at, mine = xx, across[bins]
                    send(piece, piece, fwd_send, fwd_recv.at[bins, part, mine], x_at, y_at, z_at, core)
    for d in range(4):
        widen(0, d, zz, 0)
        if d > 0:
            widen(1, xx, d, 1)
    for to in (1, 3, 2):
        z_at = (zz + to) % NZ
        arrived(every.at[0, :, z_at, split[0]], fwd_recv.at[0, 0, z_at])
        for d in range(4):
            widen(0, d, z_at, 0)
    for d in range(4):
        widen(0, xx, d, 1)
    for to in (1, 3, 2):
        x_at = (xx + to) % NX
        for bins in range(SETS):
            arrived(every.at[bins, x_at, :, split[1]], fwd_recv.at[bins, 1, x_at])
            for d in range(bins, 4):
                widen(bins, x_at, d, 1)
    for pair, late in ((0, (1,)), (1, (3, 2))):
        for to in late:
            y_at = (y + to) % NY
            arrived(every.at[1, :, y_at, split[0]], fwd_recv.at[1, 0, y_at])
        for x_at in range(NX):
            for z_at in range(NZ):
                widen(1, x_at, z_at, 0, (pair,))
            widen(1, x_at, 0, 1, (pair,))
    for z_at in range(NZ):
        for core_at in range(NC):
            arrived(lists.at[z_at, core_at], list_recv.at[z_at, core_at])

    def slot_products(bins, first, second):
        plain, crossed = [None] * 9, [None] * 9
        for pair in range(HOURS // 2):
            one = [left[bins, first, pair, comp] for comp in range(3)]
            turn = [swapped[bins, first, pair, comp] for comp in range(3)]
            two = [left[bins, second, pair, comp] for comp in range(3)]
            for a in range(3):
                for b in range(3):
                    at = 3 * a + b
                    p, q = one[a] * two[b], turn[a] * two[b]
                    plain[at] = p if pair == 0 else plain[at] + p
                    crossed[at] = q if pair == 0 else crossed[at] + q
        joined = []
        for at in range(9):
            keep = jnp.where(is_re, plain[at], crossed[at])
            move = jnp.where(is_re, crossed[at], plain[at])
            joined.append(keep + pltpu.roll(move, 64, 1))
        return joined

    def fold(one, two, mask, distance):
        keep = jnp.where(mask, one, two)
        move = jnp.where(mask, two, one)
        return keep + pltpu.roll(move, distance, 0)

    def fill(target, bins, z_at, core_at, first_slot):
        def make(slot, slots, tile):
            values = []
            for at in range(slots):
                values += slot_products(bins, lists[z_at, core_at, 0, slot + at], lists[z_at, core_at, 1, slot + at])
            values += values[-2:] * ((-len(values) % 4) // 2)
            for at in range(len(values) // 4):
                a, b, c, d = values[4 * at : 4 * at + 4]
                target[tile + at] = fold(
                    fold(a, b, is_even, 2), fold(c, d, is_even, 2), is_low, 4
                ).astype(jnp.bfloat16)

        for at in range(SHARE // 4):
            make(first_slot + 4 * at, 4, 9 * at)
        make(first_slot + SHARE // 4 * 4, SHARE % 4, SHARE // 4 * 9)

    offsets = ((2, 0), (1, 0), (3, 0), (2, 1), (1, 1), (3, 1), (0, 1))
    batches = (((0, 0), (2, 0)), ((1, 0), (3, 0)), ((0, 1), (2, 1)), ((1, 1),), ((3, 1),))
    batch_of = {offset: at for at, batch in enumerate(batches) for offset in batch}
    for at, (d, dc) in enumerate(offsets):
        for bins in range(SETS):
            core_at = (core + dc) % NC
            y_at, z_at = ((y + d) % NY, zz) if bins == 0 else (y, (zz + d) % NZ)
            fill(out_buf.at[bins, at], bins, z_at, core_at, SHARE * y_at)
            send(out_buf.at[bins, at], daily.at[bins, chunks[bins]], day_send,
                 day_recv.at[batch_of[d, dc]], xx, y_at, z_at, core_at)
    for bins in range(SETS):
        fill(daily.at[bins, chunks[bins]], bins, zz, core, SHARE * y)

    for table in tables:
        table.wait()

    def stage_one(bins, chunk):
        rows = daily[bins, chunk].reshape(TILES * 8, 128)
        product = jnp.dot(rows, first_ref[...], preferred_element_type=jnp.float32)
        re = product[:, :128].reshape(TILES, 8, 128)
        im = product[:, 128:].reshape(TILES, 8, 128)
        source = CHUNKS * bins + chunk
        turn_re, turn_im = twiddle_ref[source, 0], twiddle_ref[source, 1]
        middle[source, 0] = (re * turn_re - im * turn_im).astype(jnp.bfloat16)
        middle[source, 1] = (re * turn_im + im * turn_re).astype(jnp.bfloat16)

    for at, batch in enumerate(batches):
        ready = [
            (bins, NC * (((y if bins == 0 else zz) + 4 - d) % 4) + (core + dc) % NC)
            for d, dc in batch for bins in range(SETS)
        ]
        coming = SETS * sum(offset != (0, 0) for offset in batch)
        arrived(daily.at[0, pl.ds(0, coming)], day_recv.at[at])
        for bins, chunk in ready:
            stage_one(bins, chunk)

    for at in range(7):
        arrived(lists.at[0, 0], list_send.at[at])
    arrived(sent, one_send)
    arrived(every.at[:, pl.ds(0, 3)], fwd_send)
    arrived(out_buf, day_send)


def lags_kernel(count_ref, middle, second, out_ref, staged, out_sem):
    first_slot = lax.axis_index("tm") * SHARE
    count = count_ref[0]
    stores = []
    for at, (begin, end) in enumerate(zip(CUTS, CUTS[1:])):
        for odd in (1, 0):
            groups = range(begin + odd, end, 2)
            columns = []
            for group in groups:
                tile = 3 * group // 2
                columns.append(jnp.concatenate(
                    [middle[source, part, tile : tile + 2].astype(jnp.float32).reshape(16, 128)
                     for part in range(2) for source in range(SOURCES)], axis=0
                ).astype(jnp.bfloat16))
            totals = jnp.dot(
                second[odd], jnp.concatenate(columns, axis=1), preferred_element_type=jnp.float32
            )
            for side, group in enumerate(groups):
                for which in range(2):
                    index = 2 * group + which
                    live = first_slot + index // 3 < count
                    for coarse in range(32):
                        start = 128 * which + 4 * coarse
                        value = totals[start : start + 3, 128 * side : 128 * side + 128]
                        value = jnp.where(live, value, jnp.zeros_like(value))
                        staged[index, :, 128 * coarse : 128 * coarse + 128] = value.astype(jnp.bfloat16)
        block = pl.ds(2 * begin, 2 * (end - begin))
        store = pltpu.make_async_copy(staged.at[block], out_ref.at[block], out_sem.at[at])
        store.start()
        stores.append(store)
    for store in stores:
        store.wait()


def body(spectra, pair_blocks, block_count):
    values = spectra.reshape(SEGS * 3, 2, WIDTH)
    pairs = pair_blocks[0].T
    first, twiddle, second = (jnp.asarray(value) for value in constants())
    f32, bf16 = jnp.float32, jnp.bfloat16
    anywhere = pl.BlockSpec(memory_space=pl.ANY)
    middle_shape = (SOURCES, 2, TILES, 8, 128)
    in_vmem = pl.BlockSpec(memory_space=pltpu.VMEM)
    middle = pl.pallas_call(
        kernel,
        out_shape=jax.ShapeDtypeStruct(middle_shape, bf16),
        in_specs=[pl.BlockSpec(memory_space=pltpu.HBM)] * 4,
        out_specs=in_vmem,
        scratch_shapes=[
            VMEM(values.shape, bf16),
            VMEM(first.shape, bf16),
            VMEM(twiddle.shape, f32),
            VMEM((31 * SETS, 3, ROWS, 128), bf16),
            VMEM((2, 128, 128), f32),
            VMEM((SOURCES, 3, ROWS, 128), bf16),
            VMEM((SETS, NX, 4, NC * 4, 3, ROWS, 128), bf16),
            VMEM((SETS, STATIONS, HOURS // 2, 3, 8, 128), f32),
            VMEM((SETS, STATIONS, HOURS // 2, 3, 8, 128), f32),
            pltpu.SMEM((NZ, NC) + pairs.shape, jnp.int32),
            VMEM((SETS, 7, TILES, 8, 128), bf16),
            VMEM((SETS, CHUNKS, TILES, 8, 128), bf16),
            DMA((3,)),
            DMA((7,)),
            DMA((NZ, NC)),
            DMA(()),
            DMA((SETS, 2, 4)),
            DMA(()),
            DMA((SETS, 2, 4)),
            DMA(()),
            DMA((5,)),
        ],
        compiler_params=pltpu.CompilerParams(
            collective_id=0, has_side_effects=True, vmem_limit_bytes=24 << 20
        ),
        name="correlate",
    )(*(pltpu.with_memory_space_constraint(value, pltpu.HBM) for value in (values, pairs, first, twiddle)))
    lags = pl.pallas_call(
        lags_kernel,
        out_shape=jax.ShapeDtypeStruct((SHARE * 3, 3, LAGS), bf16),
        in_specs=[pl.BlockSpec(memory_space=pltpu.SMEM), in_vmem, in_vmem],
        out_specs=anywhere,
        scratch_shapes=[
            VMEM((SHARE * 3, 3, LAGS), bf16),
            DMA((len(CUTS) - 1,)),
        ],
        compiler_params=pltpu.CompilerParams(vmem_limit_bytes=16 << 20),
        name="lags",
    )(block_count, middle, second)
    return lags.reshape(1, SHARE, 1, 1, 3, 3, LAGS)


def solution(mesh):
    placed = (P("tm", "sta", None, None, None, None), P("sta", None, None), P("sta"))
    return jax.shard_map(
        body,
        mesh=mesh,
        in_specs=placed,
        out_specs=P("sta", "tm", None, None, None, None, None),
        check_vma=False,
    )
```

```python
import functools
import math

import jax
import jax.numpy as jnp
import numpy as np
from jax import lax
from jax.experimental import pallas as pl
from jax.experimental.pallas import tpu as pltpu
from jax.sharding import PartitionSpec as P

MESH = pl.DeviceIdType.MESH
VMEM = pltpu.VMEM
DMA = pltpu.SemaphoreType.DMA

SMOOTH = 64
epsilon = 1e-05

NY, NX, NZ, NC = 4, 4, 4, 2
SETS = 2
CHUNKS = 8
SOURCES = SETS * CHUNKS
F2 = 32
LOCAL = F2 // SOURCES
WIDTH = 2048
LAGS = 4096
STATIONS = 32
HOURS = 4
SEGS = 2
ROWS = SEGS * LOCAL
SHARE = 10
TILES = -(-SHARE * 9 * LOCAL // 8)
GROUPS = SHARE * 3 // 2
CUTS = (0, 4, 8, 12, 15)


GREETED = sorted(
    [d for d in np.ndindex(NX, NY, NZ) if 0 in d], key=lambda d: -sum(min(at, 4 - at) for at in d)
)


def constants():
    lane = np.arange(128)
    part, m, u = lane // 64, (lane // 16) % 4, lane % 16
    f1 = 4 * u + m
    fine = np.arange(128)
    angle = 2.0 * math.pi * ((f1[:, None] * fine[None, :]) % 128) / 128.0
    cos, sin = np.cos(angle), np.sin(angle)
    is_re = (part == 0)[:, None]
    first = np.concatenate([np.where(is_re, cos, -sin), np.where(is_re, sin, cos)], axis=1)
    f2 = np.arange(F2)
    turn = 2.0 * math.pi * (f2[:, None] * fine[None, :]) / LAGS
    sign = np.where(f2 % 2 == 0, 1.0, -1.0)[:, None] * WIDTH ** (-0.5)
    twiddle = np.stack([np.cos(turn) * sign, np.sin(turn) * sign], axis=0)
    twiddle = twiddle.reshape(2, SOURCES, 1, LOCAL, 128)
    twiddle = np.broadcast_to(twiddle, (2, SOURCES, 8 // LOCAL, LOCAL, 128))
    twiddle = twiddle.reshape(2, SOURCES, 8, 128).transpose(1, 0, 2, 3)
    coarse = np.arange(32)
    spin = 2.0 * math.pi * ((coarse[:, None] * f2[None, :]) % 32) / 32.0
    second = np.zeros((2, 2, 32, 4, 2, SOURCES, 8, LOCAL))
    for odd in range(2):
        for which in range(2):
            for comp in range(3):
                at = 2 * odd + 3 * which + comp
                for part_at, table in enumerate((np.cos(spin), -np.sin(spin))):
                    second[odd, which, :, comp, part_at, :, at, :] = table.reshape(32, SOURCES, LOCAL)
    second = second.reshape(2, 256, 2 * SOURCES * 8 * LOCAL)
    return (
        first.astype(jnp.bfloat16),
        twiddle.astype(np.float32),
        second.astype(jnp.bfloat16),
    )


def band():
    row = lax.broadcasted_iota(jnp.int32, (128, 128), 0)
    col = lax.broadcasted_iota(jnp.int32, (128, 128), 1)
    gap = row - col
    one, zero = jnp.float32(1.0), jnp.float32(0.0)
    same = jnp.where(jnp.abs(gap) <= SMOOTH, one, zero)
    before = jnp.where(gap >= SMOOTH, one, zero)
    after = jnp.where(gap <= -SMOOTH, one, zero)
    return jnp.concatenate([before, same, after], axis=0).astype(jnp.bfloat16)


def whiten_blocks(x_ref):
    fill = jnp.zeros((2, WIDTH), jnp.float32)
    re = jnp.concatenate([x_ref[:, 0, :].astype(jnp.float32), fill], axis=0)
    im = jnp.concatenate([x_ref[:, 1, :].astype(jnp.float32), fill], axis=0)
    blocks = WIDTH // 128

    def rows(value):
        return jnp.concatenate([value[:, 128 * k : 128 * k + 128] for k in range(blocks)], axis=0)

    re, im = rows(re), rows(im)
    amplitude = jnp.sqrt(re * re + im * im)
    high = amplitude.astype(jnp.bfloat16)
    low = (amplitude - high.astype(jnp.float32)).astype(jnp.bfloat16)
    weights = band()
    total = None
    for value in (high, low):
        value = value.astype(jnp.float32)
        edge = jnp.zeros((8, 128), jnp.float32)
        before = jnp.concatenate([edge, value[:-8]], axis=0)
        after = jnp.concatenate([value[8:], edge], axis=0)
        wide = jnp.concatenate([before, value, after], axis=1).astype(jnp.bfloat16)
        term = jnp.dot(wide, weights, preferred_element_type=jnp.float32)
        total = term if total is None else total + term
    row = lax.broadcasted_iota(jnp.int32, (128, 128), 0)
    col = lax.broadcasted_iota(jnp.int32, (128, 128), 1)
    position = (row // 8) * 128 + col
    lower = jnp.maximum(position - SMOOTH, 0)
    upper = jnp.minimum(position + SMOOTH, WIDTH - 1)
    bins = (upper - lower + 1).astype(jnp.float32)
    smoothed = total / bins
    scale = smoothed + epsilon
    return re / scale, im / scale


def station(x_at, z_at, core_at):
    return (x_at * NZ + z_at) * NC + core_at


def arrived(block, sem):
    pltpu.make_async_copy(block, block, sem).wait()


def kernel(x_hbm, pairs_ref, first_hbm, twiddle_hbm, middle,
           x_ref, first_ref, twiddle_ref, sent,
           flat, packed, every, left, swapped, lists, out_buf, daily,
           const_sem, list_send, list_recv, one_send, one_recv, fwd_send, fwd_recv, day_send, day_recv):
    y = lax.axis_index("tm")
    sta = lax.axis_index("sta")
    core = sta % NC
    column = sta // NC
    xx, zz = column // NZ, column % NZ
    chunks = (NC * y + core, NC * zz + core)

    def send(src, dst, send_sem, recv_sem, x_at, y_at, z_at, core_at):
        pltpu.make_async_remote_copy(
            src_ref=src,
            dst_ref=dst,
            send_sem=send_sem,
            recv_sem=recv_sem,
            device_id=(y_at, station(x_at, z_at, core_at)),
            device_id_type=MESH,
        ).start()

    load = pltpu.make_async_copy(x_hbm, x_ref, const_sem.at[0])
    load.start()
    barrier = pltpu.get_barrier_semaphore()
    greeted = 0
    for dx, dy, dz in GREETED:
        for dc in range(NC):
            if (dx, dy, dz, dc) == (0, 0, 0, 0):
                continue
            peer = station((xx + dx) % NX, (zz + dz) % NZ, (core + dc) % NC)
            pl.semaphore_signal(barrier, inc=1, device_id=((y + dy) % NY, peer), device_id_type=MESH)
            greeted += 1

    pltpu.make_async_copy(pairs_ref, lists.at[zz, core], list_recv.at[zz, core]).start()
    tables = [
        pltpu.make_async_copy(first_hbm, first_ref, const_sem.at[1]),
        pltpu.make_async_copy(twiddle_hbm, twiddle_ref, const_sem.at[2]),
    ]
    for table in tables:
        table.start()
    load.wait()

    white_re, white_im = whiten_blocks(x_ref)
    flat[0] = white_re
    flat[1] = white_im
    turned = []
    for row in range(SEGS * 3):
        pieces = []
        for part in range(2):
            tile = flat[part, pl.ds(row, 16, stride=8), :]
            for m in range(4):
                pieces.append(tile if m == 0 else pltpu.roll(tile, 128 - 32 * m, 1))
        stacked = jnp.concatenate(pieces, axis=0)
        turned.append(jnp.transpose(stacked, (1, 0))[:F2])
    for source in range(SOURCES):
        for comp in range(3):
            tile = jnp.concatenate(
                [turned[seg * 3 + comp][LOCAL * source : LOCAL * source + LOCAL] for seg in range(SEGS)],
                axis=0,
            )
            packed[source, comp] = tile.astype(jnp.bfloat16)

    pl.semaphore_wait(barrier, greeted)

    scatter, across = (y, zz), (zz, y)
    spots = tuple(NY * core + s_at for s_at in scatter)
    parts = tuple(core * ((s_at + 3) // 4) for s_at in scatter)
    places = tuple(xx * (1 - p) + w_at * p for p, w_at in zip(parts, across))

    def at_axes(bins, s_at, w_at):
        return (s_at, w_at) if bins == 0 else (w_at, s_at)

    for dj, di in ((2, 2), (2, 1), (2, 3), (1, 2), (3, 2), (1, 1), (3, 3), (1, 3), (3, 1),
                   (2, 0), (0, 2), (1, 0), (3, 0), (0, 1), (0, 3), (0, 0)):
        for dc in range(NC):
            for bins in range(SETS):
                if (dj, di, dc) == (0, 0, 0):
                    continue
                core_at = (core + dc) % NC
                s_at = (scatter[bins] + dj) % 4
                x_at = (xx + di * (1 - parts[bins])) % NX
                w_at = (across[bins] + di * parts[bins]) % 4
                y_at, z_at = at_axes(bins, s_at, w_at)
                send(packed.at[CHUNKS * bins + NC * s_at + core_at], every.at[bins, xx, across[bins], spots[bins]],
                     one_send, one_recv.at[bins, parts[bins], places[bins]], x_at, y_at, z_at, core_at)
    for bins in range(SETS):
        pltpu.make_async_copy(
            packed.at[CHUNKS * bins + chunks[bins]],
            every.at[bins, xx, across[bins], spots[bins]],
            one_recv.at[bins, parts[bins], places[bins]],
        ).start()
    list_peers = [(dz, dc) for dz in (2, 1, 3, 0) for dc in range(NC) if (dz, dc) != (0, 0)]
    for at, (dz, dc) in enumerate(list_peers):
        send(pairs_ref, lists.at[zz, core], list_send.at[at], list_recv.at[zz, core],
             xx, y, (zz + dz) % NZ, (core + dc) % NC)

    lane = lax.broadcasted_iota(jnp.int32, (8, 128), 1)
    sub = lax.broadcasted_iota(jnp.int32, (8, 128), 0)
    is_re = lane < 64
    is_low = sub < 4
    is_even = (sub // 2) % 2 == 0
    sign = jnp.where(is_re, jnp.float32(-1.0), jnp.float32(1.0))

    def widen(bins, x_at, z_at, core_at, pairs=(0, 1)):
        at = station(x_at, z_at, core_at)
        for pair in pairs:
            for comp in range(3):
                hours = (2 * pair, 2 * pair + 1)
                if bins == 0:
                    halves = [every[0, x_at, z_at, NY * core_at + hour, comp] for hour in hours]
                else:
                    hours = [(y + hour) % HOURS for hour in hours]
                    halves = [every[1, x_at, hour, NZ * core_at + z_at, comp] for hour in hours]
                value = jnp.concatenate([half.astype(jnp.float32) for half in halves], axis=0)
                left[bins, at, pair, comp] = value
                swapped[bins, at, pair, comp] = pltpu.roll(value, 64, 1) * sign

    split = (pl.ds(0, 5), pl.ds(5, 3))
    for d in (0, 1, 3, 2):
        for bins in range(SETS):
            for part in range(2):
                if part == 0:
                    spot = (xx + d) % NX
                    piece = every.at[bins, spot, across[bins], split[0]]
                else:
                    spot = (across[bins] + d) % 4
                    piece = every.at[bins, xx, spot, split[1]]
                arrived(piece, one_recv.at[bins, part, spot])
                for to in (2, 1, 3):
                    if part == 1:
                        x_at, y_at, z_at, mine = (xx + to) % NX, y, zz, xx
                    else:
                        y_at, z_at = at_axes(bins, scatter[bins], (across[bins] + to) % 4)
                        x_at, mine = xx, across[bins]
                    send(piece, piece, fwd_send, fwd_recv.at[bins, part, mine], x_at, y_at, z_at, core)
    for d in range(4):
        widen(0, d, zz, 0)
        if d > 0:
            widen(1, xx, d, 1)
    for to in (1, 3, 2):
        z_at = (zz + to) % NZ
        arrived(every.at[0, :, z_at, split[0]], fwd_recv.at[0, 0, z_at])
        for d in range(4):
            widen(0, d, z_at, 0)
    for d in range(4):
        widen(0, xx, d, 1)
    for to in (1, 3, 2):
        x_at = (xx + to) % NX
        for bins in range(SETS):
            arrived(every.at[bins, x_at, :, split[1]], fwd_recv.at[bins, 1, x_at])
            for d in range(bins, 4):
                widen(bins, x_at, d, 1)
    for pair, late in ((0, (1,)), (1, (3, 2))):
        for to in late:
            y_at = (y + to) % NY
            arrived(every.at[1, :, y_at, split[0]], fwd_recv.at[1, 0, y_at])
        for x_at in range(NX):
            for z_at in range(NZ):
                widen(1, x_at, z_at, 0, (pair,))
            widen(1, x_at, 0, 1, (pair,))
    for z_at in range(NZ):
        for core_at in range(NC):
            arrived(lists.at[z_at, core_at], list_recv.at[z_at, core_at])

    def slot_products(bins, first, second):
        plain, crossed = [None] * 9, [None] * 9
        for pair in range(HOURS // 2):
            one = [left[bins, first, pair, comp] for comp in range(3)]
            turn = [swapped[bins, first, pair, comp] for comp in range(3)]
            two = [left[bins, second, pair, comp] for comp in range(3)]
            for a in range(3):
                for b in range(3):
                    at = 3 * a + b
                    p, q = one[a] * two[b], turn[a] * two[b]
                    plain[at] = p if pair == 0 else plain[at] + p
                    crossed[at] = q if pair == 0 else crossed[at] + q
        joined = []
        for at in range(9):
            keep = jnp.where(is_re, plain[at], crossed[at])
            move = jnp.where(is_re, crossed[at], plain[at])
            joined.append(keep + pltpu.roll(move, 64, 1))
        return joined

    def fold(one, two, mask, distance):
        keep = jnp.where(mask, one, two)
        move = jnp.where(mask, two, one)
        return keep + pltpu.roll(move, distance, 0)

    def fill(target, bins, z_at, core_at, first_slot):
        def make(slot, slots, tile):
            values = []
            for at in range(slots):
                values += slot_products(bins, lists[z_at, core_at, 0, slot + at], lists[z_at, core_at, 1, slot + at])
            values += values[-2:] * ((-len(values) % 4) // 2)
            for at in range(len(values) // 4):
                a, b, c, d = values[4 * at : 4 * at + 4]
                target[tile + at] = fold(
                    fold(a, b, is_even, 2), fold(c, d, is_even, 2), is_low, 4
                ).astype(jnp.bfloat16)

        for at in range(SHARE // 4):
            make(first_slot + 4 * at, 4, 9 * at)
        make(first_slot + SHARE // 4 * 4, SHARE % 4, SHARE // 4 * 9)

    offsets = ((2, 0), (1, 0), (3, 0), (2, 1), (1, 1), (3, 1), (0, 1))
    batches = (((0, 0), (2, 0)), ((1, 0), (3, 0)), ((0, 1), (2, 1)), ((1, 1), (3, 1)))
    batch_of = {offset: at for at, batch in enumerate(batches) for offset in batch}
    for at, (d, dc) in enumerate(offsets):
        for bins in range(SETS):
            core_at = (core + dc) % NC
            y_at, z_at = ((y + d) % NY, zz) if bins == 0 else (y, (zz + d) % NZ)
            fill(out_buf.at[bins, at], bins, z_at, core_at, SHARE * y_at)
            send(out_buf.at[bins, at], daily.at[bins, chunks[bins]], day_send,
                 day_recv.at[batch_of[d, dc]], xx, y_at, z_at, core_at)
    for bins in range(SETS):
        fill(daily.at[bins, chunks[bins]], bins, zz, core, SHARE * y)

    for table in tables:
        table.wait()

    def stage_one(bins, chunk):
        rows = daily[bins, chunk].reshape(TILES * 8, 128)
        product = jnp.dot(rows, first_ref[...], preferred_element_type=jnp.float32)
        re = product[:, :128].reshape(TILES, 8, 128)
        im = product[:, 128:].reshape(TILES, 8, 128)
        source = CHUNKS * bins + chunk
        turn_re, turn_im = twiddle_ref[source, 0], twiddle_ref[source, 1]
        middle[source, 0] = (re * turn_re - im * turn_im).astype(jnp.bfloat16)
        middle[source, 1] = (re * turn_im + im * turn_re).astype(jnp.bfloat16)

    for at, batch in enumerate(batches):
        ready = [
            (bins, NC * (((y if bins == 0 else zz) + 4 - d) % 4) + (core + dc) % NC)
            for d, dc in batch for bins in range(SETS)
        ]
        coming = SETS * sum(offset != (0, 0) for offset in batch)
        arrived(daily.at[0, pl.ds(0, coming)], day_recv.at[at])
        for bins, chunk in ready:
            stage_one(bins, chunk)

    for at in range(7):
        arrived(lists.at[0, 0], list_send.at[at])
    arrived(sent, one_send)
    arrived(every.at[:, pl.ds(0, 3)], fwd_send)
    arrived(out_buf, day_send)


def lags_kernel(count_ref, middle, second, out_ref, staged, out_sem):
    first_slot = lax.axis_index("tm") * SHARE
    count = count_ref[0]
    stores = []
    for at, (begin, end) in enumerate(zip(CUTS, CUTS[1:])):
        for odd in (1, 0):
            groups = range(begin + odd, end, 2)
            columns = []
            for group in groups:
                tile = 3 * group // 2
                columns.append(jnp.concatenate(
                    [middle[source, part, tile : tile + 2].reshape(16, 128)
                     for part in range(2) for source in range(SOURCES)], axis=0
                ))
            totals = jnp.dot(
                second[odd], jnp.concatenate(columns, axis=1), preferred_element_type=jnp.float32
            )
            for side, group in enumerate(groups):
                for which in range(2):
                    index = 2 * group + which
                    live = first_slot + index // 3 < count
                    for coarse in range(32):
                        start = 128 * which + 4 * coarse
                        value = totals[start : start + 3, 128 * side : 128 * side + 128]
                        value = jnp.where(live, value, jnp.zeros_like(value))
                        staged[index, :, 128 * coarse : 128 * coarse + 128] = value.astype(jnp.bfloat16)
        block = pl.ds(2 * begin, 2 * (end - begin))
        store = pltpu.make_async_copy(staged.at[block], out_ref.at[block], out_sem.at[at])
        store.start()
        stores.append(store)
    for store in stores:
        store.wait()


def body(spectra, pair_blocks, block_count):
    values = spectra.reshape(SEGS * 3, 2, WIDTH)
    pairs = pair_blocks[0].T
    first, twiddle, second = (jnp.asarray(value) for value in constants())
    f32, bf16 = jnp.float32, jnp.bfloat16
    anywhere = pl.BlockSpec(memory_space=pl.ANY)
    middle_shape = (SOURCES, 2, TILES, 8, 128)
    in_vmem = pl.BlockSpec(memory_space=pltpu.VMEM)
    middle = pl.pallas_call(
        kernel,
        out_shape=jax.ShapeDtypeStruct(middle_shape, bf16),
        in_specs=[pl.BlockSpec(memory_space=pltpu.HBM)] * 4,
        out_specs=in_vmem,
        scratch_shapes=[
            VMEM(values.shape, bf16),
            VMEM(first.shape, bf16),
            VMEM(twiddle.shape, f32),
            VMEM((31 * SETS, 3, ROWS, 128), bf16),
            VMEM((2, 128, 128), f32),
            VMEM((SOURCES, 3, ROWS, 128), bf16),
            VMEM((SETS, NX, 4, NC * 4, 3, ROWS, 128), bf16),
            VMEM((SETS, STATIONS, HOURS // 2, 3, 8, 128), f32),
            VMEM((SETS, STATIONS, HOURS // 2, 3, 8, 128), f32),
            pltpu.SMEM((NZ, NC) + pairs.shape, jnp.int32),
            VMEM((SETS, 7, TILES, 8, 128), bf16),
            VMEM((SETS, CHUNKS, TILES, 8, 128), bf16),
            DMA((3,)),
            DMA((7,)),
            DMA((NZ, NC)),
            DMA(()),
            DMA((SETS, 2, 4)),
            DMA(()),
            DMA((SETS, 2, 4)),
            DMA(()),
            DMA((4,)),
        ],
        compiler_params=pltpu.CompilerParams(
            collective_id=0, has_side_effects=True, vmem_limit_bytes=24 << 20
        ),
        name="correlate",
    )(*(pltpu.with_memory_space_constraint(value, pltpu.HBM) for value in (values, pairs, first, twiddle)))
    lags = pl.pallas_call(
        lags_kernel,
        out_shape=jax.ShapeDtypeStruct((SHARE * 3, 3, LAGS), bf16),
        in_specs=[pl.BlockSpec(memory_space=pltpu.SMEM), in_vmem, in_vmem],
        out_specs=anywhere,
        scratch_shapes=[
            VMEM((SHARE * 3, 3, LAGS), bf16),
            DMA((len(CUTS) - 1,)),
        ],
        compiler_params=pltpu.CompilerParams(vmem_limit_bytes=16 << 20),
        name="lags",
    )(block_count, middle, second)
    return lags.reshape(1, SHARE, 1, 1, 3, 3, LAGS)


def solution(mesh):
    placed = (P("tm", "sta", None, None, None, None), P("sta", None, None), P("sta"))
    return jax.shard_map(
        body,
        mesh=mesh,
        in_specs=placed,
        out_specs=P("sta", "tm", None, None, None, None, None),
        check_vma=False,
    )
```
